32 devices in a mesh: dp: 2 (over x), ctx: 2 (over y), exp: 8 (over z, core).
Axes of the slice: x: 2, y: 2, z: 4, core: 2. Of those that a mesh axis runs over, the one named last changes fastest.
Arguments:
- tokens: float32 [16, 1536, 512], P(('dp', 'exp'), 'ctx'), may hold values from -6 to 6
- lengths: int32 [16, 3], P(('dp', 'exp')), may hold values from 1 to 1536, as said below
- routes: int32 [16, 1536, 8], P(('dp', 'exp'), 'ctx'), may hold values from 0 to 23, all different within a row; in each aligned block of 768 rows (0 to 767, 768 to 1535, ..., all dimensions but the last counted through in order) at most 320 rows name the same one
- route_gates: float32 [16, 1536, 8], P(('dp', 'exp'), 'ctx'), may hold values from 0.06 to 0.2
- cotangent: float32 [16, 1536, 512], P(('dp', 'exp'), 'ctx'), may hold values from -6 to 6
- gain_one: float32 [512], replicated, may hold values from 0.25 to 1.75
- shift_one: float32 [512], replicated, may hold values from -1 to 1
- kv_weight: float32 [512, 128], replicated, may hold values from -0.25 to 0.25
- query_weight: float32 [24, 512, 64], P('exp'), may hold values from -0.25 to 0.25
- out_weight: float32 [24, 64, 512], P('exp'), may hold values from -18 to 18
- gain_two: float32 [512], replicated, may hold values from 0.25 to 1.75
- shift_two: float32 [512], replicated, may hold values from -1 to 1
- up_weight: float32 [512, 2048], replicated, may hold values from -0.25 to 0.25
- up_bias: float32 [2048], replicated, may hold values from -1 to 1
- down_weight: float32 [2048, 512], replicated, may hold values from -0.125 to 0.125
- down_bias: float32 [512], replicated, may hold values from -1 to 1
Outputs:
- output: float32 [16, 1536, 512], P(('dp', 'exp'), 'ctx')
- grad_tokens: float32 [16, 1536, 512], P(('dp', 'exp'), 'ctx')
- grad_gain_one: float32 [512], replicated
- grad_shift_one: float32 [512], replicated
- grad_kv_weight: float32 [512, 128], replicated
- grad_query_weight: float32 [24, 512, 64], P('exp')
- grad_out_weight: float32 [24, 64, 512], P('exp')
- grad_gain_two: float32 [512], replicated
- grad_shift_two: float32 [512], replicated
- grad_up_weight: float32 [512, 2048], replicated
- grad_up_bias: float32 [2048], replicated
- grad_down_weight: float32 [2048, 512], replicated
- grad_down_bias: float32 [512], replicated
The draws below stay inside these ranges and needn't reach their ends.
Inputs may be any that keep to these rules, and one draw needn't show every extreme that they name: Each row lists the lengths of 3 documents that lie end to end in this order and fill the 1536 tokens of the group. `routes`: each row names 8 different head experts; in the 768 rows of one device no head expert is named by more than 320 rows.
All inputs are finite; a program needn't handle non-finite values.
Results may differ from the reference program's by a relative error of at most 0.012.
Values may be sent and summed in bfloat16 or wider, within the bound.
A program may use at most 192 MiB of HBM per device.

```python
import math
import jax
import jax.numpy as jnp
import numpy as np
from jax import lax

D = 512
HEAD = 64
FF = 2048
TOP = 8
TOK_DEV = 768
QT = 64
EXPERTS = 24
GROUP_TOK = 1536
GROUPS = 16
CAP = 320


def draw_lengths(key, part):
    key_head, key_tail = jax.random.split(jax.random.fold_in(key, 17))
    short_top = max(TOK_DEV // 4, 2)
    head_len = jax.random.randint(key_head, (GROUPS,), 1, short_top)
    tail_len = jax.random.randint(key_tail, (GROUPS,), 1, short_top)
    long_len = GROUP_TOK - head_len - tail_len
    return jnp.stack([head_len, long_len, tail_len], axis=1).astype(jnp.int32)


def level_of(stream_key, shape, shards, least, high):
    factor_of = 1.0
    for axis_at, blocks in shards:
        heights = jax.random.uniform(jax.random.fold_in(jax.random.fold_in(stream_key, 6), axis_at), (blocks,), jnp.float32, least / len(shards), high / len(shards))
        factor_of = factor_of * jnp.repeat(jnp.exp(heights), shape[axis_at] // blocks).reshape((-1,) + (1,) * (len(shape) - 1 - axis_at))
    return factor_of


def routed_block(own_key, own, number, rows, count, top, limit, skew):
    sequence = jax.random.permutation(own_key, count)
    heavy_load, usual = load_shares(count, rows * top, limit, skew, True), load_shares(count, rows * top, limit, skew, False)
    places = jnp.arange(count)

    def named(tallies, offset_by):
        used = int((tallies > 0).sum())
        fixed = max(1, used // 4)
        moved = fixed + (places - fixed + offset_by * (used - fixed)) % max(1, count - fixed)
        return jnp.zeros((count,), jnp.int32).at[sequence[jnp.where(places < fixed, places, moved)]].set(jnp.asarray(tallies, jnp.int32))

    tallies = jnp.where(number % 4 == 0, named(heavy_load, number // 4), named(usual, number - number // 4 - 1))
    mixed = jax.random.permutation(jax.random.fold_in(own, 3), count)
    giver, receiver = mixed[0:count // 2 * 2:2], mixed[1:count // 2 * 2:2]
    room = jnp.minimum(tallies[giver] - 1, limit - tallies[receiver]) // 2
    room = jnp.where((giver == sequence[0]) | (receiver == sequence[0]) | (tallies[receiver] == 0), 0, jnp.maximum(room, 0))
    moved = jax.random.randint(jax.random.fold_in(own, 4), (count // 2,), 0, 1 << 20) % (room + 1)
    tallies = tallies.at[giver].add(-moved).at[receiver].add(moved)
    members = jnp.searchsorted(jnp.cumsum(tallies), jnp.arange(rows * top), side="right").astype(jnp.int32)
    listing = members.reshape(top, rows).T
    listing = listing[jax.random.permutation(jax.random.fold_in(own, 1), rows)]
    offset_by = jax.random.randint(jax.random.fold_in(own, 2), (rows, 1), 0, top)
    return jnp.take_along_axis(listing, (jnp.arange(top)[None, :] + offset_by) % top, axis=1)


def load_shares(amount, total, reach, lean, full):
    portions = [(1 << 20) // math.isqrt(grade ** lean) + 1 for grade in range(1, amount + 1)]
    largest = reach if full else min(reach, max(-(-total // amount), total * portions[0] // sum(portions)))
    least = 1 if total - largest >= amount - 1 else 0
    counts, rest = [largest] + [least] * (amount - 1), total - largest - least * (amount - 1)
    while rest > 0:
        free = [i for i in range(1, amount) if counts[i] < largest] or [i for i in range(1, amount) if counts[i] < reach]
        pool, budget = sum([portions[i] for i in free]), rest
        for i in free:
            extra = min(reach - counts[i], max(1, budget * portions[i] // pool), rest)
            counts[i] = counts[i] + extra
            rest = rest - extra
    return np.array(counts)


def gaussian(key, shape, scale, most, pieces=(), held_as=jnp.bfloat16):
    result = jax.random.normal(key, shape, jnp.float32) * scale
    if len(pieces) > 0:
        result = level_of(key, shape, pieces, -0.22, 0.18) * result
    return jnp.clip(result, min=-most, max=most).astype(held_as)


def setup_inputs(seed: int = 0) -> dict:
    keys = jax.random.split(jax.random.key(seed), 17)
    tokens = gaussian(keys[0], (GROUPS, GROUP_TOK, D), 1.0, 6.0, ((0, 16), (1, 2)), jnp.float32)
    lengths = draw_lengths(jax.random.fold_in(keys[16], 71), 0)
    routes_keys = jax.random.split(jax.random.fold_in(keys[2], 1), GROUPS * GROUP_TOK // TOK_DEV)
    routes_turns = jax.random.permutation(jax.random.fold_in(keys[2], 3), GROUPS * GROUP_TOK // TOK_DEV)
    routes = jax.vmap(lambda own, number: routed_block(jax.random.fold_in(keys[2], 2), own, number, TOK_DEV, EXPERTS, TOP, CAP, 1))(routes_keys, routes_turns).reshape((GROUPS, GROUP_TOK, TOP))
    route_gates = jnp.clip(0.06 + 0.14 * jax.random.uniform(keys[3], (GROUPS, GROUP_TOK, TOP), jnp.float32) ** level_of(keys[3], (GROUPS, GROUP_TOK, TOP), ((0, 16), (1, 2)), -0.2, 0.2), 0.06, 0.2)
    cotangent = gaussian(keys[4], (GROUPS, GROUP_TOK, D), 1.0, 6.0, ((0, 16), (1, 2)), jnp.float32)
    gain_one = jnp.clip(1.0 + 0.15 * jax.random.normal(keys[5], (D,), jnp.float32), 0.25, 1.75)
    shift_one = gaussian(keys[6], (D,), 0.2, 1.0, (), jnp.float32)
    kv_weight = gaussian(keys[7], (D, 2 * HEAD), D ** -0.5, 0.25, (), jnp.float32)
    query_weight = gaussian(keys[8], (EXPERTS, D, HEAD), D ** -0.5, 0.25, ((0, 8),), jnp.float32)
    out_weight = gaussian(keys[9], (EXPERTS, HEAD, D), 3.0, 18.0, ((0, 8),), jnp.float32)
    gain_two = jnp.clip(1.0 + 0.15 * jax.random.normal(keys[10], (D,), jnp.float32), 0.25, 1.75)
    shift_two = gaussian(keys[11], (D,), 0.2, 1.0, (), jnp.float32)
    up_weight = gaussian(keys[12], (D, FF), D ** -0.5, 0.25, (), jnp.float32)
    up_bias = gaussian(keys[13], (FF,), 0.2, 1.0, (), jnp.float32)
    down_weight = gaussian(keys[14], (FF, D), FF ** -0.5, 0.125, (), jnp.float32)
    down_bias = gaussian(keys[15], (D,), 0.2, 1.0, (), jnp.float32)
    return dict(tokens=tokens, lengths=lengths, routes=routes, route_gates=route_gates, cotangent=cotangent, gain_one=gain_one, shift_one=shift_one, kv_weight=kv_weight, query_weight=query_weight, out_weight=out_weight, gain_two=gain_two, shift_two=shift_two, up_weight=up_weight, up_bias=up_bias, down_weight=down_weight, down_bias=down_bias)


exact_prec = lax.Precision.HIGHEST

@jax.custom_vjp
def low(v):
    return lax.optimization_barrier(v.astype(jnp.bfloat16)).astype(jnp.float32)

@jax.custom_vjp
def low_back(v):
    return v

def low_keep(v):
    return (low(v), None)

def low_pass(kept, grad):
    return (grad,)

def back_keep(v):
    return (v, None)

def back_low(kept, grad):
    return (low(grad),)
low.defvjp(low_keep, low_pass)
low_back.defvjp(back_keep, back_low)

def layer_norm(values, ln_gain, ln_shift):
    center_val = values - lax.optimization_barrier(jnp.mean(values, axis=-1, keepdims=True))
    var_val = lax.optimization_barrier(jnp.mean(center_val * center_val, axis=-1, keepdims=True))
    return center_val * lax.rsqrt(var_val + 1e-05) * ln_gain + ln_shift

def group_forward(params, group_in):
    gain_one, shift_one, kv_weight, query_weight, out_weight, gain_two, shift_two, up_weight, up_bias, down_weight, down_bias = params
    tokens_grp, lengths_grp, routes_grp, gates_grp = group_in
    group_len = tokens_grp.shape[0]
    act_one = low(layer_norm(tokens_grp, gain_one, shift_one))
    keyval = low_back(low(jnp.dot(act_one, low(kv_weight), precision=exact_prec)))
    keys_part = keyval[:, :HEAD]
    values_part = keyval[:, HEAD:]
    expert_in = low_back(jnp.broadcast_to(act_one[:, None, :], (group_len, EXPERTS, D)))
    queries_all = low_back(low(jnp.einsum('ted,edh->teh', expert_in, low(query_weight), precision=exact_prec)))
    queries = jnp.take_along_axis(queries_all, routes_grp[:, :, None].astype(jnp.int32), axis=1)
    positions = jnp.arange(group_len, dtype=jnp.int32)
    doc_ends = jnp.cumsum(lengths_grp).astype(jnp.int32)
    doc_ids = lax.optimization_barrier(jnp.sum((positions[:, None] >= doc_ends[None, :]).astype(jnp.int32), axis=1))

    def attend(block_in):
        query_blk, pos_blk, doc_blk = block_in
        scores = jnp.einsum('tkh,jh->tkj', query_blk, keys_part, precision=exact_prec) * 0.125
        allowed = (positions[None, :] <= pos_blk[:, None]) & (doc_ids[None, :] == doc_blk[:, None])
        scores = low_back(jnp.where(allowed[:, None, :], scores, -1e+30))
        attn_probs = low(jax.nn.softmax(scores, axis=-1))
        return low_back(low(jnp.einsum('tkj,jh->tkh', attn_probs, values_part, precision=exact_prec)))
    num_blocks = group_len // QT
    context = lax.map(jax.checkpoint(attend), (queries.reshape(num_blocks, QT, TOP, HEAD), positions.reshape(num_blocks, QT), doc_ids.reshape(num_blocks, QT)))
    context = context.reshape(group_len, TOP, HEAD)
    onehot = (routes_grp[:, :, None] == jnp.arange(EXPERTS, dtype=jnp.int32)[None, None, :]).astype(jnp.float32)
    context_dense = jnp.einsum('tke,tkh->teh', onehot, context, precision=exact_prec)
    branch = low_back(low(jnp.einsum('teh,ehd->ted', context_dense, low(out_weight), precision=exact_prec)))
    gate_dense = jnp.einsum('tke,tk->te', onehot, gates_grp, precision=exact_prec)
    attn_out = jnp.einsum('te,ted->td', gate_dense, branch, precision=exact_prec)
    mid_stream = tokens_grp + attn_out
    act_two = low(layer_norm(mid_stream, gain_two, shift_two))
    hidden_pre = low_back(jnp.dot(act_two, low(up_weight), precision=exact_prec) + up_bias)
    hidden = low(jax.nn.gelu(hidden_pre))
    ffn_out = low_back(jnp.dot(hidden, low(down_weight), precision=exact_prec) + down_bias)
    return mid_stream + ffn_out

def reference(tokens, lengths, routes, route_gates, cotangent, gain_one, shift_one, kv_weight, query_weight, out_weight, gain_two, shift_two, up_weight, up_bias, down_weight, down_bias):
    params = (gain_one, shift_one, kv_weight, query_weight, out_weight, gain_two, shift_two, up_weight, up_bias, down_weight, down_bias)

    def forward(tokens_in, params_in):

        def one_group(group_in):
            return group_forward(params_in, group_in)
        return lax.map(jax.checkpoint(one_group), (tokens_in, lengths, routes, route_gates))
    output, pullback = jax.vjp(forward, tokens, params)
    grad_tokens, grad_params = pullback(cotangent)
    grad_gain_one, grad_shift_one, grad_kv_weight, grad_query_weight, grad_out_weight, grad_gain_two, grad_shift_two, grad_up_weight, grad_up_bias, grad_down_weight, grad_down_bias = grad_params
    return (output, grad_tokens, grad_gain_one, grad_shift_one, grad_kv_weight, grad_query_weight, grad_out_weight, grad_gain_two, grad_shift_two, grad_up_weight, grad_up_bias, grad_down_weight, grad_down_bias)
```

```python
import functools
import math

import jax
import jax.numpy as jnp
from jax import lax
from jax.experimental import pallas as pl
from jax.experimental.pallas import tpu as pltpu
from jax.sharding import PartitionSpec as P

f32 = jnp.float32
bf16 = jnp.bfloat16
D = 512
HEAD = 64
TOP = 8
TB = 128
W = TOP * TB
NEG = -1e30
LOG2E = math.log2(math.e)
LN2 = math.log(2.0)
SAFE = 50.0
NN = (((1,), (0,)), ((), ()))
NT = (((1,), (1,)), ((), ()))
TN = (((0,), (0,)), ((), ()))
C0 = math.sqrt(2 / math.pi)
C1 = 0.044715


def attn_fwd_kernel(cidx_ref, act_ref, wq_ref, routes_ref, gates_ref, qdoc_ref, kaug_ref, vt_ref, kn_ref,
                    cd_ref, q_ref, ctx_ref, lse_ref,
                    qt, qaug, s, acc, *, experts, tok, KB):
    i=pl.program_id(0)
    c=cidx_ref[0]
    qt[...]=lax.dot_general(wq_ref[...], act_ref[...], NT, preferred_element_type=f32)*(0.125*LOG2E)
    n2=[]
    for k0 in range(0,TOP,4):
        r=[jnp.broadcast_to(routes_ref[k0+k:k0+k+1,:],(8,TB))[None] for k in range(4)]
        sel=[jnp.zeros((HEAD//8,8,TB),f32) for _ in range(4)]
        for e in range(experts):
            v=qt[e*HEAD:(e+1)*HEAD,:].reshape(HEAD//8,8,TB)
            sel=[jnp.where(r[k]==e,v,sel[k]) for k in range(4)]
        for k in range(4):
            sk=sel[k].reshape(HEAD,TB)
            n2.append(jnp.max(jnp.sum(sk*sk,axis=0,keepdims=True)))
            qaug[0:HEAD,(k0+k)*TB:(k0+k+1)*TB]=sk.astype(bf16)
    n2=functools.reduce(jnp.maximum,n2)*kn_ref[0]
    fast=n2<=SAFE*SAFE
    q_ref[0]=qaug[0:HEAD,:]
    qd=qdoc_ref[...]
    qaug[HEAD:HEAD+16,:]=jnp.concatenate([jnp.concatenate([qd,jnp.zeros_like(qd)],0)]*TOP,1).astype(bf16)
    qaug[HEAD+16:,:]=jnp.zeros((128-HEAD-16,W),bf16)
    q0=c*tok+i*TB
    nfull=q0//KB
    kd=pl.multiple_of(nfull*KB,KB)
    kp=lax.broadcasted_iota(jnp.int32,(KB,TB),0)+(kd-q0)
    tp=lax.broadcasted_iota(jnp.int32,(KB,TB),1)
    mask=kp<=tp
    acc[...]=jnp.zeros_like(acc)
    def scores(k0,n):
        return jnp.dot(kaug_ref[pl.ds(k0,n),:],qaug[...],preferred_element_type=f32)
    def masked(x):
        return jnp.concatenate([jnp.where(mask,x[:,k*TB:(k+1)*TB],NEG) for k in range(TOP)],1)
    def pv(k0,n,p):
        acc[...]+=jnp.dot(vt_ref[:,pl.ds(k0,n)],p,preferred_element_type=f32)
    def finish(m):
        l=acc[HEAD:HEAD+1,:]
        lse_ref[0]=m+jnp.log2(l)
        acc[0:HEAD,:]=acc[0:HEAD,:]*(1.0/l)
    @pl.when(fast)
    def _():
        def body(b,_):
            k0=pl.multiple_of(b*KB,KB)
            pv(k0,KB,jnp.exp2(scores(k0,KB)).astype(bf16))
            return 0
        lax.fori_loop(0,nfull,body,0)
        pv(kd,KB,jnp.exp2(masked(scores(kd,KB))).astype(bf16))
        finish(0.0)
    @pl.when(jnp.logical_not(fast))
    def _():
        def spass(b,m):
            k0=pl.multiple_of(b*KB,KB)
            x=scores(k0,KB)
            s[pl.ds(k0,KB),:]=x
            return jnp.maximum(m,jnp.max(x.reshape(KB//8,8,W),axis=0))
        m=lax.fori_loop(0,nfull,spass,jnp.full((8,W),NEG*2,f32))
        x=masked(scores(kd,KB))
        s[pl.ds(kd,KB),:]=x
        m=jnp.maximum(m,jnp.max(x.reshape(KB//8,8,W),axis=0))
        m=jnp.max(m,axis=0,keepdims=True)
        def ppass(b,_):
            k0=pl.multiple_of(b*KB,KB)
            pv(k0,KB,jnp.exp2(s[pl.ds(k0,KB),:]-m).astype(bf16))
            return 0
        lax.fori_loop(0,nfull+1,ppass,0)
        finish(m)
    ctx_ref[0]=acc[0:HEAD,:]
    for k in range(TOP):
        acc[0:HEAD,k*TB:(k+1)*TB]*=gates_ref[k:k+1,:]
    r=[jnp.broadcast_to(routes_ref[k:k+1,:],(8,TB))[None] for k in range(TOP)]
    for h0 in range(0,HEAD,32):
        g=[acc[h0:h0+32,k*TB:(k+1)*TB].reshape(4,8,TB) for k in range(TOP)]
        for e in range(experts):
            o=jnp.zeros((4,8,TB),f32)
            for k in range(TOP):
                o=jnp.where(r[k]==e,g[k],o)
            cd_ref[e*HEAD+h0:e*HEAD+h0+32,:]=o.reshape(32,TB).astype(bf16)

def attn_fwd(cidx, act, wq, routesT, gatesT, qdoc, kaug, vt, kn, KB=256):
    tok=act.shape[0]; experts=wq.shape[0]//HEAD; keys=kaug.shape[0]; n=tok//TB; vr=vt.shape[0]
    full=lambda a: pl.BlockSpec(a.shape,lambda i,*_:(0,)*a.ndim)
    return pl.pallas_call(
        functools.partial(attn_fwd_kernel,experts=experts,tok=tok,KB=KB),
        grid_spec=pltpu.PrefetchScalarGridSpec(num_scalar_prefetch=1,grid=(n,),
          in_specs=[pl.BlockSpec((TB,D),lambda i,*_:(i,0)),full(wq),
            pl.BlockSpec((TOP,TB),lambda i,*_:(0,i)),pl.BlockSpec((TOP,TB),lambda i,*_:(0,i)),
            pl.BlockSpec((8,TB),lambda i,*_:(0,i)),full(kaug),full(vt),pl.BlockSpec(memory_space=pltpu.SMEM)],
          out_specs=[pl.BlockSpec((experts*HEAD,TB),lambda i,*_:(0,i)),
            pl.BlockSpec((1,HEAD,W),lambda i,*_:(i,0,0)),
            pl.BlockSpec((1,HEAD,W),lambda i,*_:(i,0,0)),
            pl.BlockSpec((1,1,W),lambda i,*_:(i,0,0))],
          scratch_shapes=[pltpu.VMEM((experts*HEAD,TB),f32),pltpu.VMEM((128,W),bf16),
            pltpu.VMEM((keys,W),f32),pltpu.VMEM((vr,W),f32)]),
        out_shape=[jax.ShapeDtypeStruct((experts*HEAD,tok),bf16),
          jax.ShapeDtypeStruct((n,HEAD,W),bf16),jax.ShapeDtypeStruct((n,HEAD,W),f32),
          jax.ShapeDtypeStruct((n,1,W),f32)],
        compiler_params=pltpu.CompilerParams(vmem_limit_bytes=60*2**20),
        name="attn_fwd",
    )(cidx,act,wq,routesT,gatesT,qdoc,kaug,vt,kn)


def split3(x):
    hi=x.astype(bf16).astype(f32); r=x-hi
    mid=r.astype(bf16).astype(f32); lo=r-mid
    return hi,mid,lo

def attn_bwd_kernel(cidx_ref, dct_ref, q_ref, ctx_ref, lse_ref, routes_ref, gates_ref, qdoc_ref,
                    kaug_ref, vaug_ref, kt_ref,
                    dqd_ref, dkv_ref,
                    qaug, daug, rhs, pds, dq, *, experts, tok, KB):
    i=pl.program_id(0)
    c=cidx_ref[0]
    @pl.when(i==0)
    def _():
        dkv_ref[...]=jnp.zeros_like(dkv_ref)
        rhs[...]=jnp.zeros_like(rhs)
    q=q_ref[0]
    qaug[0:HEAD,:]=q
    rhs[0:HEAD,0:W]=q
    hi,mid,lo=split3(-lse_ref[0])
    qd=qdoc_ref[...]
    qaug[HEAD:HEAD+16,:]=jnp.concatenate([jnp.concatenate([qd[0:3,:]]*TOP,1),hi,mid,lo,jnp.zeros((10,W),f32)],0).astype(bf16)
    qaug[HEAD+16:,:]=jnp.zeros((128-HEAD-16,W),bf16)
    r=[jnp.broadcast_to(routes_ref[k:k+1,:],(8,TB))[None] for k in range(TOP)]
    for k0 in range(0,TOP,4):
        sel=[jnp.zeros((HEAD//8,8,TB),f32) for _ in range(4)]
        for e in range(experts):
            v=dct_ref[e*HEAD:(e+1)*HEAD,:].astype(f32).reshape(HEAD//8,8,TB)
            sel=[jnp.where(r[k0+k]==e,v,sel[k]) for k in range(4)]
        for k in range(4):
            sl=slice((k0+k)*TB,(k0+k+1)*TB)
            dc=(sel[k].reshape(HEAD,TB)*gates_ref[k0+k:k0+k+1,:]).astype(bf16)
            daug[0:HEAD,sl]=dc
            rhs[HEAD:,W+(k0+k)*TB:W+(k0+k+1)*TB]=dc
            dq[0:1,sl]=jnp.sum(dc.astype(f32)*ctx_ref[0,:,sl].astype(f32),axis=0,keepdims=True)
    hi,mid,lo=split3(-dq[0:1,:])
    daug[HEAD:HEAD+16,:]=jnp.concatenate([hi,mid,lo,jnp.zeros((13,W),f32)],0).astype(bf16)
    daug[HEAD+16:,:]=jnp.zeros((128-HEAD-16,W),bf16)
    dq[...]=jnp.zeros_like(dq)
    q0=c*tok+i*TB
    nfull=q0//KB
    kd=pl.multiple_of(nfull*KB,KB)
    def block(k0,mask):
        p=jnp.exp2(jnp.dot(kaug_ref[pl.ds(k0,KB),:],qaug[...],preferred_element_type=f32))
        if mask is not None:
            p=jnp.concatenate([jnp.where(mask,p[:,k*TB:(k+1)*TB],0.0) for k in range(TOP)],1)
        dp=jnp.dot(vaug_ref[pl.ds(k0,KB),:],daug[...],preferred_element_type=f32)
        pds[:,W:]=p.astype(bf16)
        pds[:,:W]=(p*dp).astype(bf16)
        dq[...]+=jnp.dot(kt_ref[:,pl.ds(k0,KB)],pds[:,:W],preferred_element_type=f32)
        dkv_ref[pl.ds(k0,KB),:]+=lax.dot_general(pds[...],rhs[...],NT,preferred_element_type=f32)
    def body(b,_):
        block(pl.multiple_of(b*KB,KB),None)
        return 0
    lax.fori_loop(0,nfull,body,0)
    kp=lax.broadcasted_iota(jnp.int32,(KB,TB),0)+(kd-q0)
    tp=lax.broadcasted_iota(jnp.int32,(KB,TB),1)
    block(kd,kp<=tp)
    dq[...]*=0.125
    for h0 in range(0,HEAD,32):
        g=[dq[h0:h0+32,k*TB:(k+1)*TB].reshape(4,8,TB) for k in range(TOP)]
        for e in range(experts):
            o=jnp.zeros((4,8,TB),f32)
            for k in range(TOP):
                o=jnp.where(r[k]==e,g[k],o)
            dqd_ref[e*HEAD+h0:e*HEAD+h0+32,:]=o.reshape(32,TB).astype(bf16)
    @pl.when(i==pl.num_programs(0)-1)
    def _():
        lane=lax.broadcasted_iota(jnp.int32,(1,128),1)
        dkv_ref[...]*=jnp.where(lane<HEAD,LN2,1.0)

def attn_bwd(cidx, dct, q, ctx, lse, routesT, gatesT, qdoc, kaug, vaug, kt, KB=256):
    tok=routesT.shape[1]; experts=dct.shape[0]//HEAD; keys=kaug.shape[0]; n=tok//TB
    full=lambda a: pl.BlockSpec(a.shape,lambda i,*_:(0,)*a.ndim)
    blk=lambda rows: pl.BlockSpec((rows,TB),lambda i,*_:(0,i))
    return pl.pallas_call(
        functools.partial(attn_bwd_kernel,experts=experts,tok=tok,KB=KB),
        grid_spec=pltpu.PrefetchScalarGridSpec(num_scalar_prefetch=1,grid=(n,),
          in_specs=[blk(experts*HEAD),
            pl.BlockSpec((1,HEAD,W),lambda i,*_:(i,0,0)),
            pl.BlockSpec((1,HEAD,W),lambda i,*_:(i,0,0)),
            pl.BlockSpec((1,1,W),lambda i,*_:(i,0,0)),
            blk(TOP),blk(TOP),blk(8),full(kaug),full(vaug),full(kt)],
          out_specs=[blk(experts*HEAD),pl.BlockSpec((keys,128),lambda i,*_:(0,0))],
          scratch_shapes=[pltpu.VMEM((128,W),bf16),pltpu.VMEM((128,W),bf16),pltpu.VMEM((128,2*W),bf16),
            pltpu.VMEM((KB,2*W),bf16),pltpu.VMEM((HEAD,W),f32)]),
        out_shape=[jax.ShapeDtypeStruct((experts*HEAD,tok),bf16),
          jax.ShapeDtypeStruct((keys,128),f32)],
        compiler_params=pltpu.CompilerParams(vmem_limit_bytes=60*2**20),
        name="attn_bwd",
    )(cidx,dct,q,ctx,lse,routesT,gatesT,qdoc,kaug,vaug,kt)


def dot(a,b,dims=NN): return lax.dot_general(a,b,dims,preferred_element_type=f32)

def ffn_kernel(cd_ref, wo_ref, tok_ref, cot_ref, g2_ref, s2_ref, up_ref, upb_ref, down_ref, downb_ref,
               out_ref, dmid_ref, dct_ref, gwo_ref, gup_ref, gub_ref, gdown_ref, gsm_ref,
               mid, xhat, rstd, act, actT, dffn, acc, da2):
    j=pl.program_id(0); n=pl.num_programs(0)
    @pl.when(j==0)
    def _():
        m=tok_ref[...]+dot(cd_ref[...],wo_ref[...],TN)
        mid[...]=m
        cen=m-jnp.mean(m,axis=-1,keepdims=True)
        rs=lax.rsqrt(jnp.mean(cen*cen,axis=-1,keepdims=True)+1e-5)
        xh=cen*rs
        xhat[...]=xh; rstd[...]=jnp.broadcast_to(rs,rstd.shape)
        a=(xh*g2_ref[...]+s2_ref[...])
        act[...]=a.astype(bf16)
        actT[...]=jnp.transpose(a).astype(bf16)
        dffn[...]=cot_ref[...].astype(bf16)
        acc[...]=jnp.zeros_like(acc); da2[...]=jnp.zeros_like(da2)
    up=up_ref[...].astype(bf16); down=down_ref[...].astype(bf16)
    pre=dot(act[...],up)+upb_ref[...]
    x2=pre*pre
    th=jnp.tanh(pre*(C0+C0*C1*x2))
    h=0.5*(1.0+th)
    hid=(pre*h).astype(bf16)
    gp=h+(0.5*pre)*(1.0-th*th)*(C0+3.0*C0*C1*x2)
    acc[...]+=dot(hid,down)
    gdown_ref[...]=dot(hid,dffn[...],TN).astype(gdown_ref.dtype)
    dp=dot(dffn[...],down,NT)*gp
    dpb=dp.astype(bf16)
    gub_ref[...]=jnp.sum(dpb.astype(f32),axis=0,keepdims=True)
    gup_ref[...]=dot(actT[...],dpb).astype(gup_ref.dtype)
    da2[...]+=dot(dpb,up,NT)
    @pl.when(j==n-1)
    def _():
        out_ref[...]=mid[...]+acc[...]+downb_ref[...]
        d=da2[...]; xh=xhat[...]
        gx=d*g2_ref[...]
        dm=cot_ref[...]+rstd[:,0:1]*(gx-jnp.mean(gx,axis=-1,keepdims=True)-xh*jnp.mean(gx*xh,axis=-1,keepdims=True))
        dmid_ref[...]=dm
        dmb=dm.astype(bf16)
        dct_ref[...]=dot(wo_ref[...],dmb,NT).astype(bf16)
        gwo_ref[...]=dot(cd_ref[...],dmb).astype(gwo_ref.dtype)
        gsm_ref[...]=jnp.concatenate([jnp.sum(d*xh,axis=0,keepdims=True),jnp.sum(d,axis=0,keepdims=True),
            jnp.sum(dffn[...].astype(f32),axis=0,keepdims=True),jnp.zeros((5,D),f32)],0)

def ffn(cd, wo, tokens, cot, g2, s2, up, upb, down, downb, FB=256, gdt=bf16):
    tok=tokens.shape[0]; FF=up.shape[1]; n=FF//FB; EH=wo.shape[0]
    full=lambda a: pl.BlockSpec(a.shape,lambda i:(0,)*a.ndim,pipeline_mode=pl.Buffered(1))
    fo=lambda *s: pl.BlockSpec(s,lambda i:(0,)*len(s))
    sd=jax.ShapeDtypeStruct
    return pl.pallas_call(ffn_kernel,grid=(n,),
        in_specs=[full(cd),full(wo),full(tokens),full(cot),full(g2),full(s2),
          pl.BlockSpec((D,FB),lambda i:(0,i)),pl.BlockSpec((1,FB),lambda i:(0,i)),
          pl.BlockSpec((FB,D),lambda i:(i,0)),full(downb)],
        out_specs=[fo(tok,D),fo(tok,D),fo(EH,tok),fo(EH,D),
          pl.BlockSpec((D,FB),lambda i:(0,i)),pl.BlockSpec((1,FB),lambda i:(0,i)),
          pl.BlockSpec((FB,D),lambda i:(i,0)),fo(8,D)],
        out_shape=[sd((tok,D),f32),sd((tok,D),f32),sd((EH,tok),bf16),sd((EH,D),gdt),
          sd((D,FF),gdt),sd((1,FF),f32),sd((FF,D),gdt),sd((8,D),f32)],
        scratch_shapes=[pltpu.VMEM((tok,D),f32),pltpu.VMEM((tok,D),f32),pltpu.VMEM((tok,128),f32),
          pltpu.VMEM((tok,D),bf16),pltpu.VMEM((D,tok),bf16),pltpu.VMEM((tok,D),bf16),
          pltpu.VMEM((tok,D),f32),pltpu.VMEM((tok,D),f32)],
        compiler_params=pltpu.CompilerParams(vmem_limit_bytes=60*2**20),
        name="ffn",
    )(cd,wo,tokens,cot,g2,s2,up,upb,down,downb)


def local(sizes, tokens, lengths, routes, route_gates, cotangent, gain_one, shift_one, kv_weight,
          query_weight, out_weight, gain_two, shift_two, up_weight, up_bias, down_weight, down_bias):
    x = tokens[0]
    tok = x.shape[0]
    ncx = sizes["ctx"]
    group = tok * ncx
    nexp = query_weight.shape[0]
    experts = nexp * sizes["exp"]
    cidx = lax.axis_index("ctx")
    wq_own = jnp.swapaxes(query_weight, 1, 2).reshape(nexp * HEAD, D).astype(bf16)
    wo_own = out_weight.reshape(nexp * HEAD, D).astype(bf16)
    wq = lax.all_gather(wq_own, "exp", axis=0, tiled=True)
    wo = lax.all_gather(wo_own, "exp", axis=0, tiled=True)
    cen = x - jnp.mean(x, axis=-1, keepdims=True)
    rs1 = lax.rsqrt(jnp.mean(cen * cen, axis=-1, keepdims=True) + 1e-5)
    xh1 = cen * rs1
    act = (xh1 * gain_one + shift_one).astype(bf16)
    kvw = kv_weight.astype(bf16)
    kv_own = dot(act, kvw).astype(bf16)
    kv = lax.all_gather(kv_own, "ctx", axis=0, tiled=True)
    keys, vals = kv[:, :HEAD], kv[:, HEAD:]
    kn = jnp.max(jnp.sum(jnp.square(keys.astype(f32)), axis=1)).reshape(1)
    pos = jnp.arange(group, dtype=jnp.int32)
    docs, end = jnp.zeros_like(pos), 0
    for d in range(lengths.shape[1] - 1):
        end = end + lengths[0, d]
        docs = docs + (pos >= end).astype(jnp.int32)
    hot = (docs[:, None] == jnp.arange(3)[None, :]).astype(bf16)
    one3 = jnp.ones((group, 3), bf16)
    kaug = jnp.concatenate([keys, hot, one3, jnp.zeros((group, HEAD - 6), bf16)], axis=1)
    vaug = jnp.concatenate([vals, one3, jnp.zeros((group, HEAD - 3), bf16)], axis=1)
    kt = keys.T
    vt = jnp.concatenate([vals.T, jnp.ones((1, group), bf16), jnp.zeros((15, group), bf16)], axis=0)
    qdocs = lax.dynamic_slice_in_dim(docs, cidx * tok, tok)
    slot = jnp.arange(8, dtype=jnp.int32)[:, None]
    qdoc = jnp.where((qdocs[None, :] == slot) | (slot > 2), 0.0, NEG).astype(f32)
    routes_t = routes[0].T
    gates_t = route_gates[0].T
    cvec = cidx.reshape(1).astype(jnp.int32)

    cd, q, ctx, lse = attn_fwd(cvec, act, wq, routes_t, gates_t, qdoc, kaug, vt, kn, KB=384)
    row = lambda v: v.reshape(1, -1)
    out, dmid, dct, gwo, gup, gub, gdown, gsm = ffn(
        cd, wo, x, cotangent[0], row(gain_two), row(shift_two), up_weight, row(up_bias),
        down_weight, row(down_bias), FB=512)
    dqd, dkv_part = attn_bwd(cvec, dct, q, ctx, lse, routes_t, gates_t, qdoc, kaug, vaug, kt, KB=384)
    dkv = lax.psum_scatter(dkv_part, "ctx", scatter_dimension=0, tiled=True).astype(bf16)
    gkv = dot(act, dkv, TN)
    gwq = dot(dqd, act).astype(bf16)
    da1 = dot(dqd, wq, TN) + dot(dkv, kvw, NT)
    gg1 = jnp.sum(da1 * xh1, axis=0)
    gs1 = jnp.sum(da1, axis=0)
    gx = da1 * gain_one
    dx = dmid + rs1 * (gx - jnp.mean(gx, axis=-1, keepdims=True) - xh1 * jnp.mean(gx * xh1, axis=-1, keepdims=True))

    gw = lax.psum_scatter(jnp.concatenate([gwq, gwo], axis=1), "exp", scatter_dimension=0, tiled=True)
    gw = lax.psum(gw, ("dp", "ctx")).astype(f32)
    gq = jnp.swapaxes(gw[:, :D].reshape(nexp, HEAD, D), 1, 2)
    go = gw[:, D:].reshape(nexp, HEAD, D)
    gup, gdown = lax.psum((gup, gdown), ("dp", "ctx", "exp"))
    gg1, gs1, gkv, gub, gsm = lax.psum((gg1, gs1, gkv, gub, gsm), ("dp", "ctx", "exp"))
    return (out[None], dx[None], gg1, gs1, gkv, gq, go, gsm[0], gsm[1], gup.astype(f32), gub[0],
            gdown.astype(f32), gsm[2])


def solution(mesh):
    tok3 = P(("dp", "exp"), "ctx", None)
    ex = P("exp", None, None)
    r = P()
    in_specs = (tok3, P(("dp", "exp"), None), tok3, tok3, tok3, r, r, r, ex, ex, r, r, r, r, r, r)
    out_specs = (tok3, tok3, r, r, r, ex, ex, r, r, r, r, r, r)
    fn = functools.partial(local, dict(mesh.shape))
    return jax.shard_map(fn, mesh=mesh, in_specs=in_specs, out_specs=out_specs, check_vma=False)
```

```python
import functools
import math

import jax
import jax.numpy as jnp
from jax import lax
from jax.experimental import pallas as pl
from jax.experimental.pallas import tpu as pltpu
from jax.sharding import PartitionSpec as P

f32 = jnp.float32
bf16 = jnp.bfloat16
D = 512
HEAD = 64
TOP = 8
TB = 128
W = TOP * TB
NEG = -1e30
LOG2E = math.log2(math.e)
LN2 = math.log(2.0)
SAFE = 50.0
NN = (((1,), (0,)), ((), ()))
NT = (((1,), (1,)), ((), ()))
TN = (((0,), (0,)), ((), ()))
C0 = math.sqrt(2 / math.pi)
C1 = 0.044715
MESH = pl.DeviceIdType.MESH
AXES = ("dp", "ctx", "exp")


def attn_fwd_kernel(cidx_ref, act_ref, wq_ref, routes_ref, gates_ref, qdoc_ref, kaug_ref, vt_ref, kn_ref,
                    cd_ref, q_ref, ctx_ref, lse_ref,
                    qt, qaug, s, acc, *, experts, tok, KB):
    i=pl.program_id(0)
    c=cidx_ref[0]
    qt[...]=lax.dot_general(wq_ref[...], act_ref[...], NT, preferred_element_type=f32)*(0.125*LOG2E)
    n2=[]
    for k0 in range(0,TOP,4):
        r=[jnp.broadcast_to(routes_ref[k0+k:k0+k+1,:],(8,TB))[None] for k in range(4)]
        sel=[jnp.zeros((HEAD//8,8,TB),f32) for _ in range(4)]
        for e in range(experts):
            v=qt[e*HEAD:(e+1)*HEAD,:].reshape(HEAD//8,8,TB)
            sel=[jnp.where(r[k]==e,v,sel[k]) for k in range(4)]
        for k in range(4):
            sk=sel[k].reshape(HEAD,TB)
            n2.append(jnp.max(jnp.sum(sk*sk,axis=0,keepdims=True)))
            qaug[0:HEAD,(k0+k)*TB:(k0+k+1)*TB]=sk.astype(bf16)
    n2=functools.reduce(jnp.maximum,n2)*kn_ref[0]
    fast=n2<=SAFE*SAFE
    q_ref[0]=qaug[0:HEAD,:]
    qd=qdoc_ref[...]
    qaug[HEAD:HEAD+16,:]=jnp.concatenate([jnp.concatenate([qd,jnp.zeros_like(qd)],0)]*TOP,1).astype(bf16)
    qaug[HEAD+16:,:]=jnp.zeros((128-HEAD-16,W),bf16)
    q0=c*tok+i*TB
    nfull=q0//KB
    kd=pl.multiple_of(nfull*KB,KB)
    kp=lax.broadcasted_iota(jnp.int32,(KB,TB),0)+(kd-q0)
    tp=lax.broadcasted_iota(jnp.int32,(KB,TB),1)
    mask=kp<=tp
    acc[...]=jnp.zeros_like(acc)
    def scores(k0,n):
        return jnp.dot(kaug_ref[pl.ds(k0,n),:],qaug[...],preferred_element_type=f32)
    def masked(x):
        return jnp.concatenate([jnp.where(mask,x[:,k*TB:(k+1)*TB],NEG) for k in range(TOP)],1)
    def pv(k0,n,p):
        acc[...]+=jnp.dot(vt_ref[:,pl.ds(k0,n)],p,preferred_element_type=f32)
    def finish(m):
        l=acc[HEAD:HEAD+1,:]
        lse_ref[0]=m+jnp.log2(l)
        acc[0:HEAD,:]=acc[0:HEAD,:]*(1.0/l)
    @pl.when(fast)
    def _():
        def body(b,_):
            k0=pl.multiple_of(b*KB,KB)
            pv(k0,KB,jnp.exp2(scores(k0,KB)).astype(bf16))
            return 0
        lax.fori_loop(0,nfull,body,0)
        pv(kd,KB,jnp.exp2(masked(scores(kd,KB))).astype(bf16))
        finish(0.0)
    @pl.when(jnp.logical_not(fast))
    def _():
        def spass(b,m):
            k0=pl.multiple_of(b*KB,KB)
            x=scores(k0,KB)
            s[pl.ds(k0,KB),:]=x
            return jnp.maximum(m,jnp.max(x.reshape(KB//8,8,W),axis=0))
        m=lax.fori_loop(0,nfull,spass,jnp.full((8,W),NEG*2,f32))
        x=masked(scores(kd,KB))
        s[pl.ds(kd,KB),:]=x
        m=jnp.maximum(m,jnp.max(x.reshape(KB//8,8,W),axis=0))
        m=jnp.max(m,axis=0,keepdims=True)
        def ppass(b,_):
            k0=pl.multiple_of(b*KB,KB)
            pv(k0,KB,jnp.exp2(s[pl.ds(k0,KB),:]-m).astype(bf16))
            return 0
        lax.fori_loop(0,nfull+1,ppass,0)
        finish(m)
    ctx_ref[0]=acc[0:HEAD,:]
    for k in range(TOP):
        acc[0:HEAD,k*TB:(k+1)*TB]*=gates_ref[k:k+1,:]
    r=[jnp.broadcast_to(routes_ref[k:k+1,:],(8,TB))[None] for k in range(TOP)]
    for h0 in range(0,HEAD,32):
        g=[acc[h0:h0+32,k*TB:(k+1)*TB].reshape(4,8,TB) for k in range(TOP)]
        for e in range(experts):
            o=jnp.zeros((4,8,TB),f32)
            for k in range(TOP):
                o=jnp.where(r[k]==e,g[k],o)
            cd_ref[e*HEAD+h0:e*HEAD+h0+32,:]=o.reshape(32,TB).astype(bf16)

def attn_fwd(cidx, act, wq, routesT, gatesT, qdoc, kaug, vt, kn, KB=256):
    tok=act.shape[0]; experts=wq.shape[0]//HEAD; keys=kaug.shape[0]; n=tok//TB; vr=vt.shape[0]
    full=lambda a: pl.BlockSpec(a.shape,lambda i,*_:(0,)*a.ndim)
    return pl.pallas_call(
        functools.partial(attn_fwd_kernel,experts=experts,tok=tok,KB=KB),
        grid_spec=pltpu.PrefetchScalarGridSpec(num_scalar_prefetch=1,grid=(n,),
          in_specs=[pl.BlockSpec((TB,D),lambda i,*_:(i,0)),full(wq),
            pl.BlockSpec((TOP,TB),lambda i,*_:(0,i)),pl.BlockSpec((TOP,TB),lambda i,*_:(0,i)),
            pl.BlockSpec((8,TB),lambda i,*_:(0,i)),full(kaug),full(vt),pl.BlockSpec(memory_space=pltpu.SMEM)],
          out_specs=[pl.BlockSpec((experts*HEAD,TB),lambda i,*_:(0,i)),
            pl.BlockSpec((1,HEAD,W),lambda i,*_:(i,0,0)),
            pl.BlockSpec((1,HEAD,W),lambda i,*_:(i,0,0)),
            pl.BlockSpec((1,1,W),lambda i,*_:(i,0,0))],
          scratch_shapes=[pltpu.VMEM((experts*HEAD,TB),f32),pltpu.VMEM((128,W),bf16),
            pltpu.VMEM((keys,W),f32),pltpu.VMEM((vr,W),f32)]),
        out_shape=[jax.ShapeDtypeStruct((experts*HEAD,tok),bf16),
          jax.ShapeDtypeStruct((n,HEAD,W),bf16),jax.ShapeDtypeStruct((n,HEAD,W),f32),
          jax.ShapeDtypeStruct((n,1,W),f32)],
        compiler_params=pltpu.CompilerParams(vmem_limit_bytes=60*2**20),
        name="attn_fwd",
    )(cidx,act,wq,routesT,gatesT,qdoc,kaug,vt,kn)


def split3(x):
    hi=x.astype(bf16).astype(f32); r=x-hi
    mid=r.astype(bf16).astype(f32); lo=r-mid
    return hi,mid,lo

def attn_bwd_kernel(cidx_ref, dct_ref, q_ref, ctx_ref, lse_ref, routes_ref, gates_ref, qdoc_ref,
                    kaug_ref, vaug_ref, kt_ref,
                    dqd_ref, dkv_ref,
                    qaug, daug, rhs, pds, dq, *, experts, tok, KB):
    i=pl.program_id(0)
    c=cidx_ref[0]
    @pl.when(i==0)
    def _():
        dkv_ref[...]=jnp.zeros_like(dkv_ref)
        rhs[...]=jnp.zeros_like(rhs)
    q=q_ref[0]
    qaug[0:HEAD,:]=q
    rhs[0:HEAD,0:W]=q
    hi,mid,lo=split3(-lse_ref[0])
    qd=qdoc_ref[...]
    qaug[HEAD:HEAD+16,:]=jnp.concatenate([jnp.concatenate([qd[0:3,:]]*TOP,1),hi,mid,lo,jnp.zeros((10,W),f32)],0).astype(bf16)
    qaug[HEAD+16:,:]=jnp.zeros((128-HEAD-16,W),bf16)
    r=[jnp.broadcast_to(routes_ref[k:k+1,:],(8,TB))[None] for k in range(TOP)]
    for k0 in range(0,TOP,4):
        sel=[jnp.zeros((HEAD//8,8,TB),f32) for _ in range(4)]
        for e in range(experts):
            v=dct_ref[e*HEAD:(e+1)*HEAD,:].astype(f32).reshape(HEAD//8,8,TB)
            sel=[jnp.where(r[k0+k]==e,v,sel[k]) for k in range(4)]
        for k in range(4):
            sl=slice((k0+k)*TB,(k0+k+1)*TB)
            dc=(sel[k].reshape(HEAD,TB)*gates_ref[k0+k:k0+k+1,:]).astype(bf16)
            daug[0:HEAD,sl]=dc
            rhs[HEAD:,W+(k0+k)*TB:W+(k0+k+1)*TB]=dc
            dq[0:1,sl]=jnp.sum(dc.astype(f32)*ctx_ref[0,:,sl].astype(f32),axis=0,keepdims=True)
    hi,mid,lo=split3(-dq[0:1,:])
    daug[HEAD:HEAD+16,:]=jnp.concatenate([hi,mid,lo,jnp.zeros((13,W),f32)],0).astype(bf16)
    daug[HEAD+16:,:]=jnp.zeros((128-HEAD-16,W),bf16)
    dq[...]=jnp.zeros_like(dq)
    q0=c*tok+i*TB
    nfull=q0//KB
    kd=pl.multiple_of(nfull*KB,KB)
    def block(k0,mask):
        p=jnp.exp2(jnp.dot(kaug_ref[pl.ds(k0,KB),:],qaug[...],preferred_element_type=f32))
        if mask is not None:
            p=jnp.concatenate([jnp.where(mask,p[:,k*TB:(k+1)*TB],0.0) for k in range(TOP)],1)
        dp=jnp.dot(vaug_ref[pl.ds(k0,KB),:],daug[...],preferred_element_type=f32)
        pds[:,W:]=p.astype(bf16)
        pds[:,:W]=(p*dp).astype(bf16)
        dq[...]+=jnp.dot(kt_ref[:,pl.ds(k0,KB)],pds[:,:W],preferred_element_type=f32)
        dkv_ref[pl.ds(k0,KB),:]+=lax.dot_general(pds[...],rhs[...],NT,preferred_element_type=f32)
    def body(b,_):
        block(pl.multiple_of(b*KB,KB),None)
        return 0
    lax.fori_loop(0,nfull,body,0)
    kp=lax.broadcasted_iota(jnp.int32,(KB,TB),0)+(kd-q0)
    tp=lax.broadcasted_iota(jnp.int32,(KB,TB),1)
    block(kd,kp<=tp)
    dq[...]*=0.125
    for h0 in range(0,HEAD,32):
        g=[dq[h0:h0+32,k*TB:(k+1)*TB].reshape(4,8,TB) for k in range(TOP)]
        for e in range(experts):
            o=jnp.zeros((4,8,TB),f32)
            for k in range(TOP):
                o=jnp.where(r[k]==e,g[k],o)
            dqd_ref[e*HEAD+h0:e*HEAD+h0+32,:]=o.reshape(32,TB).astype(bf16)
    @pl.when(i==pl.num_programs(0)-1)
    def _():
        lane=lax.broadcasted_iota(jnp.int32,(1,128),1)
        dkv_ref[...]*=jnp.where(lane<HEAD,LN2,1.0)

def attn_bwd(cidx, dct, q, ctx, lse, routesT, gatesT, qdoc, kaug, vaug, kt, KB=256):
    tok=routesT.shape[1]; experts=dct.shape[0]//HEAD; keys=kaug.shape[0]; n=tok//TB
    full=lambda a: pl.BlockSpec(a.shape,lambda i,*_:(0,)*a.ndim)
    blk=lambda rows: pl.BlockSpec((rows,TB),lambda i,*_:(0,i))
    return pl.pallas_call(
        functools.partial(attn_bwd_kernel,experts=experts,tok=tok,KB=KB),
        grid_spec=pltpu.PrefetchScalarGridSpec(num_scalar_prefetch=1,grid=(n,),
          in_specs=[blk(experts*HEAD),
            pl.BlockSpec((1,HEAD,W),lambda i,*_:(i,0,0)),
            pl.BlockSpec((1,HEAD,W),lambda i,*_:(i,0,0)),
            pl.BlockSpec((1,1,W),lambda i,*_:(i,0,0)),
            blk(TOP),blk(TOP),blk(8),full(kaug),full(vaug),full(kt)],
          out_specs=[blk(experts*HEAD),pl.BlockSpec((keys,128),lambda i,*_:(0,0))],
          scratch_shapes=[pltpu.VMEM((128,W),bf16),pltpu.VMEM((128,W),bf16),pltpu.VMEM((128,2*W),bf16),
            pltpu.VMEM((KB,2*W),bf16),pltpu.VMEM((HEAD,W),f32)]),
        out_shape=[jax.ShapeDtypeStruct((experts*HEAD,tok),bf16),
          jax.ShapeDtypeStruct((keys,128),f32)],
        compiler_params=pltpu.CompilerParams(vmem_limit_bytes=60*2**20),
        name="attn_bwd",
    )(cidx,dct,q,ctx,lse,routesT,gatesT,qdoc,kaug,vaug,kt)


def dot(a,b,dims=NN): return lax.dot_general(a,b,dims,preferred_element_type=f32)

def ffn_kernel(cd_ref, wo_ref, tok_ref, cot_ref, g2_ref, s2_ref, up_ref, upb_ref, down_ref, downb_ref,
               out_ref, dmid_ref, dct_ref, gwo_ref, gup_ref, gub_ref, gdown_ref, gsm_ref,
               mid, xhat, rstd, act, actT, dffn, acc, da2):
    j=pl.program_id(0); n=pl.num_programs(0)
    @pl.when(j==0)
    def _():
        m=tok_ref[...]+dot(cd_ref[...],wo_ref[...],TN)
        mid[...]=m
        cen=m-jnp.mean(m,axis=-1,keepdims=True)
        rs=lax.rsqrt(jnp.mean(cen*cen,axis=-1,keepdims=True)+1e-5)
        xh=cen*rs
        xhat[...]=xh; rstd[...]=jnp.broadcast_to(rs,rstd.shape)
        a=(xh*g2_ref[...]+s2_ref[...])
        act[...]=a.astype(bf16)
        actT[...]=jnp.transpose(a).astype(bf16)
        dffn[...]=cot_ref[...].astype(bf16)
        acc[...]=jnp.zeros_like(acc); da2[...]=jnp.zeros_like(da2)
    up=up_ref[...].astype(bf16); down=down_ref[...].astype(bf16)
    pre=dot(act[...],up)+upb_ref[...]
    x2=pre*pre
    th=jnp.tanh(pre*(C0+C0*C1*x2))
    h=0.5*(1.0+th)
    hid=(pre*h).astype(bf16)
    gp=h+(0.5*pre)*(1.0-th*th)*(C0+3.0*C0*C1*x2)
    acc[...]+=dot(hid,down)
    gdown_ref[...]=dot(hid,dffn[...],TN).astype(gdown_ref.dtype)
    dp=dot(dffn[...],down,NT)*gp
    dpb=dp.astype(bf16)
    gub_ref[...]=jnp.sum(dpb.astype(f32),axis=0,keepdims=True)
    gup_ref[...]=dot(actT[...],dpb).astype(gup_ref.dtype)
    da2[...]+=dot(dpb,up,NT)
    @pl.when(j==n-1)
    def _():
        out_ref[...]=mid[...]+acc[...]+downb_ref[...]
        d=da2[...]; xh=xhat[...]
        gx=d*g2_ref[...]
        dm=cot_ref[...]+rstd[:,0:1]*(gx-jnp.mean(gx,axis=-1,keepdims=True)-xh*jnp.mean(gx*xh,axis=-1,keepdims=True))
        dmid_ref[...]=dm
        dmb=dm.astype(bf16)
        dct_ref[...]=dot(wo_ref[...],dmb,NT).astype(bf16)
        gwo_ref[...]=dot(cd_ref[...],dmb).astype(gwo_ref.dtype)
        gsm_ref[...]=jnp.concatenate([jnp.sum(d*xh,axis=0,keepdims=True),jnp.sum(d,axis=0,keepdims=True),
            jnp.sum(dffn[...].astype(f32),axis=0,keepdims=True),jnp.zeros((5,D),f32)],0)

def ffn(cd, wo, tokens, cot, g2, s2, up, upb, down, downb, FB=256, gdt=bf16):
    tok=tokens.shape[0]; FF=up.shape[1]; n=FF//FB; EH=wo.shape[0]
    full=lambda a: pl.BlockSpec(a.shape,lambda i:(0,)*a.ndim,pipeline_mode=pl.Buffered(1))
    fo=lambda *s: pl.BlockSpec(s,lambda i:(0,)*len(s))
    sd=jax.ShapeDtypeStruct
    return pl.pallas_call(ffn_kernel,grid=(n,),
        in_specs=[full(cd),full(wo),full(tokens),full(cot),full(g2),full(s2),
          pl.BlockSpec((D,FB),lambda i:(0,i)),pl.BlockSpec((1,FB),lambda i:(0,i)),
          pl.BlockSpec((FB,D),lambda i:(i,0)),full(downb)],
        out_specs=[fo(tok,D),fo(tok,D),fo(EH,tok),fo(EH,D),
          pl.BlockSpec((D,FB),lambda i:(i,0)),pl.BlockSpec((1,FB),lambda i:(0,i)),
          pl.BlockSpec((FB,D),lambda i:(i,0)),fo(8,D)],
        out_shape=[sd((tok,D),f32),sd((tok,D),f32),sd((EH,tok),bf16),sd((EH,D),gdt),
          sd((n*D,FB),gdt),sd((1,FF),f32),sd((FF,D),gdt),sd((8,D),f32)],
        scratch_shapes=[pltpu.VMEM((tok,D),f32),pltpu.VMEM((tok,D),f32),pltpu.VMEM((tok,128),f32),
          pltpu.VMEM((tok,D),bf16),pltpu.VMEM((D,tok),bf16),pltpu.VMEM((tok,D),bf16),
          pltpu.VMEM((tok,D),f32),pltpu.VMEM((tok,D),f32)],
        compiler_params=pltpu.CompilerParams(vmem_limit_bytes=60*2**20),
        name="ffn",
    )(cd,wo,tokens,cot,g2,s2,up,upb,down,downb)


def partner(bit):
    ax, m = bit
    i = lax.axis_index(ax)
    b = lax.rem(i // m, 2)
    return {a: (i + m - 2 * m * b if a == ax else lax.axis_index(a)) for a in AXES}, b


def mesh_bits(sizes):
    return {a: [(a, 1 << i) for i in range(sizes[a].bit_length() - 1)] for a in AXES}


def chain_orders(sizes):
    b = mesh_bits(sizes)
    e, d, c = b["exp"], b["dp"], b["ctx"]
    late = e + d + c
    if len(d) + len(c) > 2:
        return [late, late, late]
    return [e[:1] + d + c + e[1:], e[:1] + c + d + e[1:], late]


def greet(bits):
    bar = pltpu.get_barrier_semaphore()
    for bit in bits:
        pl.semaphore_signal(bar, inc=1, device_id=partner(bit)[0], device_id_type=MESH)
    pl.semaphore_wait(bar, len(bits))


def rows(ref, start, n):
    return ref.at[pl.ds(pl.multiple_of(start, 16), n), :]


def add_rows(dst, d0, a, a0, b, b0, n):
    ch = math.gcd(n, 64)

    @pl.loop(0, n // ch)
    def _(t):
        o = pl.multiple_of(t * ch, ch)
        g = lambda r, s: r[pl.ds(pl.multiple_of(s + o, 16), ch), :].astype(f32)
        dst[pl.ds(pl.multiple_of(d0 + o, 16), ch), :] = (g(a, a0) + g(b, b0)).astype(bf16)


def chain_plan(n, order):
    plan = []
    for bit in order:
        halve = n % 32 == 0
        n = n // 2 if halve else n
        plan.append((halve, bit, n))
    return plan


class Chain:
    def __init__(self, src, work, final, base, n, order, fbase=None):
        self.src, self.out, self.base, self.n, self.order = src, work, base, n, order
        self.final, self.fbase = final, fbase
        self.plan = chain_plan(n, order)
        self.landed = sum(m for _, _, m in self.plan)
        self.back = [i for i in reversed(range(len(order))) if self.plan[i][0] and (fbase is None or order[i][0] != "exp")]
        if fbase is not None:
            self.back.sort(key=lambda i: (order[i][0], order[i][1]), reverse=True)
        self.nsem = len(self.plan) + len(self.back)
        self.nsteps = self.nsem + 1
        self.copies = {}

    def place(self, land, lbase, ss, rs, sem):
        self.land, self.ss, self.rs, self.sem = land, ss, rs, sem
        self.lb, self.offs, off = [], [], self.base
        for halve, bit, m in self.plan:
            self.lb.append(lbase)
            lbase += m
            b = partner(bit)[1]
            self.offs.append((off + b * m, off + (1 - b) * m) if halve else (off, off))
            off = self.offs[-1][0]
        self.last = off

    def copy(self, i, src, dst, bit):
        c = pltpu.make_async_remote_copy(
            src_ref=src, dst_ref=dst, send_sem=self.ss.at[self.sem + i], recv_sem=self.rs.at[self.sem + i],
            device_id=partner(bit)[0], device_id_type=MESH)
        c.start()
        self.copies[i] = c

    def fold(self, i):
        self.copies[i].wait()
        d = self.offs[i][0]
        last = i == len(self.plan) - 1
        add_rows(self.final if last else self.out, self.final_range(0)[0] if last else d,
                 self.src if i == 0 else self.out, d, self.land, self.lb[i], self.plan[i][2])

    def final_range(self, j):
        if self.fbase is None:
            i = self.back[j] if j < len(self.back) else 0
            return (self.offs[i][0], self.plan[i][2]) if j or self.plan[-1][0] else (self.last, self.plan[-1][2])
        m = self.plan[-1][2]
        off, size = self.fbase, m
        for k, i in enumerate(self.back):
            if k < j:
                size *= 2
        w = m
        for k, i in enumerate(self.back):
            if k >= j:
                off = off + partner(self.order[i])[1] * w
            w *= 2
        return off, size

    def step(self, k):
        m = len(self.plan)
        if k < m:
            if k:
                self.fold(k - 1)
            _, bit, n = self.plan[k]
            self.copy(k, rows(self.src if k == 0 else self.out, self.offs[k][1], n), rows(self.land, self.lb[k], n), bit)
            return
        j = k - m
        if j == 0:
            self.fold(m - 1)
        else:
            self.copies[k - 1].wait()
        if j < len(self.back):
            i = self.back[j]
            r = rows(self.final, *self.final_range(j))
            self.copy(k, r, r, self.order[i])


def place_all(chains, land, ss, rs):
    lb = sem = 0
    for c in chains:
        c.place(land, lb, ss, rs, sem)
        lb += c.landed
        sem += c.nsem


def owner_rows(g, sizes, order):
    n, width = g.shape
    bits = [bit for halve, bit, _ in chain_plan(n, order) if halve]
    own = [b for b in bits if b[0] == "exp"]
    rest = sorted([b for b in bits if b[0] != "exp"])
    nat = sorted(own, reverse=True) + rest
    block = n >> len(nat)
    y = g.reshape((2,) * len(nat) + (block, width))
    y = y.transpose([nat.index(b) for b in bits] + [len(nat), len(nat) + 1])
    return y.reshape(n, width)


def dense_parts(n, orders):
    a = n * 3 // 8 // 32 * 32
    return [(0, a, orders[0]), (a, a, orders[1]), (2 * a, n - 2 * a, orders[2])]


def make_chains(orders, gd, gu, go, gq, sm, gd_o, gu_o, sm_o, go_f, gq_f, gd_w, gu_w, sm_w, go_w, gq_w):
    chains = []
    for src, work, out in ((gd, gd_w, gd_o), (gu, gu_w, gu_o)):
        chains += [Chain(src, work, out, b, n, o) for b, n, o in dense_parts(src.shape[0], orders)]
    for src, work, fin in ((go, go_w, go_f), (gq, gq_w, gq_f)):
        n = src.shape[0] // 3
        chains += [Chain(src, work, fin, j * n, n, orders[j], j * HEAD) for j in range(3)]
    chains.append(Chain(sm, sm_w, sm_o, 0, sm.shape[0], orders[0]))
    return chains


def reduce_kernel(sizes, *refs):
    land, ss, rs = refs[-3:]
    greet([b for a in AXES for b in mesh_bits(sizes)[a]])
    chains = make_chains(chain_orders(sizes), *refs[:-3])
    place_all(chains, land, ss, rs)
    for t in range(max(c.nsteps for c in chains)):
        for c in chains:
            if t < c.nsteps:
                c.step(t)


def reduce_all(sizes, gd, gu, go, gq, sm):
    shapes = [jax.ShapeDtypeStruct(v.shape, bf16) for v in (gd, gu, go, gq, sm)]
    chains = make_chains(chain_orders(sizes), *shapes, *[None] * 10)
    nsem = sum(c.nsem for c in chains)
    land = sum(c.landed for c in chains)
    v = pl.BlockSpec(memory_space=pltpu.VMEM)
    fin = jax.ShapeDtypeStruct((go.shape[0] // sizes["exp"], go.shape[1]), bf16)
    return pl.pallas_call(
        functools.partial(reduce_kernel, sizes),
        out_shape=[shapes[0], shapes[1], shapes[4], fin, fin],
        in_specs=[v] * 5,
        out_specs=[v] * 5,
        scratch_shapes=[pltpu.VMEM(t.shape, bf16) for t in (gd, gu, sm, go, gq)]
        + [pltpu.VMEM((land, D), bf16), pltpu.SemaphoreType.DMA((nsem,)), pltpu.SemaphoreType.DMA((nsem,))],
        compiler_params=pltpu.CompilerParams(collective_id=0, has_side_effects=True, vmem_limit_bytes=60 * 2**20),
        name="reduce_all",
    )(gd, gu, go, gq, sm)


def local(sizes, tokens, lengths, routes, route_gates, cotangent, gain_one, shift_one, kv_weight,
          query_weight, out_weight, gain_two, shift_two, up_weight, up_bias, down_weight, down_bias):
    x = tokens[0]
    tok = x.shape[0]
    ncx = sizes["ctx"]
    group = tok * ncx
    nexp = query_weight.shape[0]
    experts = nexp * sizes["exp"]
    cidx = lax.axis_index("ctx")
    wq_own = jnp.swapaxes(query_weight, 1, 2).reshape(nexp * HEAD, D).astype(bf16)
    wo_own = out_weight.reshape(nexp * HEAD, D).astype(bf16)
    wq = lax.all_gather(wq_own, "exp", axis=0, tiled=True)
    wo = lax.all_gather(wo_own, "exp", axis=0, tiled=True)
    cen = x - jnp.mean(x, axis=-1, keepdims=True)
    rs1 = lax.rsqrt(jnp.mean(cen * cen, axis=-1, keepdims=True) + 1e-5)
    xh1 = cen * rs1
    act = (xh1 * gain_one + shift_one).astype(bf16)
    kvw = kv_weight.astype(bf16)
    kv_own = dot(act, kvw).astype(bf16)
    kv = lax.all_gather(kv_own, "ctx", axis=0, tiled=True)
    keys, vals = kv[:, :HEAD], kv[:, HEAD:]
    kn = jnp.max(jnp.sum(jnp.square(keys.astype(f32)), axis=1)).reshape(1)
    pos = jnp.arange(group, dtype=jnp.int32)
    docs, end = jnp.zeros_like(pos), 0
    for d in range(lengths.shape[1] - 1):
        end = end + lengths[0, d]
        docs = docs + (pos >= end).astype(jnp.int32)
    hot = (docs[:, None] == jnp.arange(3)[None, :]).astype(bf16)
    one3 = jnp.ones((group, 3), bf16)
    kaug = jnp.concatenate([keys, hot, one3, jnp.zeros((group, HEAD - 6), bf16)], axis=1)
    vaug = jnp.concatenate([vals, one3, jnp.zeros((group, HEAD - 3), bf16)], axis=1)
    kt = keys.T
    vt = jnp.concatenate([vals.T, jnp.ones((1, group), bf16), jnp.zeros((15, group), bf16)], axis=0)
    qdocs = lax.dynamic_slice_in_dim(docs, cidx * tok, tok)
    slot = jnp.arange(8, dtype=jnp.int32)[:, None]
    qdoc = jnp.where((qdocs[None, :] == slot) | (slot > 2), 0.0, NEG).astype(f32)
    routes_t = routes[0].T
    gates_t = route_gates[0].T
    cvec = cidx.reshape(1).astype(jnp.int32)

    cd, q, ctx, lse = attn_fwd(cvec, act, wq, routes_t, gates_t, qdoc, kaug, vt, kn, KB=384)
    row = lambda v: v.reshape(1, -1)
    out, dmid, dct, gwo, gup, gub, gdown, gsm = ffn(
        cd, wo, x, cotangent[0], row(gain_two), row(shift_two), up_weight, row(up_bias),
        down_weight, row(down_bias), FB=512)
    dqd, dkv_part = attn_bwd(cvec, dct, q, ctx, lse, routes_t, gates_t, qdoc, kaug, vaug, kt, KB=384)
    dkv = lax.psum_scatter(dkv_part, "ctx", scatter_dimension=0, tiled=True).astype(bf16)
    gkv = dot(act, dkv, TN)
    gwq = dot(dqd, act).astype(bf16)
    da1 = dot(dqd, wq, TN) + dot(dkv, kvw, NT)
    gg1 = jnp.sum(da1 * xh1, axis=0)
    gs1 = jnp.sum(da1, axis=0)
    gx = da1 * gain_one
    dx = dmid + rs1 * (gx - jnp.mean(gx, axis=-1, keepdims=True) - xh1 * jnp.mean(gx * xh1, axis=-1, keepdims=True))

    orders = chain_orders(sizes)

    def parts(g):
        g = g.reshape(sizes["exp"], nexp, HEAD, D)
        return jnp.concatenate([owner_rows(g[:, j].reshape(-1, D), sizes, orders[j]) for j in range(nexp)], axis=0)

    small = jnp.concatenate([gkv.reshape(-1, D), gub.reshape(-1, D), gsm[:3], row(gg1), row(gs1)], axis=0)
    used = small.shape[0]
    small = jnp.pad(small.astype(bf16), ((0, 256 - used), (0, 0)))
    gdown, gup, small, go, gq = reduce_all(sizes, gdown, gup, parts(gwo), parts(gwq), small)
    go = go.astype(f32).reshape(nexp, HEAD, D)
    gq = jnp.swapaxes(gq.astype(f32).reshape(nexp, HEAD, D), 1, 2)
    small = small[:used].astype(f32)
    nkv, nub = gkv.size // D, gub.size // D
    gkv = small[:nkv].reshape(gkv.shape)
    gub = small[nkv:nkv + nub].reshape(-1)
    tail = small[nkv + nub:]
    gup = gup.astype(f32).reshape(-1, D, gup.shape[1]).transpose(1, 0, 2).reshape(D, -1)
    return (out[None], dx[None], tail[3], tail[4], gkv, gq, go, tail[0], tail[1], gup, gub,
            gdown.astype(f32), tail[2])


def solution(mesh):
    tok3 = P(("dp", "exp"), "ctx", None)
    ex = P("exp", None, None)
    r = P()
    in_specs = (tok3, P(("dp", "exp"), None), tok3, tok3, tok3, r, r, r, ex, ex, r, r, r, r, r, r)
    out_specs = (tok3, tok3, r, r, r, ex, ex, r, r, r, r, r, r)
    fn = functools.partial(local, dict(mesh.shape))
    return jax.shard_map(fn, mesh=mesh, in_specs=in_specs, out_specs=out_specs, check_vma=False)
```

```python
import functools
import math

import jax
import jax.numpy as jnp
from jax import lax
from jax.experimental import pallas as pl
from jax.experimental.pallas import tpu as pltpu
from jax.sharding import PartitionSpec as P

f32 = jnp.float32
bf16 = jnp.bfloat16
D = 512
HEAD = 64
TOP = 8
TB = 128
W = TOP * TB
NEG = -1e30
LOG2E = math.log2(math.e)
LN2 = math.log(2.0)
SMALL = 576
KBB = 384
STRIDE = 8
JOIN = 2
SAFE = 50.0
NN = (((1,), (0,)), ((), ()))
NT = (((1,), (1,)), ((), ()))
TN = (((0,), (0,)), ((), ()))
C0 = math.sqrt(2 / math.pi)
C1 = 0.044715
MESH = pl.DeviceIdType.MESH
AXES = ("dp", "ctx", "exp")


def attn_fwd_kernel(cidx_ref, act_ref, wq_ref, routes_ref, gates_ref, qdoc_ref, kaug_ref, vt_ref, kn_ref,
                    cd_ref, q_ref, ctx_ref, lse_ref,
                    qt, qaug, s, acc, *, experts, tok, KB):
    i=pl.program_id(0)
    c=cidx_ref[0]
    qt[...]=lax.dot_general(wq_ref[...], act_ref[...], NT, preferred_element_type=f32)*(0.125*LOG2E)
    n2=[]
    for k0 in range(0,TOP,4):
        r=[jnp.broadcast_to(routes_ref[k0+k:k0+k+1,:],(8,TB))[None] for k in range(4)]
        sel=[jnp.zeros((HEAD//8,8,TB),f32) for _ in range(4)]
        for e in range(experts):
            v=qt[e*HEAD:(e+1)*HEAD,:].reshape(HEAD//8,8,TB)
            sel=[jnp.where(r[k]==e,v,sel[k]) for k in range(4)]
        for k in range(4):
            sk=sel[k].reshape(HEAD,TB)
            n2.append(jnp.max(jnp.sum(sk*sk,axis=0,keepdims=True)))
            qaug[0:HEAD,(k0+k)*TB:(k0+k+1)*TB]=sk.astype(bf16)
    n2=functools.reduce(jnp.maximum,n2)*kn_ref[0]
    fast=n2<=SAFE*SAFE
    q_ref[0]=qaug[0:HEAD,:]
    qd=qdoc_ref[...]
    qaug[HEAD:HEAD+16,:]=jnp.concatenate([jnp.concatenate([qd,jnp.zeros_like(qd)],0)]*TOP,1).astype(bf16)
    qaug[HEAD+16:,:]=jnp.zeros((128-HEAD-16,W),bf16)
    q0=c*tok+i*TB
    nfull=q0//KB
    kd=pl.multiple_of(nfull*KB,KB)
    kp=lax.broadcasted_iota(jnp.int32,(KB,TB),0)+(kd-q0)
    tp=lax.broadcasted_iota(jnp.int32,(KB,TB),1)
    mask=kp<=tp
    acc[...]=jnp.zeros_like(acc)
    def scores(k0,n):
        return jnp.dot(kaug_ref[pl.ds(k0,n),:],qaug[...],preferred_element_type=f32)
    def masked(x):
        return jnp.concatenate([jnp.where(mask,x[:,k*TB:(k+1)*TB],NEG) for k in range(TOP)],1)
    def pv(k0,n,p):
        acc[...]+=jnp.dot(vt_ref[:,pl.ds(k0,n)],p,preferred_element_type=f32)
    def finish(m):
        l=acc[HEAD:HEAD+1,:]
        lse_ref[0]=m+jnp.log2(l)
        acc[0:HEAD,:]=acc[0:HEAD,:]*(1.0/l)
    @pl.when(fast)
    def _():
        def body(b,_):
            k0=pl.multiple_of(b*KB,KB)
            pv(k0,KB,jnp.exp2(scores(k0,KB)).astype(bf16))
            return 0
        lax.fori_loop(0,nfull,body,0)
        pv(kd,KB,jnp.exp2(masked(scores(kd,KB))).astype(bf16))
        finish(0.0)
    @pl.when(jnp.logical_not(fast))
    def _():
        def spass(b,m):
            k0=pl.multiple_of(b*KB,KB)
            x=scores(k0,KB)
            s[pl.ds(k0,KB),:]=x
            return jnp.maximum(m,jnp.max(x.reshape(KB//8,8,W),axis=0))
        m=lax.fori_loop(0,nfull,spass,jnp.full((8,W),NEG*2,f32))
        x=masked(scores(kd,KB))
        s[pl.ds(kd,KB),:]=x
        m=jnp.maximum(m,jnp.max(x.reshape(KB//8,8,W),axis=0))
        m=jnp.max(m,axis=0,keepdims=True)
        def ppass(b,_):
            k0=pl.multiple_of(b*KB,KB)
            pv(k0,KB,jnp.exp2(s[pl.ds(k0,KB),:]-m).astype(bf16))
            return 0
        lax.fori_loop(0,nfull+1,ppass,0)
        finish(m)
    ctx_ref[0]=acc[0:HEAD,:].astype(bf16)
    for k in range(TOP):
        acc[0:HEAD,k*TB:(k+1)*TB]*=gates_ref[k:k+1,:]
    r=[jnp.broadcast_to(routes_ref[k:k+1,:],(8,TB))[None] for k in range(TOP)]
    for h0 in range(0,HEAD,32):
        g=[acc[h0:h0+32,k*TB:(k+1)*TB].reshape(4,8,TB) for k in range(TOP)]
        for e in range(experts):
            o=jnp.zeros((4,8,TB),f32)
            for k in range(TOP):
                o=jnp.where(r[k]==e,g[k],o)
            cd_ref[e*HEAD+h0:e*HEAD+h0+32,:]=o.reshape(32,TB).astype(bf16)

def attn_fwd(cidx, act, wq, routesT, gatesT, qdoc, kaug, vt, kn, KB=256):
    tok=act.shape[0]; experts=wq.shape[0]//HEAD; keys=kaug.shape[0]; n=tok//TB; vr=vt.shape[0]
    full=lambda a: pl.BlockSpec(a.shape,lambda i,*_:(0,)*a.ndim)
    return pl.pallas_call(
        functools.partial(attn_fwd_kernel,experts=experts,tok=tok,KB=KB),
        grid_spec=pltpu.PrefetchScalarGridSpec(num_scalar_prefetch=1,grid=(n,),
          in_specs=[pl.BlockSpec((TB,D),lambda i,*_:(i,0)),full(wq),
            pl.BlockSpec((TOP,TB),lambda i,*_:(0,i)),pl.BlockSpec((TOP,TB),lambda i,*_:(0,i)),
            pl.BlockSpec((8,TB),lambda i,*_:(0,i)),full(kaug),full(vt),pl.BlockSpec(memory_space=pltpu.SMEM)],
          out_specs=[pl.BlockSpec((experts*HEAD,TB),lambda i,*_:(0,i)),
            pl.BlockSpec((1,HEAD,W),lambda i,*_:(i,0,0)),
            pl.BlockSpec((1,HEAD,W),lambda i,*_:(i,0,0)),
            pl.BlockSpec((1,1,W),lambda i,*_:(i,0,0))],
          scratch_shapes=[pltpu.VMEM((experts*HEAD,TB),f32),pltpu.VMEM((128,W),bf16),
            pltpu.VMEM((keys,W),f32),pltpu.VMEM((vr,W),f32)]),
        out_shape=[jax.ShapeDtypeStruct((experts*HEAD,tok),bf16),
          jax.ShapeDtypeStruct((n,HEAD,W),bf16),jax.ShapeDtypeStruct((n,HEAD,W),bf16),
          jax.ShapeDtypeStruct((n,1,W),f32)],
        compiler_params=pltpu.CompilerParams(vmem_limit_bytes=60*2**20),
        name="attn_fwd",
    )(cidx,act,wq,routesT,gatesT,qdoc,kaug,vt,kn)


def dot(a, b, dims=NN):
    return lax.dot_general(a, b, dims, preferred_element_type=f32)


def split3(x):
    hi = x.astype(bf16).astype(f32)
    r = x - hi
    mid = r.astype(bf16).astype(f32)
    return hi, mid, r - mid


class Here:
    def __init__(self, sizes):
        at = {a: lax.axis_index(a) for a in AXES}
        self.bit, self.dev = {}, {}
        for bits in mesh_bits(sizes).values():
            for ax, m in bits:
                b = lax.rem(at[ax] // m, 2)
                self.bit[ax, m] = b
                self.dev[ax, m] = tuple(at[a] + m - 2 * m * b if a == ax else at[a] for a in AXES)


def mesh_bits(sizes):
    return {a: [(a, 1 << i) for i in range(sizes[a].bit_length() - 1)] for a in AXES}


def chain_orders(sizes):
    b = mesh_bits(sizes)
    e, d, c = b["exp"], b["dp"], b["ctx"]
    late = e + d + c
    if len(d) + len(c) > 2:
        return [late, late, late]
    return [e[:1] + d + c + e[1:], e[:1] + c + d + e[1:], late]


def chain_plan(n, order):
    plan = []
    for bit in order:
        halve = n % 32 == 0
        n = n // 2 if halve else n
        plan.append((halve, bit, n))
    return plan


def rows(ref, start, n):
    return ref.at[pl.ds(pl.multiple_of(start, 16), n), :]


def add_rows(dst, d0, a, a0, b, b0, n):
    ch = math.gcd(n, 64)

    @pl.loop(0, n // ch)
    def _(t):
        o = pl.multiple_of(t * ch, ch)
        g = lambda r, s: r[pl.ds(pl.multiple_of(s + o, 16), ch), :]
        dst[pl.ds(pl.multiple_of(d0 + o, 16), ch), :] = g(a, a0) + g(b, b0)


def block_places(n, order, owner):
    bits = [bit for halve, bit, _ in chain_plan(n, order) if halve]
    own = sorted([b for b in bits if b[0] == owner], reverse=True)
    nat = own + sorted([b for b in bits if b[0] != owner])
    places = []
    for i in range(1 << len(nat)):
        v = {b: (i >> (len(nat) - 1 - k)) & 1 for k, b in enumerate(nat)}
        places.append(sum(v[b] << (len(bits) - 1 - k) for k, b in enumerate(bits)))
    return n >> len(nat), places


class Chain:
    def __init__(self, work, final, base, n, order, owner=None, fbase=0):
        self.work, self.final, self.base, self.n, self.order = work, final, base, n, order
        self.owner, self.fbase = owner, fbase
        self.plan = chain_plan(n, order)
        self.landed = sum(m for _, _, m in self.plan)
        self.back = [i for i in reversed(range(len(order))) if self.plan[i][0] and order[i][0] != owner]
        if owner:
            self.back.sort(key=lambda i: order[i], reverse=True)
        self.m = len(self.plan)
        self.nsem = self.m + len(self.back)
        self.nsteps = self.nsem + 1

    def place(self, here, land, lbase, ss, rs, sem):
        self.here, self.land, self.ss, self.rs, self.sem = here, land, ss, rs, sem
        self.lb = []
        for _, _, m in self.plan:
            self.lb.append(lbase)
            lbase += m
        self.offs = self.offsets()

    def offsets(self):
        offs, off = [], self.base
        for halve, bit, m in self.plan:
            b = self.here.bit[bit]
            offs.append((off + b * m, off + (1 - b) * m) if halve else (off, off))
            off = offs[-1][0]
        return offs

    def final_range(self, j):
        m = self.plan[-1][2]
        if self.owner is None:
            offs = self.offs
            if j == 0:
                return offs[-1][0], m
            i = self.back[j]
            return offs[i][0], self.plan[i][2]
        off, w = self.fbase, m
        for k, i in enumerate(self.back):
            if k >= j:
                off = off + self.here.bit[self.order[i]] * w
            w *= 2
        return off, m << j

    def copy(self, k):
        if k < self.m:
            _, bit, n = self.plan[k]
            src, dst = rows(self.work, self.offs[k][1], n), rows(self.land, self.lb[k], n)
        else:
            bit = self.order[self.back[k - self.m]]
            src = dst = rows(self.final, *self.final_range(k - self.m))
        return pltpu.make_async_remote_copy(
            src_ref=src, dst_ref=dst, send_sem=self.ss.at[self.sem + k], recv_sem=self.rs.at[self.sem + k],
            device_id=self.here.dev[bit], device_id_type=MESH)

    def step(self, k):
        if k:
            self.copy(k - 1).wait()
            if k <= self.m:
                i = k - 1
                last = i == self.m - 1
                d = self.offs[i][0]
                add_rows(self.final if last else self.work, self.final_range(0)[0] if last else d,
                         self.work, d, self.land, self.lb[i], self.plan[i][2])
        if k < self.nsem:
            self.copy(k).start()


def greet(here):
    bar = pltpu.get_barrier_semaphore()
    for dev in here.dev.values():
        pl.semaphore_signal(bar, inc=1, device_id=dev, device_id_type=MESH)
    pl.semaphore_wait(bar, len(here.dev))


def dense_parts(n, orders):
    a = n * 3 // 8 // 32 * 32
    return [(0, a, orders[0]), (a, a, orders[1]), (2 * a, n - 2 * a, orders[2])]


def make_chains(sizes, steps, part, nexp, keys, dsrc, fin, osrc, go, qsrc, gq, ksrc, kfin, ssrc, sfin):
    orders = chain_orders(sizes)
    n = sizes["exp"] * HEAD
    kbits = mesh_bits(sizes)["ctx"][::-1]
    part = part * JOIN
    dense = [[Chain(dsrc, fin, j * part + b, m, o) for b, m, o in dense_parts(part, orders)] for j in range(steps // JOIN)]
    return dict(
        dense=dense,
        o=[Chain(osrc, go, j * n, n, orders[j % 3], "exp", j * HEAD) for j in range(nexp)],
        q=[Chain(qsrc, gq, j * n, n, orders[j % 3], "exp", j * HEAD) for j in range(nexp)],
        k=[Chain(ksrc, kfin, 0, keys, kbits, "ctx", 0)],
        s=[Chain(ssrc, sfin, 0, SMALL, orders[0])],
    )


def flat(chains):
    wide = [c for g in chains["dense"] for c in g] + chains["o"] + chains["q"]
    return wide, chains["k"] + chains["s"]


def place_all(here, chains, land, nland, ss, rs):
    sem = 0
    for group, buf in zip(flat(chains), (land, nland)):
        lb = 0
        for c in group:
            c.place(here, buf, lb, ss, rs, sem)
            lb += c.landed
            sem += c.nsem


def mega_kernel(sizes, nf, nb, nexp, fb,
                cd, wo, tok, cot, g2, s2, up_ref, upb, down_ref, downb, q_ref, ctx_ref, lse_ref, routes_ref, gates_ref,
                qdoc_ref, kaug_ref, vaug_ref, kt_ref, act1, wq, kvw, g1,
                out, dx, fin_o, go_o, gq_o, sm_o,
                mid, rstd, act, actT, dffn, dct, dqd, gub, gsm,
                qaug, daug, rhs, pds, dq, dkv,
                dsrc, fin, osrc, go, qsrc, gq, ksrc, kfin, ssrc, sfin, land, nland, ss, rs, lsem):
    s = pl.program_id(0)
    experts = cd.shape[0] // HEAD
    ntok, keys = tok.shape[0], kaug_ref.shape[0]
    part = 2 * fb
    chains = make_chains(sizes, nf, part, nexp, keys, dsrc, fin, osrc, go, qsrc, gq, ksrc, kfin, ssrc, sfin)
    here = Here(sizes)
    place_all(here, chains, land, nland, ss, rs)
    ticks = [(j, p) for j in range(nf) for p in range(3)] + [(nf + i, p) for i in range(nb) for p in range(4)]
    ticks += [(nf + nb, p) for p in range(4)]
    table, late = {}, []
    for j, group in enumerate(chains["dense"] + [chains["o"]]):
        t0 = ticks.index((j * JOIN + JOIN - 1, 2)) if j < nf // JOIN else ticks.index((nf, 0))
        for k in range(max(c.nsteps for c in group)):
            todo = [(c, k) for c in group if k < c.nsteps]
            if t0 + STRIDE * k // 2 < len(ticks):
                table.setdefault(ticks[t0 + STRIDE * k // 2], []).extend(todo)
            else:
                late.extend(todo)

    def tick(step, pos):
        for at, todo in table.items():
            if at[1] != pos or step != ("f" if at[0] < nf else "b" if at[0] < nf + nb else "t"):
                continue
            if step == "t":
                for c, k in todo:
                    c.step(k)
                continue

            @pl.when(s == at[0])
            def _():
                for c, k in todo:
                    c.step(k)

    def put_owner(src_rows, value, e, order_of):
        for j in range(nexp):
            c = order_of[j]
            block, places = block_places(c.n, c.order, "exp")
            per = HEAD // block
            for b in range(per):
                at = c.base + places[e * per + b] * block
                src_rows[at:at + block, :] = value[j * HEAD + b * block:j * HEAD + (b + 1) * block, :]

    @pl.when(s == 0)
    def _():
        m = tok[...] + dot(cd[...], wo[...], TN)
        mid[...] = m
        cen = m - jnp.mean(m, axis=-1, keepdims=True)
        r = lax.rsqrt(jnp.mean(cen * cen, axis=-1, keepdims=True) + 1e-5)
        xh = cen * r
        rstd[...] = jnp.broadcast_to(r, rstd.shape)
        a = xh * g2[...] + s2[...]
        act[...] = a.astype(bf16)
        actT[...] = jnp.transpose(a).astype(bf16)
        dffn[...] = cot[...].astype(bf16)
        out[...] = m + downb[...]
        dx[...] = jnp.zeros_like(dx)
        greet(here)

    @pl.when(s < nf)
    def _():
        up, down = up_ref[...], down_ref[...]
        pre = dot(act[...], up) + upb[...]
        x2 = pre * pre
        th = jnp.tanh(pre * (C0 + C0 * C1 * x2))
        h = 0.5 * (1.0 + th)
        hid = (pre * h).astype(bf16)
        gp = h + (0.5 * pre) * (1.0 - th * th) * (C0 + 3.0 * C0 * C1 * x2)
        out[...] += dot(hid, down)
        tick("f", 0)
        r0 = pl.multiple_of(s * part, part)
        dsrc[pl.ds(r0, fb), :] = dot(hid, dffn[...], TN).astype(bf16)
        tick("f", 1)
        dpb = (dot(dffn[...], down, NT) * gp).astype(bf16)
        gub[pl.ds(s, 1), :] = jnp.sum(dpb.astype(f32), axis=0, keepdims=True)
        dsrc[pl.ds(pl.multiple_of(r0 + fb, fb), fb), :] = dot(actT[...], dpb).astype(bf16)
        dx[...] += dot(dpb, up, NT)
        tick("f", 2)

    @pl.when(s == nf - 1)
    def _():
        d = dx[...]
        m = mid[...]
        xh = (m - jnp.mean(m, axis=-1, keepdims=True)) * rstd[:, 0:1]
        gx = d * g2[...]
        dm = cot[...] + rstd[:, 0:1] * (gx - jnp.mean(gx, axis=-1, keepdims=True)
                                        - xh * jnp.mean(gx * xh, axis=-1, keepdims=True))
        mid[...] = dm
        gsm[...] = jnp.concatenate([jnp.sum(d * xh, axis=0, keepdims=True), jnp.sum(d, axis=0, keepdims=True),
                                    jnp.sum(dffn[...].astype(f32), axis=0, keepdims=True)], axis=0)
        dmb = dm.astype(bf16)
        act[...] = dmb
        dct[...] = dot(wo[...], dmb, NT).astype(bf16)
        w = nexp * HEAD
        for e in range(sizes["exp"]):
            put_owner(osrc, dot(cd[e * w:(e + 1) * w, :], dmb).astype(bf16), e, chains["o"])

    @pl.when(s == nf)
    def _():
        dkv[...] = jnp.zeros_like(dkv)
        rhs[...] = jnp.zeros_like(rhs)

    @pl.when((s >= nf) & (s < nf + nb))
    def _():
        i = s - nf
        lanes = pl.ds(pl.multiple_of(i * TB, TB), TB)
        q = q_ref[0]
        qaug[0:HEAD, :] = q
        rhs[0:HEAD, 0:W] = q
        hi, md, lo = split3(-lse_ref[0])
        qd = qdoc_ref[...]
        qaug[HEAD:HEAD + 16, :] = jnp.concatenate(
            [jnp.concatenate([qd[0:3, :]] * TOP, 1), hi, md, lo, jnp.zeros((10, W), f32)], 0).astype(bf16)
        qaug[HEAD + 16:, :] = jnp.zeros((128 - HEAD - 16, W), bf16)
        r = [jnp.broadcast_to(routes_ref[k:k + 1, :], (8, TB))[None] for k in range(TOP)]
        for k0 in range(0, TOP, 4):
            sel = [jnp.zeros((HEAD // 8, 8, TB), f32) for _ in range(4)]
            for e in range(experts):
                v = dct[e * HEAD:(e + 1) * HEAD, lanes].astype(f32).reshape(HEAD // 8, 8, TB)
                sel = [jnp.where(r[k0 + k] == e, v, sel[k]) for k in range(4)]
            for k in range(4):
                sl = slice((k0 + k) * TB, (k0 + k + 1) * TB)
                dc = (sel[k].reshape(HEAD, TB) * gates_ref[k0 + k:k0 + k + 1, :]).astype(bf16)
                daug[0:HEAD, sl] = dc
                rhs[HEAD:, W + (k0 + k) * TB:W + (k0 + k + 1) * TB] = dc
                dq[0:1, sl] = jnp.sum(dc.astype(f32) * ctx_ref[0, :, sl].astype(f32), axis=0, keepdims=True)
        hi, md, lo = split3(-dq[0:1, :])
        daug[HEAD:HEAD + 16, :] = jnp.concatenate([hi, md, lo, jnp.zeros((13, W), f32)], 0).astype(bf16)
        daug[HEAD + 16:, :] = jnp.zeros((128 - HEAD - 16, W), bf16)
        dq[...] = jnp.zeros_like(dq)
        q0 = lax.axis_index("ctx") * ntok + i * TB
        nfull = q0 // KBB
        kd = pl.multiple_of(nfull * KBB, KBB)

        def block(k0, mask):
            p = jnp.exp2(dot(kaug_ref[pl.ds(k0, KBB), :], qaug[...]))
            if mask is not None:
                p = jnp.concatenate([jnp.where(mask, p[:, k * TB:(k + 1) * TB], 0.0) for k in range(TOP)], 1)
            dp = dot(vaug_ref[pl.ds(k0, KBB), :], daug[...])
            pds[:, W:] = p.astype(bf16)
            pds[:, :W] = (p * dp).astype(bf16)
            dq[...] += dot(kt_ref[:, pl.ds(k0, KBB)], pds[:, :W])
            dkv[pl.ds(k0, KBB), :] += dot(pds[...], rhs[...], NT)

        def body(b, _):
            block(pl.multiple_of(b * KBB, KBB), None)
            return 0

        tick("b", 0)
        lax.fori_loop(0, nfull, body, 0)
        tick("b", 1)
        kp = lax.broadcasted_iota(jnp.int32, (KBB, TB), 0) + (kd - q0)
        tp = lax.broadcasted_iota(jnp.int32, (KBB, TB), 1)
        block(kd, kp <= tp)
        tick("b", 2)
        dq[...] *= 0.125
        for h0 in range(0, HEAD, 32):
            g = [dq[h0:h0 + 32, k * TB:(k + 1) * TB].reshape(4, 8, TB) for k in range(TOP)]
            for e in range(experts):
                o = jnp.zeros((4, 8, TB), f32)
                for k in range(TOP):
                    o = jnp.where(r[k] == e, g[k], o)
                dqd[e * HEAD + h0:e * HEAD + h0 + 32, lanes] = o.reshape(32, TB).astype(bf16)
        tick("b", 3)

    @pl.when(s == nf + nb)
    def _():
        lane = lax.broadcasted_iota(jnp.int32, (1, 128), 1)
        ksrc[...] = (dkv[...] * jnp.where(lane < HEAD, LN2, 1.0)).astype(bf16)
        kc, sc = chains["k"][0], chains["s"][0]
        kc.step(0)
        tick("t", 0)
        w = nexp * HEAD
        for e in range(sizes["exp"]):
            put_owner(qsrc, dot(dqd[e * w:(e + 1) * w, :], act1[...]).astype(bf16), e, chains["q"])
        for c in chains["q"]:
            c.step(0)
        tick("t", 1)
        for k in range(1, kc.nsteps):
            kc.step(k)
        da = dot(dqd[...], wq[...], TN) + dot(kfin[...], kvw[...], NT)
        for c in chains["q"]:
            c.step(1)
        tick("t", 2)
        x = tok[...]
        cen = x - jnp.mean(x, axis=-1, keepdims=True)
        r1 = lax.rsqrt(jnp.mean(cen * cen, axis=-1, keepdims=True) + 1e-5)
        xh = cen * r1
        gg1, gs1 = jnp.sum(da * xh, axis=0, keepdims=True), jnp.sum(da, axis=0, keepdims=True)
        gx = da * g1[...]
        dx[...] = mid[...] + r1 * (gx - jnp.mean(gx, axis=-1, keepdims=True)
                                   - xh * jnp.mean(gx * xh, axis=-1, keepdims=True))
        ssrc[0:D, :] = dot(act1[...], kfin[...], TN).astype(bf16)
        vecs = [gsm[0:1, :], gsm[1:2, :], gsm[2:3, :], gg1, gs1] + [gub[j:j + 1, :] for j in range(nf)]
        vecs = [v[:, o:o + 128] for v in vecs for o in range(0, v.shape[1], 128)]
        vecs.append(jnp.zeros((SMALL - D - len(vecs), 128), f32))
        ssrc[D:SMALL, :] = jnp.concatenate(vecs, 0).astype(bf16)
        tick("t", 3)
        tail = [[(c, k + 2) for c in chains["q"] if k + 2 < c.nsteps] + ([(sc, k)] if k < sc.nsteps else []) for k in range(20)]
        for k in range(20):
            for c, n in tail[k]:
                c.step(n)
            for c, n in late[k * len(late) // 6:(k + 1) * len(late) // 6]:
                c.step(n)
            if k == 6:
                moved = pltpu.make_async_copy(fin, fin_o, lsem.at[0])
                moved.start()
        qg = pltpu.make_async_copy(gq, gq_o, lsem.at[2])
        qg.start()
        og = pltpu.make_async_copy(go, go_o, lsem.at[1])
        og.start()
        sg = pltpu.make_async_copy(sfin, sm_o, lsem.at[3])
        sg.start()
        for c in (moved, og, qg, sg):
            c.wait()


def mega(sizes, nexp, cd, wo, tok, cot, g2, s2, up, upb, down, downb, q, ctx, lse, routes, gates, qdoc, kaug, vaug, kt,
         act1, wq, kvw, g1, fb=512):
    ntok, keys, ff, eh = tok.shape[0], kaug.shape[0], up.shape[1], wo.shape[0]
    nf, nb = ff // fb, ntok // TB
    part = 2 * fb
    sd = jax.ShapeDtypeStruct
    z = [None] * 10
    chains = make_chains(sizes, nf, part, nexp, keys, *z)
    wide, narrow = flat(chains)
    land, nland = sum(c.landed for c in wide), sum(c.landed for c in narrow)
    nsem = sum(c.nsem for c in wide + narrow)
    once = pl.Buffered(1)
    full = lambda a: pl.BlockSpec(a.shape, lambda s: (0,) * a.ndim, pipeline_mode=once)
    fo = lambda *sh: pl.BlockSpec(sh, lambda s: (0,) * len(sh), pipeline_mode=once)
    fj = lambda s: jnp.minimum(s, nf - 1)
    bi = lambda s: jnp.clip(s - nf, 0, nb - 1)
    blk = lambda r: pl.BlockSpec((r, TB), lambda s: (0, bi(s)))
    b3 = lambda a: pl.BlockSpec((1,) + a.shape[1:], lambda s: (bi(s), 0, 0))
    any_ = pl.BlockSpec(memory_space=pl.ANY)
    v = pltpu.VMEM
    return pl.pallas_call(
        functools.partial(mega_kernel, sizes, nf, nb, nexp, fb),
        grid=(nf + nb + 1,),
        in_specs=[full(cd), full(wo), full(tok), full(cot), full(g2), full(s2),
                  pl.BlockSpec((D, fb), lambda s: (0, fj(s))), pl.BlockSpec((1, fb), lambda s: (0, fj(s))),
                  pl.BlockSpec((fb, D), lambda s: (fj(s), 0)), full(downb), b3(q), b3(ctx), b3(lse),
                  blk(TOP), blk(TOP), blk(8), full(kaug), full(vaug), full(kt), full(act1), full(wq), full(kvw), full(g1)],
        out_specs=[fo(ntok, D), fo(ntok, D), any_, any_, any_, any_],
        out_shape=[sd((ntok, D), f32), sd((ntok, D), f32), sd((nf * part, D), bf16), sd((nexp * HEAD, D), bf16),
                   sd((nexp * HEAD, D), bf16), sd((SMALL, 128), bf16)],
        scratch_shapes=[
            v((ntok, D), f32), v((ntok, 128), f32), v((ntok, D), bf16), v((D, ntok), bf16),
            v((ntok, D), bf16), v((eh, ntok), bf16), v((eh, ntok), bf16), v((nf, fb), f32), v((3, D), f32),
            v((128, W), bf16), v((128, W), bf16), v((128, 2 * W), bf16), v((KBB, 2 * W), bf16), v((HEAD, W), f32),
            v((keys, 128), f32),
            v((nf * part, D), bf16), v((nf * part, D), bf16), v((eh, D), bf16), v((nexp * HEAD, D), bf16),
            v((eh, D), bf16), v((nexp * HEAD, D), bf16), v((keys, 128), bf16), v((ntok, 128), bf16),
            v((SMALL, 128), bf16), v((SMALL, 128), bf16), v((land, D), bf16), v((nland, 128), bf16),
            pltpu.SemaphoreType.DMA((nsem,)), pltpu.SemaphoreType.DMA((nsem,)), pltpu.SemaphoreType.DMA((4,))],
        compiler_params=pltpu.CompilerParams(collective_id=0, has_side_effects=True, vmem_limit_bytes=62 * 2**20),
        name="mega",
    )(cd, wo, tok, cot, g2, s2, up, upb, down, downb, q, ctx, lse, routes, gates, qdoc, kaug, vaug, kt, act1, wq, kvw, g1)


def local(sizes, tokens, lengths, routes, route_gates, cotangent, gain_one, shift_one, kv_weight,
          query_weight, out_weight, gain_two, shift_two, up_weight, up_bias, down_weight, down_bias):
    x = tokens[0]
    tok = x.shape[0]
    ncx = sizes["ctx"]
    group = tok * ncx
    nexp = query_weight.shape[0]
    experts = nexp * sizes["exp"]
    cidx = lax.axis_index("ctx")
    wq_own = jnp.swapaxes(query_weight, 1, 2).reshape(nexp * HEAD, D).astype(bf16)
    wo_own = out_weight.reshape(nexp * HEAD, D).astype(bf16)
    wq = lax.all_gather(wq_own, "exp", axis=0, tiled=True)
    wo = lax.all_gather(wo_own, "exp", axis=0, tiled=True)
    cen = x - jnp.mean(x, axis=-1, keepdims=True)
    rs1 = lax.rsqrt(jnp.mean(cen * cen, axis=-1, keepdims=True) + 1e-5)
    xh1 = cen * rs1
    act = (xh1 * gain_one + shift_one).astype(bf16)
    kvw = kv_weight.astype(bf16)
    kv_own = dot(act, kvw).astype(bf16)
    kv = lax.all_gather(kv_own, "ctx", axis=0, tiled=True)
    keys, vals = kv[:, :HEAD], kv[:, HEAD:]
    kn = jnp.max(jnp.sum(jnp.square(keys.astype(f32)), axis=1)).reshape(1)
    pos = jnp.arange(group, dtype=jnp.int32)
    docs, end = jnp.zeros_like(pos), 0
    for d in range(lengths.shape[1] - 1):
        end = end + lengths[0, d]
        docs = docs + (pos >= end).astype(jnp.int32)
    hot = (docs[:, None] == jnp.arange(3)[None, :]).astype(bf16)
    one3 = jnp.ones((group, 3), bf16)
    kaug = jnp.concatenate([keys, hot, one3, jnp.zeros((group, HEAD - 6), bf16)], axis=1)
    vaug = jnp.concatenate([vals, one3, jnp.zeros((group, HEAD - 3), bf16)], axis=1)
    kt = keys.T
    vt = jnp.concatenate([vals.T, jnp.ones((1, group), bf16), jnp.zeros((15, group), bf16)], axis=0)
    qdocs = lax.dynamic_slice_in_dim(docs, cidx * tok, tok)
    slot = jnp.arange(8, dtype=jnp.int32)[:, None]
    qdoc = jnp.where((qdocs[None, :] == slot) | (slot > 2), 0.0, NEG).astype(f32)
    routes_t = routes[0].T
    gates_t = route_gates[0].T
    cvec = cidx.reshape(1).astype(jnp.int32)

    cd, q, ctx, lse = attn_fwd(cvec, act, wq, routes_t, gates_t, qdoc, kaug, vt, kn, KB=384)
    row = lambda v: v.reshape(1, -1)
    out, dx, dense, go, gq, small = mega(
        sizes, nexp, cd, wo, x, cotangent[0], row(gain_two), row(shift_two), up_weight.astype(bf16),
        row(up_bias), down_weight.astype(bf16), row(down_bias), q, ctx, lse, routes_t, gates_t, qdoc, kaug, vaug, kt, act, wq, kvw, row(gain_one))
    go = go.astype(f32).reshape(nexp, HEAD, D)
    gq = jnp.swapaxes(gq.astype(f32).reshape(nexp, HEAD, D), 1, 2)
    dense = dense.reshape(-1, 2, D, D)
    gdown = dense[:, 0].astype(f32).reshape(-1, D)
    gup = dense[:, 1].astype(f32).transpose(1, 0, 2).reshape(D, -1)
    small = small.astype(f32)
    vec = small[D:].reshape(-1)
    v = lambda i: vec[i * D:(i + 1) * D]
    return (out[None], dx[None], v(3), v(4), small[:D], gq, go, v(0), v(1), gup, vec[5 * D:5 * D + up_bias.shape[0]],
            gdown, v(2))


def solution(mesh):
    tok3 = P(("dp", "exp"), "ctx", None)
    ex = P("exp", None, None)
    r = P()
    in_specs = (tok3, P(("dp", "exp"), None), tok3, tok3, tok3, r, r, r, ex, ex, r, r, r, r, r, r)
    out_specs = (tok3, tok3, r, r, r, ex, ex, r, r, r, r, r, r)
    fn = functools.partial(local, dict(mesh.shape))
    return jax.shard_map(fn, mesh=mesh, in_specs=in_specs, out_specs=out_specs, check_vma=False)
```

```python
import functools
import math

import jax
import jax.numpy as jnp
from jax import lax
from jax.experimental import pallas as pl
from jax.experimental.pallas import tpu as pltpu
from jax.sharding import PartitionSpec as P

f32 = jnp.float32
bf16 = jnp.bfloat16
D = 512
HEAD = 64
TOP = 8
TB = 128
W = TOP * TB
NEG = -1e30
LOG2E = math.log2(math.e)
LN2 = math.log(2.0)
SMALL = 576
KBB = 384
STRIDE = 8
JOIN = 2
SAFE = 50.0
NN = (((1,), (0,)), ((), ()))
NT = (((1,), (1,)), ((), ()))
TN = (((0,), (0,)), ((), ()))
C0 = math.sqrt(2 / math.pi)
C1 = 0.044715
MESH = pl.DeviceIdType.MESH
AXES = ("dp", "ctx", "exp")


def attn_fwd_kernel(act_ref, wq_ref, routes_ref, gates_ref, qdoc_ref, kaug_ref, vt_ref,
                    cd_ref, q_ref, ctx_ref, lse_ref,
                    qt, qaug, s, acc, kn_ref, *, experts, tok, KB):
    i=pl.program_id(0)
    c=lax.axis_index("ctx")
    @pl.when(i==0)
    def _():
        kk=kaug_ref[...].astype(f32)
        kk=jnp.where(lax.broadcasted_iota(jnp.int32,kk.shape,1)<HEAD,kk*kk,0.0)
        kn_ref[0]=jnp.max(jnp.sum(kk,axis=1,keepdims=True))
    qt[...]=lax.dot_general(wq_ref[...], act_ref[...], NT, preferred_element_type=f32)*(0.125*LOG2E)
    n2=[]
    for k0 in range(0,TOP,4):
        r=[jnp.broadcast_to(routes_ref[k0+k:k0+k+1,:],(8,TB))[None] for k in range(4)]
        sel=[jnp.zeros((HEAD//8,8,TB),f32) for _ in range(4)]
        for e in range(experts):
            v=qt[e*HEAD:(e+1)*HEAD,:].reshape(HEAD//8,8,TB)
            sel=[jnp.where(r[k]==e,v,sel[k]) for k in range(4)]
        for k in range(4):
            sk=sel[k].reshape(HEAD,TB)
            n2.append(jnp.max(jnp.sum(sk*sk,axis=0,keepdims=True)))
            qaug[0:HEAD,(k0+k)*TB:(k0+k+1)*TB]=sk.astype(bf16)
    n2=functools.reduce(jnp.maximum,n2)*kn_ref[0]
    fast=n2<=SAFE*SAFE
    q_ref[0]=qaug[0:HEAD,:]
    qd=qdoc_ref[...]
    qaug[HEAD:HEAD+16,:]=jnp.concatenate([jnp.concatenate([qd,jnp.zeros_like(qd)],0)]*TOP,1).astype(bf16)
    qaug[HEAD+16:,:]=jnp.zeros((128-HEAD-16,W),bf16)
    q0=c*tok+i*TB
    nfull=q0//KB
    kd=pl.multiple_of(nfull*KB,KB)
    kp=lax.broadcasted_iota(jnp.int32,(KB,TB),0)+(kd-q0)
    tp=lax.broadcasted_iota(jnp.int32,(KB,TB),1)
    mask=kp<=tp
    acc[...]=jnp.zeros_like(acc)
    def scores(k0,n):
        return jnp.dot(kaug_ref[pl.ds(k0,n),:],qaug[...],preferred_element_type=f32)
    def masked(x):
        return jnp.concatenate([jnp.where(mask,x[:,k*TB:(k+1)*TB],NEG) for k in range(TOP)],1)
    def pv(k0,n,p):
        acc[...]+=jnp.dot(vt_ref[:,pl.ds(k0,n)],p,preferred_element_type=f32)
    def finish(m):
        l=acc[HEAD:HEAD+1,:]
        lse_ref[0]=m+jnp.log2(l)
        acc[0:HEAD,:]=acc[0:HEAD,:]*(1.0/l)
    @pl.when(fast)
    def _():
        def body(b,_):
            k0=pl.multiple_of(b*KB,KB)
            pv(k0,KB,jnp.exp2(scores(k0,KB)).astype(bf16))
            return 0
        lax.fori_loop(0,nfull,body,0)
        pv(kd,KB,jnp.exp2(masked(scores(kd,KB))).astype(bf16))
        finish(0.0)
    @pl.when(jnp.logical_not(fast))
    def _():
        def spass(b,m):
            k0=pl.multiple_of(b*KB,KB)
            x=scores(k0,KB)
            s[pl.ds(k0,KB),:]=x
            return jnp.maximum(m,jnp.max(x.reshape(KB//8,8,W),axis=0))
        m=lax.fori_loop(0,nfull,spass,jnp.full((8,W),NEG*2,f32))
        x=masked(scores(kd,KB))
        s[pl.ds(kd,KB),:]=x
        m=jnp.maximum(m,jnp.max(x.reshape(KB//8,8,W),axis=0))
        m=jnp.max(m,axis=0,keepdims=True)
        def ppass(b,_):
            k0=pl.multiple_of(b*KB,KB)
            pv(k0,KB,jnp.exp2(s[pl.ds(k0,KB),:]-m).astype(bf16))
            return 0
        lax.fori_loop(0,nfull+1,ppass,0)
        finish(m)
    ctx_ref[0]=acc[0:HEAD,:].astype(bf16)
    for k in range(TOP):
        acc[0:HEAD,k*TB:(k+1)*TB]*=gates_ref[k:k+1,:]
    r=[jnp.broadcast_to(routes_ref[k:k+1,:],(8,TB))[None] for k in range(TOP)]
    for h0 in range(0,HEAD,32):
        g=[acc[h0:h0+32,k*TB:(k+1)*TB].reshape(4,8,TB) for k in range(TOP)]
        for e in range(experts):
            o=jnp.zeros((4,8,TB),f32)
            for k in range(TOP):
                o=jnp.where(r[k]==e,g[k],o)
            cd_ref[e*HEAD+h0:e*HEAD+h0+32,:]=o.reshape(32,TB).astype(bf16)

def attn_fwd(act, wq, routesT, gatesT, qdoc, kaug, vt, KB=256):
    tok=act.shape[0]; experts=wq.shape[0]//HEAD; keys=kaug.shape[0]; n=tok//TB; vr=vt.shape[0]
    full=lambda a: pl.BlockSpec(a.shape,lambda i,*_:(0,)*a.ndim)
    return pl.pallas_call(
        functools.partial(attn_fwd_kernel,experts=experts,tok=tok,KB=KB),
        grid_spec=pltpu.PrefetchScalarGridSpec(num_scalar_prefetch=0,grid=(n,),
          in_specs=[pl.BlockSpec((TB,D),lambda i,*_:(i,0)),full(wq),
            pl.BlockSpec((TOP,TB),lambda i,*_:(0,i)),pl.BlockSpec((TOP,TB),lambda i,*_:(0,i)),
            pl.BlockSpec((8,TB),lambda i,*_:(0,i)),full(kaug),full(vt)],
          out_specs=[pl.BlockSpec((experts*HEAD,TB),lambda i,*_:(0,i)),
            pl.BlockSpec((1,HEAD,W),lambda i,*_:(i,0,0)),
            pl.BlockSpec((1,HEAD,W),lambda i,*_:(i,0,0)),
            pl.BlockSpec((1,1,W),lambda i,*_:(i,0,0))],
          scratch_shapes=[pltpu.VMEM((experts*HEAD,TB),f32),pltpu.VMEM((128,W),bf16),
            pltpu.VMEM((keys,W),f32),pltpu.VMEM((vr,W),f32),pltpu.SMEM((1,),f32)]),
        out_shape=[jax.ShapeDtypeStruct((experts*HEAD,tok),bf16),
          jax.ShapeDtypeStruct((n,HEAD,W),bf16),jax.ShapeDtypeStruct((n,HEAD,W),bf16),
          jax.ShapeDtypeStruct((n,1,W),f32)],
        compiler_params=pltpu.CompilerParams(vmem_limit_bytes=60*2**20),
        name="attn_fwd",
    )(act,wq,routesT,gatesT,qdoc,kaug,vt)


def dot(a, b, dims=NN):
    return lax.dot_general(a, b, dims, preferred_element_type=f32)


def split3(x):
    hi = x.astype(bf16).astype(f32)
    r = x - hi
    mid = r.astype(bf16).astype(f32)
    return hi, mid, r - mid


class Here:
    def __init__(self, sizes):
        at = {a: lax.axis_index(a) for a in AXES}
        self.bit, self.dev = {}, {}
        for bits in mesh_bits(sizes).values():
            for ax, m in bits:
                b = lax.rem(at[ax] // m, 2)
                self.bit[ax, m] = b
                self.dev[ax, m] = tuple(at[a] + m - 2 * m * b if a == ax else at[a] for a in AXES)


def mesh_bits(sizes):
    return {a: [(a, 1 << i) for i in range(sizes[a].bit_length() - 1)] for a in AXES}


def chain_orders(sizes):
    b = mesh_bits(sizes)
    e, d, c = b["exp"], b["dp"], b["ctx"]
    late = e + d + c
    if len(d) + len(c) > 2:
        return [late, late, late]
    return [e[:1] + d + c + e[1:], e[:1] + c + d + e[1:], late]


def chain_plan(n, order):
    plan = []
    for bit in order:
        halve = n % 32 == 0
        n = n // 2 if halve else n
        plan.append((halve, bit, n))
    return plan


def rows(ref, start, n):
    return ref.at[pl.ds(pl.multiple_of(start, 16), n), :]


def add_rows(dst, d0, a, a0, b, b0, n):
    ch = math.gcd(n, 64)

    @pl.loop(0, n // ch)
    def _(t):
        o = pl.multiple_of(t * ch, ch)
        g = lambda r, s: r[pl.ds(pl.multiple_of(s + o, 16), ch), :]
        dst[pl.ds(pl.multiple_of(d0 + o, 16), ch), :] = g(a, a0) + g(b, b0)


def block_places(n, order, owner):
    bits = [bit for halve, bit, _ in chain_plan(n, order) if halve]
    own = sorted([b for b in bits if b[0] == owner], reverse=True)
    nat = own + sorted([b for b in bits if b[0] != owner])
    places = []
    for i in range(1 << len(nat)):
        v = {b: (i >> (len(nat) - 1 - k)) & 1 for k, b in enumerate(nat)}
        places.append(sum(v[b] << (len(bits) - 1 - k) for k, b in enumerate(bits)))
    return n >> len(nat), places


class Chain:
    def __init__(self, work, final, base, n, order, owner=None, fbase=0):
        self.work, self.final, self.base, self.n, self.order = work, final, base, n, order
        self.owner, self.fbase = owner, fbase
        self.plan = chain_plan(n, order)
        self.landed = sum(m for _, _, m in self.plan)
        self.back = [i for i in reversed(range(len(order))) if self.plan[i][0] and order[i][0] != owner]
        if owner:
            self.back.sort(key=lambda i: order[i], reverse=True)
        self.m = len(self.plan)
        self.nsem = self.m + len(self.back)
        self.nsteps = self.nsem + 1

    def place(self, here, land, lbase, ss, rs, sem):
        self.here, self.land, self.ss, self.rs, self.sem = here, land, ss, rs, sem
        self.lb = []
        for _, _, m in self.plan:
            self.lb.append(lbase)
            lbase += m
        self.offs = self.offsets()

    def offsets(self):
        offs, off = [], self.base
        for halve, bit, m in self.plan:
            b = self.here.bit[bit]
            offs.append((off + b * m, off + (1 - b) * m) if halve else (off, off))
            off = offs[-1][0]
        return offs

    def final_range(self, j):
        m = self.plan[-1][2]
        if self.owner is None:
            offs = self.offs
            if j == 0:
                return offs[-1][0], m
            i = self.back[j]
            return offs[i][0], self.plan[i][2]
        off, w = self.fbase, m
        for k, i in enumerate(self.back):
            if k >= j:
                off = off + self.here.bit[self.order[i]] * w
            w *= 2
        return off, m << j

    def copy(self, k):
        if k < self.m:
            _, bit, n = self.plan[k]
            src, dst = rows(self.work, self.offs[k][1], n), rows(self.land, self.lb[k], n)
        else:
            bit = self.order[self.back[k - self.m]]
            src = dst = rows(self.final, *self.final_range(k - self.m))
        return pltpu.make_async_remote_copy(
            src_ref=src, dst_ref=dst, send_sem=self.ss.at[self.sem + k], recv_sem=self.rs.at[self.sem + k],
            device_id=self.here.dev[bit], device_id_type=MESH)

    def step(self, k):
        if k:
            self.copy(k - 1).wait()
            if k <= self.m:
                i = k - 1
                last = i == self.m - 1
                d = self.offs[i][0]
                add_rows(self.final if last else self.work, self.final_range(0)[0] if last else d,
                         self.work, d, self.land, self.lb[i], self.plan[i][2])
        if k < self.nsem:
            self.copy(k).start()


def greet(here):
    bar = pltpu.get_barrier_semaphore()
    for dev in here.dev.values():
        pl.semaphore_signal(bar, inc=1, device_id=dev, device_id_type=MESH)
    pl.semaphore_wait(bar, len(here.dev))


def dense_parts(n, orders):
    a = n * 3 // 8 // 32 * 32
    return [(0, a, orders[0]), (a, a, orders[1]), (2 * a, n - 2 * a, orders[2])]


def make_chains(sizes, steps, part, nexp, keys, dsrc, fin, osrc, go, qsrc, gq, ksrc, kfin, ssrc, sfin):
    orders = chain_orders(sizes)
    n = sizes["exp"] * HEAD
    kbits = mesh_bits(sizes)["ctx"][::-1]
    part = part * JOIN
    dense = [[Chain(dsrc, fin, j * part + b, m, o) for b, m, o in dense_parts(part, orders)] for j in range(steps // JOIN)]
    return dict(
        dense=dense,
        o=[Chain(osrc, go, j * n, n, orders[j % 3], "exp", j * HEAD) for j in range(nexp)],
        q=[Chain(qsrc, gq, j * n, n, orders[j % 3], "exp", j * HEAD) for j in range(nexp)],
        k=[Chain(ksrc, kfin, 0, keys, kbits, "ctx", 0)],
        s=[Chain(ssrc, sfin, 0, SMALL, orders[0])],
    )


def flat(chains):
    wide = [c for g in chains["dense"] for c in g] + chains["o"] + chains["q"]
    return wide, chains["k"] + chains["s"]


def place_all(here, chains, land, nland, ss, rs):
    sem = 0
    for group, buf in zip(flat(chains), (land, nland)):
        lb = 0
        for c in group:
            c.place(here, buf, lb, ss, rs, sem)
            lb += c.landed
            sem += c.nsem


def mega_kernel(sizes, nf, nb, nexp, fb,
                cd, wo, tok, cot, g2, s2, up_ref, upb, down_ref, downb, q_ref, ctx_ref, lse_ref, routes_ref, gates_ref,
                qdoc_ref, kaug_ref, vaug_ref, kt_ref, act1, wq, kvw, g1,
                out, dx, go_o, gq_o, gkv_o, sm_o, gd_o, gu_o,
                mid, rstd, act, actT, dffn, dct, dqd, gub, gsm,
                qaug, daug, rhs, pds, dq, dkv,
                dsrc, fin, osrc, go, qsrc, gq, ksrc, kfin, ssrc, sfin, land, nland, ss, rs, lsem):
    s = pl.program_id(0)
    experts = cd.shape[0] // HEAD
    ntok, keys = tok.shape[0], kaug_ref.shape[0]
    part = 2 * fb
    chains = make_chains(sizes, nf, part, nexp, keys, dsrc, fin, osrc, go, qsrc, gq, ksrc, kfin, ssrc, sfin)
    here = Here(sizes)
    place_all(here, chains, land, nland, ss, rs)
    ticks = [(j, p) for j in range(nf) for p in range(3)] + [(nf + i, p) for i in range(nb) for p in range(4)]
    ticks += [(nf + nb, p) for p in range(4)]
    table, late = {}, []
    for j, group in enumerate(chains["dense"] + [chains["o"]]):
        t0 = ticks.index((j * JOIN + JOIN - 1, 2)) if j < nf // JOIN else ticks.index((nf, 0))
        for k in range(max(c.nsteps for c in group)):
            todo = [(c, k) for c in group if k < c.nsteps]
            if t0 + STRIDE * k // 2 < len(ticks):
                table.setdefault(ticks[t0 + STRIDE * k // 2], []).extend(todo)
            else:
                late.extend(todo)

    def tick(step, pos):
        for at, todo in table.items():
            if at[1] != pos or step != ("f" if at[0] < nf else "b" if at[0] < nf + nb else "t"):
                continue
            if step == "t":
                for c, k in todo:
                    c.step(k)
                continue

            @pl.when(s == at[0])
            def _():
                for c, k in todo:
                    c.step(k)

    def put_owner(src_rows, value, e, order_of):
        for j in range(nexp):
            c = order_of[j]
            block, places = block_places(c.n, c.order, "exp")
            per = HEAD // block
            for b in range(per):
                at = c.base + places[e * per + b] * block
                src_rows[at:at + block, :] = value[j * HEAD + b * block:j * HEAD + (b + 1) * block, :]

    @pl.when(s == 0)
    def _():
        m = tok[...] + dot(cd[...], wo[...], TN)
        mid[...] = m
        cen = m - jnp.mean(m, axis=-1, keepdims=True)
        r = lax.rsqrt(jnp.mean(cen * cen, axis=-1, keepdims=True) + 1e-5)
        xh = cen * r
        rstd[...] = jnp.broadcast_to(r, rstd.shape)
        a = xh * g2[...] + s2[...]
        act[...] = a.astype(bf16)
        actT[...] = jnp.transpose(a).astype(bf16)
        dffn[...] = cot[...].astype(bf16)
        out[...] = m + downb[...]
        dx[...] = jnp.zeros_like(dx)
        greet(here)

    @pl.when(s < nf)
    def _():
        up, down = up_ref[...], down_ref[...]
        pre = dot(act[...], up) + upb[...]
        x2 = pre * pre
        th = jnp.tanh(pre * (C0 + C0 * C1 * x2))
        h = 0.5 * (1.0 + th)
        hid = (pre * h).astype(bf16)
        gp = h + (0.5 * pre) * (1.0 - th * th) * (C0 + 3.0 * C0 * C1 * x2)
        out[...] += dot(hid, down)
        tick("f", 0)
        r0 = pl.multiple_of(s * part, part)
        dsrc[pl.ds(r0, fb), :] = dot(hid, dffn[...], TN).astype(bf16)
        tick("f", 1)
        dpb = (dot(dffn[...], down, NT) * gp).astype(bf16)
        gub[pl.ds(s, 1), :] = jnp.sum(dpb.astype(f32), axis=0, keepdims=True)
        dsrc[pl.ds(pl.multiple_of(r0 + fb, fb), fb), :] = dot(actT[...], dpb).astype(bf16)
        dx[...] += dot(dpb, up, NT)
        tick("f", 2)

    @pl.when(s == nf - 1)
    def _():
        d = dx[...]
        m = mid[...]
        xh = (m - jnp.mean(m, axis=-1, keepdims=True)) * rstd[:, 0:1]
        gx = d * g2[...]
        dm = cot[...] + rstd[:, 0:1] * (gx - jnp.mean(gx, axis=-1, keepdims=True)
                                        - xh * jnp.mean(gx * xh, axis=-1, keepdims=True))
        mid[...] = dm
        gsm[...] = jnp.concatenate([jnp.sum(d * xh, axis=0, keepdims=True), jnp.sum(d, axis=0, keepdims=True),
                                    jnp.sum(dffn[...].astype(f32), axis=0, keepdims=True)], axis=0)
        dmb = dm.astype(bf16)
        act[...] = dmb
        dct[...] = dot(wo[...], dmb, NT).astype(bf16)
        w = nexp * HEAD
        for e in range(sizes["exp"]):
            put_owner(osrc, dot(cd[e * w:(e + 1) * w, :], dmb).astype(bf16), e, chains["o"])

    @pl.when(s == nf)
    def _():
        dkv[...] = jnp.zeros_like(dkv)
        rhs[...] = jnp.zeros_like(rhs)

    @pl.when((s >= nf) & (s < nf + nb))
    def _():
        i = s - nf
        lanes = pl.ds(pl.multiple_of(i * TB, TB), TB)
        q = q_ref[0]
        qaug[0:HEAD, :] = q
        rhs[0:HEAD, 0:W] = q
        hi, md, lo = split3(-lse_ref[0])
        qd = qdoc_ref[...]
        qaug[HEAD:HEAD + 16, :] = jnp.concatenate(
            [jnp.concatenate([qd[0:3, :]] * TOP, 1), hi, md, lo, jnp.zeros((10, W), f32)], 0).astype(bf16)
        qaug[HEAD + 16:, :] = jnp.zeros((128 - HEAD - 16, W), bf16)
        r = [jnp.broadcast_to(routes_ref[k:k + 1, :], (8, TB))[None] for k in range(TOP)]
        for k0 in range(0, TOP, 4):
            sel = [jnp.zeros((HEAD // 8, 8, TB), f32) for _ in range(4)]
            for e in range(experts):
                v = dct[e * HEAD:(e + 1) * HEAD, lanes].astype(f32).reshape(HEAD // 8, 8, TB)
                sel = [jnp.where(r[k0 + k] == e, v, sel[k]) for k in range(4)]
            for k in range(4):
                sl = slice((k0 + k) * TB, (k0 + k + 1) * TB)
                dc = (sel[k].reshape(HEAD, TB) * gates_ref[k0 + k:k0 + k + 1, :]).astype(bf16)
                daug[0:HEAD, sl] = dc
                rhs[HEAD:, W + (k0 + k) * TB:W + (k0 + k + 1) * TB] = dc
                dq[0:1, sl] = jnp.sum(dc.astype(f32) * ctx_ref[0, :, sl].astype(f32), axis=0, keepdims=True)
        hi, md, lo = split3(-dq[0:1, :])
        daug[HEAD:HEAD + 16, :] = jnp.concatenate([hi, md, lo, jnp.zeros((13, W), f32)], 0).astype(bf16)
        daug[HEAD + 16:, :] = jnp.zeros((128 - HEAD - 16, W), bf16)
        dq[...] = jnp.zeros_like(dq)
        q0 = lax.axis_index("ctx") * ntok + i * TB
        nfull = q0 // KBB
        kd = pl.multiple_of(nfull * KBB, KBB)

        def block(k0, mask):
            p = jnp.exp2(dot(kaug_ref[pl.ds(k0, KBB), :], qaug[...]))
            if mask is not None:
                p = jnp.concatenate([jnp.where(mask, p[:, k * TB:(k + 1) * TB], 0.0) for k in range(TOP)], 1)
            dp = dot(vaug_ref[pl.ds(k0, KBB), :], daug[...])
            pds[:, W:] = p.astype(bf16)
            pds[:, :W] = (p * dp).astype(bf16)
            dq[...] += dot(kt_ref[:, pl.ds(k0, KBB)], pds[:, :W])
            dkv[pl.ds(k0, KBB), :] += dot(pds[...], rhs[...], NT)

        def body(b, _):
            block(pl.multiple_of(b * KBB, KBB), None)
            return 0

        tick("b", 0)
        lax.fori_loop(0, nfull, body, 0)
        tick("b", 1)
        kp = lax.broadcasted_iota(jnp.int32, (KBB, TB), 0) + (kd - q0)
        tp = lax.broadcasted_iota(jnp.int32, (KBB, TB), 1)
        block(kd, kp <= tp)
        tick("b", 2)
        dq[...] *= 0.125
        for h0 in range(0, HEAD, 32):
            g = [dq[h0:h0 + 32, k * TB:(k + 1) * TB].reshape(4, 8, TB) for k in range(TOP)]
            for e in range(experts):
                o = jnp.zeros((4, 8, TB), f32)
                for k in range(TOP):
                    o = jnp.where(r[k] == e, g[k], o)
                dqd[e * HEAD + h0:e * HEAD + h0 + 32, lanes] = o.reshape(32, TB).astype(bf16)
        tick("b", 3)

    @pl.when(s == nf + nb)
    def _():
        lane = lax.broadcasted_iota(jnp.int32, (1, 128), 1)
        ksrc[...] = (dkv[...] * jnp.where(lane < HEAD, LN2, 1.0)).astype(bf16)
        kc, sc = chains["k"][0], chains["s"][0]
        kc.step(0)
        tick("t", 0)
        w = nexp * HEAD
        for e in range(sizes["exp"]):
            put_owner(qsrc, dot(dqd[e * w:(e + 1) * w, :], act1[...]).astype(bf16), e, chains["q"])
        for c in chains["q"]:
            c.step(0)
        tick("t", 1)
        dx[...] = dot(dqd[...], wq[...], TN)
        for c in chains["q"]:
            c.step(1)
        tick("t", 2)
        for k in range(1, kc.nsteps):
            kc.step(k)
        da = dx[...] + dot(kfin[...], kvw[...].astype(bf16), NT)
        x = tok[...]
        cen = x - jnp.mean(x, axis=-1, keepdims=True)
        r1 = lax.rsqrt(jnp.mean(cen * cen, axis=-1, keepdims=True) + 1e-5)
        xh = cen * r1
        gg1, gs1 = jnp.sum(da * xh, axis=0, keepdims=True), jnp.sum(da, axis=0, keepdims=True)
        gx = da * g1[...]
        dx[...] = mid[...] + r1 * (gx - jnp.mean(gx, axis=-1, keepdims=True)
                                   - xh * jnp.mean(gx * xh, axis=-1, keepdims=True))
        ssrc[0:D, :] = dot(act1[...], kfin[...], TN).astype(bf16)
        vecs = [gsm[0:1, :], gsm[1:2, :], gsm[2:3, :], gg1, gs1] + [gub[j:j + 1, :] for j in range(nf)]
        vecs = [v[:, o:o + 128] for v in vecs for o in range(0, v.shape[1], 128)]
        vecs.append(jnp.zeros((SMALL - D - len(vecs), 128), f32))
        ssrc[D:SMALL, :] = jnp.concatenate(vecs, 0).astype(bf16)
        tick("t", 3)
        tail = [[(c, k + 2) for c in chains["q"] if k + 2 < c.nsteps] + ([(sc, k)] if k < sc.nsteps else []) for k in range(20)]
        for k in range(20):
            for c, n in tail[k]:
                c.step(n)
            for c, n in late[k * len(late) // 6:(k + 1) * len(late) // 6]:
                c.step(n)
            if k == 6:
                moved = []
                for j in range(nf):
                    r0 = j * part
                    moved.append(pltpu.make_async_copy(
                        fin.at[r0:r0 + fb, :], gd_o.at[j * fb:(j + 1) * fb, :], lsem.at[2 * j]))
                    moved.append(pltpu.make_async_copy(
                        fin.at[r0 + fb:r0 + part, :], gu_o.at[:, j * fb:(j + 1) * fb], lsem.at[2 * j + 1]))
                for c in moved:
                    c.start()
        go_o[...] = go[...].astype(f32)
        gq_o[...] = gq[...].astype(f32)
        gkv_o[...] = sfin[0:D, :].astype(f32)
        sm_o[...] = sfin[D:SMALL, :].astype(f32)
        for c in moved:
            c.wait()


def mega(sizes, nexp, cd, wo, tok, cot, g2, s2, up, upb, down, downb, q, ctx, lse, routes, gates, qdoc, kaug, vaug, kt,
         act1, wq, kvw, g1, fb=512):
    ntok, keys, ff, eh = tok.shape[0], kaug.shape[0], up.shape[1], wo.shape[0]
    nf, nb = ff // fb, ntok // TB
    part = 2 * fb
    sd = jax.ShapeDtypeStruct
    z = [None] * 10
    chains = make_chains(sizes, nf, part, nexp, keys, *z)
    wide, narrow = flat(chains)
    land, nland = sum(c.landed for c in wide), sum(c.landed for c in narrow)
    nsem = sum(c.nsem for c in wide + narrow)
    once = pl.Buffered(1)
    full = lambda a: pl.BlockSpec(a.shape, lambda s: (0,) * a.ndim, pipeline_mode=once)
    fo = lambda *sh: pl.BlockSpec(sh, lambda s: (0,) * len(sh), pipeline_mode=once)
    fj = lambda s: jnp.minimum(s, nf - 1)
    bi = lambda s: jnp.clip(s - nf, 0, nb - 1)
    blk = lambda r: pl.BlockSpec((r, TB), lambda s: (0, bi(s)))
    b3 = lambda a: pl.BlockSpec((1,) + a.shape[1:], lambda s: (bi(s), 0, 0))
    any_ = pl.BlockSpec(memory_space=pl.ANY)
    v = pltpu.VMEM
    return pl.pallas_call(
        functools.partial(mega_kernel, sizes, nf, nb, nexp, fb),
        grid=(nf + nb + 1,),
        in_specs=[full(cd), full(wo), full(tok), full(cot), full(g2), full(s2),
                  pl.BlockSpec((D, fb), lambda s: (0, fj(s))), pl.BlockSpec((1, fb), lambda s: (0, fj(s))),
                  pl.BlockSpec((fb, D), lambda s: (fj(s), 0)), full(downb), b3(q), b3(ctx), b3(lse),
                  blk(TOP), blk(TOP), blk(8), full(kaug), full(vaug), full(kt), full(act1), full(wq), full(kvw), full(g1)],
        out_specs=[fo(ntok, D), fo(ntok, D), fo(nexp * HEAD, D), fo(nexp * HEAD, D), fo(D, 128), fo(SMALL - D, 128), any_, any_],
        out_shape=[sd((ntok, D), f32), sd((ntok, D), f32), sd((nexp * HEAD, D), f32), sd((nexp * HEAD, D), f32),
                   sd((D, 128), f32), sd((SMALL - D, 128), f32), sd((ff, D), bf16), sd((D, ff), bf16)],
        scratch_shapes=[
            v((ntok, D), f32), v((ntok, 128), f32), v((ntok, D), bf16), v((D, ntok), bf16),
            v((ntok, D), bf16), v((eh, ntok), bf16), v((eh, ntok), bf16), v((nf, fb), f32), v((3, D), f32),
            v((128, W), bf16), v((128, W), bf16), v((128, 2 * W), bf16), v((KBB, 2 * W), bf16), v((HEAD, W), f32),
            v((keys, 128), f32),
            v((nf * part, D), bf16), v((nf * part, D), bf16), v((eh, D), bf16), v((nexp * HEAD, D), bf16),
            v((eh, D), bf16), v((nexp * HEAD, D), bf16), v((keys, 128), bf16), v((ntok, 128), bf16),
            v((SMALL, 128), bf16), v((SMALL, 128), bf16), v((land, D), bf16), v((nland, 128), bf16),
            pltpu.SemaphoreType.DMA((nsem,)), pltpu.SemaphoreType.DMA((nsem,)), pltpu.SemaphoreType.DMA((2 * nf,))],
        compiler_params=pltpu.CompilerParams(collective_id=0, has_side_effects=True, vmem_limit_bytes=62 * 2**20),
        name="mega",
    )(cd, wo, tok, cot, g2, s2, up, upb, down, downb, q, ctx, lse, routes, gates, qdoc, kaug, vaug, kt, act1, wq, kvw, g1)


def gather_stages(sizes, here, shard):
    e = lax.axis_index("exp")
    if (sizes["dp"], sizes["ctx"], sizes["exp"]) != (2, 2, 8) or shard % 64:
        stages = []
        for i, bit in enumerate(mesh_bits(sizes)["exp"]):
            stages.append([((e >> i << i) * shard, shard << i, bit)])
        return stages, []
    core, zl, zh, x, y = ("exp", 1), ("exp", 2), ("exp", 4), ("dp", 1), ("ctx", 1)
    quarter = shard // 4
    flip = lambda bit, n=1: n * (1 - 2 * here.bit[bit])
    at = lambda dz: e + (dz & 1) * flip(zl, 2) + (dz >> 1) * flip(zh, 4)
    q = here.bit[x] * 2 + here.bit[y]
    row = lambda dz, dq: at(dz) * shard + (q + (dq & 1) * flip(y) + (dq >> 1) * flip(x, 2)) * quarter
    gx = lambda dq: [(row(1, dq), quarter), (row(3, dq), 16)]
    gy = lambda dq: [(row(2, dq), quarter), (row(3, dq) + 16, quarter - 16)]
    stages = [
        [(row(0, 0), quarter, zh)],
        [(row(0, 0), quarter, zl), (row(2, 0), quarter, zl)],
        [m + (x,) for m in gx(0)] + [m + (y,) for m in gy(0)],
        [m + (y,) for m in gx(0) + gx(2)] + [m + (x,) for m in gy(0) + gy(1)],
        [(at(d) * shard, shard, core) for d in (1, 2, 3)],
    ]
    return stages, [(e * shard, shard, core)]


def head_kernel(sizes, nexp, nsem, tok, g1, s1, kvw, wq3, wo3, lens, up_h, down_h,
                act, kaug, vaug, kt, vt, qdoc, wq_o, wo_o, up_o, down_o,
                wqs, wos, kv, upf, downf, upb, downb, ss, rs, ls):
    here = Here(sizes)
    ntok, keys, shard = tok.shape[0], kv.shape[0], nexp * HEAD
    fetch = [pltpu.make_async_copy(up_h, upf, ls.at[0]), pltpu.make_async_copy(down_h, downf, ls.at[1])]
    for c in fetch:
        c.start()
    mine = lax.axis_index("exp") * shard
    for j in range(nexp):
        r = pl.ds(pl.multiple_of(mine + j * HEAD, HEAD), HEAD)
        wqs[r, :] = wq3[j].astype(bf16)
        wos[r, :] = wo3[j].astype(bf16)
    greet(here)
    count = [0]

    def send(buf, moves):
        out = []
        for start, n, bit in moves:
            r = rows(buf, start, n)
            k = count[0]
            count[0] += 1
            c = pltpu.make_async_remote_copy(src_ref=r, dst_ref=r, send_sem=ss.at[k], recv_sem=rs.at[k],
                                             device_id=here.dev[bit], device_id_type=MESH)
            c.start()
            out.append(c)
        return out

    def wait(copies):
        for c in copies:
            c.wait()

    stages, early = gather_stages(sizes, here, shard)
    work = []

    def run(k):
        for buf, lag in ((wqs, 0), (wos, 0)):
            i = k - lag
            if 0 < i <= len(stages):
                wait(flying[buf is wos])
            if 0 <= i < len(stages):
                flying[buf is wos] = send(buf, stages[i])

    flying = [[], []]
    run(0)
    own = send(wqs, early) + send(wos, early)
    x = tok[...]
    cen = x - jnp.mean(x, axis=-1, keepdims=True)
    a = (cen * lax.rsqrt(jnp.mean(cen * cen, axis=-1, keepdims=True) + 1e-5) * g1[...] + s1[...]).astype(bf16)
    act[...] = a
    ctx = lax.axis_index("ctx")
    kv[pl.ds(pl.multiple_of(ctx * ntok, ntok), ntok), :] = dot(a, kvw[...].astype(bf16)).astype(bf16)
    cbits = mesh_bits(sizes)["ctx"]
    share = lambda i: send(kv, [((ctx >> i << i) * ntok, ntok << i, cbits[i])])
    swap = share(0)
    run(1)
    put = []

    def cast(k, src, dst, o):
        fetch[k].wait()

        @pl.loop(0, src.shape[0] // 64)
        def _(t):
            r = pl.ds(pl.multiple_of(t * 64, 64), 64)
            dst[r, :] = src[r, :].astype(bf16)

        c = pltpu.make_async_copy(dst, o, ls.at[2 + k])
        c.start()
        put.append(c)

    def ends(pos):
        d, end = jnp.zeros(pos.shape, jnp.int32), 0
        for j in range(lens.shape[0] - 1):
            end = end + lens[j]
            d = d + (pos >= end).astype(jnp.int32)
        return d

    cast(0, upf, upb, up_o)
    slot = lax.broadcasted_iota(jnp.int32, (8, ntok), 0)
    qpos = ends(lax.broadcasted_iota(jnp.int32, (8, ntok), 1) + ctx * ntok)
    qdoc[...] = jnp.where((qpos == slot) | (slot > 2), 0.0, NEG)
    run(2)
    wait(swap)
    for i in range(1, len(cbits)):
        wait(share(i))
    cast(1, downf, downb, down_o)
    run(3)
    lane = lax.broadcasted_iota(jnp.int32, (keys, 128), 1)
    doc = ends(lax.broadcasted_iota(jnp.int32, (keys, 128), 0))
    full = kv[...].astype(f32)
    extra = jnp.where((lane == doc + HEAD) | ((lane > HEAD + 2) & (lane < HEAD + 6)), 1.0, 0.0)
    kaug[...] = jnp.where(lane < HEAD, full, extra).astype(bf16)
    flipped = jnp.concatenate([full[:, HEAD:], full[:, :HEAD]], axis=1)
    vaug[...] = jnp.where(lane < HEAD, flipped, jnp.where(lane < HEAD + 3, 1.0, 0.0)).astype(bf16)
    both = jnp.transpose(full)
    kt[...] = both[:HEAD].astype(bf16)
    vt[...] = jnp.concatenate([both[HEAD:], jnp.ones((1, keys), f32), jnp.zeros((15, keys), f32)], 0).astype(bf16)
    run(4)
    for k in range(5, len(stages) + 1):
        run(k)
    wait(own)
    for k, (src, o) in enumerate(((wqs, wq_o), (wos, wo_o))):
        c = pltpu.make_async_copy(src, o, ls.at[4 + k])
        c.start()
        put.append(c)
    for c in put:
        c.wait()


def head(sizes, nexp, tok, g1, s1, kvw, wq3, wo3, lens, up, down):
    ntok, keys, experts = tok.shape[0], tok.shape[0] * sizes["ctx"], nexp * sizes["exp"]
    vm, any_ = pl.BlockSpec(memory_space=pltpu.VMEM), pl.BlockSpec(memory_space=pl.ANY)
    sd, v = jax.ShapeDtypeStruct, pltpu.VMEM
    nsem = 64
    wide = (experts * HEAD, D)
    return pl.pallas_call(
        functools.partial(head_kernel, sizes, nexp, nsem),
        in_specs=[vm] * 6 + [pl.BlockSpec(memory_space=pltpu.SMEM), any_, any_],
        out_specs=[vm] * 6 + [any_] * 4,
        out_shape=[sd((ntok, D), bf16), sd((keys, 128), bf16), sd((keys, 128), bf16), sd((HEAD, keys), bf16),
                   sd((HEAD + 16, keys), bf16), sd((8, ntok), f32), sd(wide, bf16), sd(wide, bf16),
                   sd(up.shape, bf16), sd(down.shape, bf16)],
        scratch_shapes=[v(wide, bf16), v(wide, bf16), v((keys, 128), bf16), v(up.shape, f32), v(down.shape, f32),
                        v(up.shape, bf16), v(down.shape, bf16), pltpu.SemaphoreType.DMA((nsem,)),
                        pltpu.SemaphoreType.DMA((nsem,)), pltpu.SemaphoreType.DMA((6,))],
        compiler_params=pltpu.CompilerParams(collective_id=1, has_side_effects=True, vmem_limit_bytes=60 * 2**20),
        name="head",
    )(tok, g1, s1, kvw, wq3, wo3, lens, up, down)


def local(sizes, tokens, lengths, routes, route_gates, cotangent, gain_one, shift_one, kv_weight,
          query_weight, out_weight, gain_two, shift_two, up_weight, up_bias, down_weight, down_bias):
    x = tokens[0]
    nexp = query_weight.shape[0]
    row = lambda v: v.reshape(1, -1)
    act, kaug, vaug, kt, vt, qdoc, wq, wo, up, down = head(
        sizes, nexp, x, row(gain_one), row(shift_one), kv_weight, jnp.swapaxes(query_weight, 1, 2), out_weight, lengths[0], up_weight,
        down_weight)
    routes_t = routes[0].T
    gates_t = route_gates[0].T
    cd, q, ctx, lse = attn_fwd(act, wq, routes_t, gates_t, qdoc, kaug, vt, KB=384)
    out, dx, go, gq, gkv, small, gdown, gup = mega(
        sizes, nexp, cd, wo, x, cotangent[0], row(gain_two), row(shift_two), up, row(up_bias), down, row(down_bias), q,
        ctx, lse, routes_t, gates_t, qdoc, kaug, vaug, kt, act, wq, kv_weight, row(gain_one))
    go = go.reshape(nexp, HEAD, D)
    gq = jnp.swapaxes(gq.reshape(nexp, HEAD, D), 1, 2)
    vec = small.reshape(-1)
    v = lambda i: vec[i * D:(i + 1) * D]
    return (out[None], dx[None], v(3), v(4), gkv, gq, go, v(0), v(1), gup.astype(f32),
            vec[5 * D:5 * D + up_bias.shape[0]], gdown.astype(f32), v(2))


def solution(mesh):
    tok3 = P(("dp", "exp"), "ctx", None)
    ex = P("exp", None, None)
    r = P()
    in_specs = (tok3, P(("dp", "exp"), None), tok3, tok3, tok3, r, r, r, ex, ex, r, r, r, r, r, r)
    out_specs = (tok3, tok3, r, r, r, ex, ex, r, r, r, r, r, r)
    fn = functools.partial(local, dict(mesh.shape))
    return jax.shard_map(fn, mesh=mesh, in_specs=in_specs, out_specs=out_specs, check_vma=False)
```

```python
import functools
import math

import jax
import jax.numpy as jnp
from jax import lax
from jax.experimental import pallas as pl
from jax.experimental.pallas import tpu as pltpu
from jax.sharding import PartitionSpec as P

f32 = jnp.float32
bf16 = jnp.bfloat16
D = 512
HEAD = 64
TOP = 8
TB = 128
W = TOP * TB
NEG = -1e30
LOG2E = math.log2(math.e)
LN2 = math.log(2.0)
SMALL = 576
KBB = 384
STRIDE = 7
JOIN = 2
SAFE = 50.0
NN = (((1,), (0,)), ((), ()))
NT = (((1,), (1,)), ((), ()))
TN = (((0,), (0,)), ((), ()))
C0 = math.sqrt(2 / math.pi)
C1 = 0.044715
MESH = pl.DeviceIdType.MESH
AXES = ("dp", "ctx", "exp")


def attn_fwd_kernel(act_ref, wq_ref, routes_ref, gates_ref, qdoc_ref, kaug_ref, vt_ref,
                    cd_ref, q_ref, ctx_ref, lse_ref,
                    qt, qaug, s, acc, kn_ref, *, experts, tok, KB):
    i=pl.program_id(0)
    c=lax.axis_index("ctx")
    @pl.when(i==0)
    def _():
        kk=kaug_ref[...].astype(f32)
        kk=jnp.where(lax.broadcasted_iota(jnp.int32,kk.shape,1)<HEAD,kk*kk,0.0)
        kn_ref[0]=jnp.max(jnp.sum(kk,axis=1,keepdims=True))
    qt[...]=lax.dot_general(wq_ref[...], act_ref[...], NT, preferred_element_type=f32)*(0.125*LOG2E)
    n2=[]
    for k0 in range(0,TOP,4):
        r=[jnp.broadcast_to(routes_ref[k0+k:k0+k+1,:],(8,TB))[None] for k in range(4)]
        sel=[jnp.zeros((HEAD//8,8,TB),f32) for _ in range(4)]
        for e in range(experts):
            v=qt[e*HEAD:(e+1)*HEAD,:].reshape(HEAD//8,8,TB)
            sel=[jnp.where(r[k]==e,v,sel[k]) for k in range(4)]
        for k in range(4):
            sk=sel[k].reshape(HEAD,TB)
            n2.append(jnp.max(jnp.sum(sk*sk,axis=0,keepdims=True)))
            qaug[0:HEAD,(k0+k)*TB:(k0+k+1)*TB]=sk.astype(bf16)
    n2=functools.reduce(jnp.maximum,n2)*kn_ref[0]
    fast=n2<=SAFE*SAFE
    q_ref[0]=qaug[0:HEAD,:]
    qd=qdoc_ref[...]
    qaug[HEAD:HEAD+16,:]=jnp.concatenate([jnp.concatenate([qd,jnp.zeros_like(qd)],0)]*TOP,1).astype(bf16)
    qaug[HEAD+16:,:]=jnp.zeros((128-HEAD-16,W),bf16)
    q0=c*tok+i*TB
    nfull=q0//KB
    kd=pl.multiple_of(nfull*KB,KB)
    kp=lax.broadcasted_iota(jnp.int32,(KB,TB),0)+(kd-q0)
    tp=lax.broadcasted_iota(jnp.int32,(KB,TB),1)
    mask=kp<=tp
    acc[...]=jnp.zeros_like(acc)
    def scores(k0,n):
        return jnp.dot(kaug_ref[pl.ds(k0,n),:],qaug[...],preferred_element_type=f32)
    def masked(x):
        return jnp.concatenate([jnp.where(mask,x[:,k*TB:(k+1)*TB],NEG) for k in range(TOP)],1)
    def pv(k0,n,p):
        acc[...]+=jnp.dot(vt_ref[:,pl.ds(k0,n)],p,preferred_element_type=f32)
    def finish(m):
        l=acc[HEAD:HEAD+1,:]
        lse_ref[0]=m+jnp.log2(l)
        acc[0:HEAD,:]=acc[0:HEAD,:]*(1.0/l)
    @pl.when(fast)
    def _():
        def body(b,_):
            k0=pl.multiple_of(b*KB,KB)
            pv(k0,KB,jnp.exp2(scores(k0,KB)).astype(bf16))
            return 0
        lax.fori_loop(0,nfull,body,0)
        pv(kd,KB,jnp.exp2(masked(scores(kd,KB))).astype(bf16))
        finish(0.0)
    @pl.when(jnp.logical_not(fast))
    def _():
        def spass(b,m):
            k0=pl.multiple_of(b*KB,KB)
            x=scores(k0,KB)
            s[pl.ds(k0,KB),:]=x
            return jnp.maximum(m,jnp.max(x.reshape(KB//8,8,W),axis=0))
        m=lax.fori_loop(0,nfull,spass,jnp.full((8,W),NEG*2,f32))
        x=masked(scores(kd,KB))
        s[pl.ds(kd,KB),:]=x
        m=jnp.maximum(m,jnp.max(x.reshape(KB//8,8,W),axis=0))
        m=jnp.max(m,axis=0,keepdims=True)
        def ppass(b,_):
            k0=pl.multiple_of(b*KB,KB)
            pv(k0,KB,jnp.exp2(s[pl.ds(k0,KB),:]-m).astype(bf16))
            return 0
        lax.fori_loop(0,nfull+1,ppass,0)
        finish(m)
    ctx_ref[0]=acc[0:HEAD,:].astype(bf16)
    for k in range(TOP):
        acc[0:HEAD,k*TB:(k+1)*TB]*=gates_ref[k:k+1,:]
    r=[jnp.broadcast_to(routes_ref[k:k+1,:],(8,TB))[None] for k in range(TOP)]
    for h0 in range(0,HEAD,32):
        g=[acc[h0:h0+32,k*TB:(k+1)*TB].reshape(4,8,TB) for k in range(TOP)]
        for e in range(experts):
            o=jnp.zeros((4,8,TB),f32)
            for k in range(TOP):
                o=jnp.where(r[k]==e,g[k],o)
            cd_ref[e*HEAD+h0:e*HEAD+h0+32,:]=o.reshape(32,TB).astype(bf16)

def attn_fwd(act, wq, routesT, gatesT, qdoc, kaug, vt, KB=256):
    tok=act.shape[0]; experts=wq.shape[0]//HEAD; keys=kaug.shape[0]; n=tok//TB; vr=vt.shape[0]
    full=lambda a: pl.BlockSpec(a.shape,lambda i,*_:(0,)*a.ndim)
    return pl.pallas_call(
        functools.partial(attn_fwd_kernel,experts=experts,tok=tok,KB=KB),
        grid_spec=pltpu.PrefetchScalarGridSpec(num_scalar_prefetch=0,grid=(n,),
          in_specs=[pl.BlockSpec((TB,D),lambda i,*_:(i,0)),full(wq),
            pl.BlockSpec((TOP,TB),lambda i,*_:(0,i)),pl.BlockSpec((TOP,TB),lambda i,*_:(0,i)),
            pl.BlockSpec((8,TB),lambda i,*_:(0,i)),full(kaug),full(vt)],
          out_specs=[pl.BlockSpec((experts*HEAD,TB),lambda i,*_:(0,i)),
            pl.BlockSpec((1,HEAD,W),lambda i,*_:(i,0,0)),
            pl.BlockSpec((1,HEAD,W),lambda i,*_:(i,0,0)),
            pl.BlockSpec((1,1,W),lambda i,*_:(i,0,0))],
          scratch_shapes=[pltpu.VMEM((experts*HEAD,TB),f32),pltpu.VMEM((128,W),bf16),
            pltpu.VMEM((keys,W),f32),pltpu.VMEM((vr,W),f32),pltpu.SMEM((1,),f32)]),
        out_shape=[jax.ShapeDtypeStruct((experts*HEAD,tok),bf16),
          jax.ShapeDtypeStruct((n,HEAD,W),bf16),jax.ShapeDtypeStruct((n,HEAD,W),bf16),
          jax.ShapeDtypeStruct((n,1,W),f32)],
        compiler_params=pltpu.CompilerParams(vmem_limit_bytes=60*2**20),
        name="attn_fwd",
    )(act,wq,routesT,gatesT,qdoc,kaug,vt)


def dot(a, b, dims=NN):
    return lax.dot_general(a, b, dims, preferred_element_type=f32)


def split3(x):
    hi = x.astype(bf16).astype(f32)
    r = x - hi
    mid = r.astype(bf16).astype(f32)
    return hi, mid, r - mid


class Here:
    def __init__(self, sizes):
        self.at = {a: lax.axis_index(a) for a in AXES}
        self.bit = {(ax, m): lax.rem(self.at[ax] // m, 2) for bits in mesh_bits(sizes).values() for ax, m in bits}
        self.known = {}

    def across(self, bits):
        bits = tuple(sorted(bits))
        if bits not in self.known:
            at = dict(self.at)
            for ax, m in bits:
                at[ax] = at[ax] + m - 2 * m * self.bit[ax, m]
            self.known[bits] = tuple(at[a] for a in AXES)
        return self.known[bits]


def subsets(group):
    return [[b for i, b in enumerate(group) if d >> i & 1] for d in range(1, 1 << len(group))]


def mesh_bits(sizes):
    return {a: [(a, 1 << i) for i in range(sizes[a].bit_length() - 1)] for a in AXES}


def small_mesh(sizes):
    return sizes["dp"] == sizes["ctx"] == 2 and sizes["exp"] == 8


def chain_orders(sizes):
    b = mesh_bits(sizes)
    e, d, c = b["exp"], b["dp"], b["ctx"]
    one = lambda bits: [(x,) for x in bits]
    late = one(e + d + c)
    if not small_mesh(sizes):
        return [late] * 3, late
    dense = [one(e[:1] + d + c + e[1:]), one(e[:1] + c + d + e[1:]), late]
    fast = [tuple(e[:1]), tuple(d + c), tuple(e[1:])]
    return dense, fast


def chain_plan(n, order):
    plan = []
    for group in order:
        ways = 1 << len(group)
        halve = n % (16 * ways) == 0
        n = n // ways if halve else n
        plan.append((halve, group, n))
    return plan


def rows(ref, start, n):
    return ref.at[pl.ds(pl.multiple_of(start, 16), n), :]


def add_rows(dst, d0, parts, n):
    ch = math.gcd(n, 64)

    @pl.loop(0, n // ch)
    def _(t):
        o = pl.multiple_of(t * ch, ch)
        g = [r[pl.ds(pl.multiple_of(s + o, 16), ch), :] for r, s in parts]
        total = g[0] + g[1] if len(g) == 2 else functools.reduce(jnp.add, [v.astype(f32) for v in g]).astype(bf16)
        dst[pl.ds(pl.multiple_of(d0 + o, 16), ch), :] = total


def block_places(n, order, owner):
    bits = [bit for halve, group, _ in chain_plan(n, order) if halve for bit in group]
    own = sorted([b for b in bits if b[0] == owner], reverse=True)
    nat = own + sorted([b for b in bits if b[0] != owner])
    places = []
    for i in range(1 << len(nat)):
        v = {b: (i >> (len(nat) - 1 - k)) & 1 for k, b in enumerate(nat)}
        places.append(sum(v[b] << (len(bits) - 1 - k) for k, b in enumerate(bits)))
    return n >> len(nat), places


class Chain:
    def __init__(self, work, final, base, n, order, owner=None, fbase=0):
        self.work, self.final, self.base, self.n, self.order = work, final, base, n, order
        self.owner, self.fbase = owner, fbase
        self.plan = chain_plan(n, order)
        self.landed = sum(m * ((1 << len(g)) - 1) for _, g, m in self.plan)
        self.back = [i for i in reversed(range(len(order))) if self.plan[i][0] and order[i][0][0] != owner]
        if owner:
            self.back.sort(key=lambda i: order[i], reverse=True)
        self.m = len(self.plan)
        self.groups = [g for _, g, _ in self.plan] + [order[i] for i in self.back]
        self.nsem = sum((1 << len(g)) - 1 for g in self.groups)
        self.nsteps = len(self.groups) + 1

    def place(self, here, land, lbase, ss, rs, sem):
        self.here, self.land, self.ss, self.rs = here, land, ss, rs
        self.lb, self.sem = [], []
        for _, g, m in self.plan:
            self.lb.append(lbase)
            lbase += m * ((1 << len(g)) - 1)
        for g in self.groups:
            for f in subsets(g):
                here.across(f)
            self.sem.append(sem)
            sem += (1 << len(g)) - 1
        self.offs, off = [], self.base
        for halve, g, m in self.plan:
            self.offs.append(off)
            if halve:
                off = off + self.index(g, []) * m
        self.last = off

    def index(self, group, flipped):
        v = 0
        for b in group:
            w = self.here.bit[b]
            v = 2 * v + (1 - w if b in flipped else w)
        return v

    def final_range(self, j):
        m = self.plan[-1][2]
        if self.owner is None:
            if j == 0:
                return self.last, m
            i = self.back[j - 1]
            return self.offs[i], self.plan[i][2] << len(self.order[i])
        rest = sorted(b for i in self.back for b in self.order[i])
        done = [b for i in self.back[:j] for b in self.order[i]]
        off = self.fbase
        for k, b in enumerate(rest):
            if b not in done:
                off = off + self.here.bit[b] * (m << (len(rest) - 1 - k))
        return off, m << len(done)

    def copies(self, k):
        out, g = [], self.groups[k]
        for d, flipped in enumerate(subsets(g)):
            if k < self.m:
                halve, _, n = self.plan[k]
                start = self.offs[k] + self.index(g, flipped) * n if halve else self.offs[k]
                src, dst = rows(self.work, start, n), rows(self.land, self.lb[k] + d * n, n)
            else:
                src = dst = rows(self.final, *self.final_range(k - self.m))
            out.append(pltpu.make_async_remote_copy(
                src_ref=src, dst_ref=dst, send_sem=self.ss.at[self.sem[k] + d], recv_sem=self.rs.at[self.sem[k] + d],
                device_id=self.here.across(flipped), device_id_type=MESH))
        return out

    def step(self, k):
        if k:
            for c in self.copies(k - 1):
                c.wait()
            if k <= self.m:
                i = k - 1
                halve, g, n = self.plan[i]
                last = i == self.m - 1
                d = self.offs[i] + self.index(g, []) * n if halve else self.offs[i]
                parts = [(self.work, d)] + [(self.land, self.lb[i] + j * n) for j in range((1 << len(g)) - 1)]
                add_rows(self.final if last else self.work, self.final_range(0)[0] if last else d, parts, n)
        if k < len(self.groups):
            for c in self.copies(k):
                c.start()


def greet(here, groups):
    devices = {tuple(sorted(f)) for g in groups for f in subsets(g)}
    bar = pltpu.get_barrier_semaphore()
    for f in sorted(devices):
        pl.semaphore_signal(bar, inc=1, device_id=here.across(f), device_id_type=MESH)
    pl.semaphore_wait(bar, len(devices))


def dense_parts(n, orders):
    a = n * 3 // 8 // 32 * 32
    return [(0, a, orders[0]), (a, a, orders[1]), (2 * a, n - 2 * a, orders[2])]


def make_chains(sizes, steps, part, nexp, keys, dsrc, fin, osrc, go, qsrc, gq, ksrc, kfin, ssrc, sfin):
    orders, small = chain_orders(sizes)
    n = sizes["exp"] * HEAD
    kbits = [(b,) for b in mesh_bits(sizes)["ctx"][::-1]]
    part = part * JOIN
    dense = [[Chain(dsrc, fin, j * part + b, m, o) for b, m, o in dense_parts(part, orders)] for j in range(steps // JOIN)]
    return dict(
        dense=dense,
        o=[Chain(osrc, go, j * n, n, orders[j % 3], "exp", j * HEAD) for j in range(nexp)],
        q=[Chain(qsrc, gq, j * n, n, orders[j % 3], "exp", j * HEAD) for j in range(nexp)],
        k=[Chain(ksrc, kfin, 0, keys, kbits, "ctx", 0)],
        g=[Chain(ssrc, sfin, 0, D, small)],
        s=[Chain(ssrc, sfin, D, SMALL - D, small)],
    )


def flat(chains):
    wide = [c for g in chains["dense"] for c in g] + chains["o"] + chains["q"]
    return wide, chains["k"] + chains["g"] + chains["s"]


def place_all(here, chains, land, nland, ss, rs):
    sem = 0
    for group, buf in zip(flat(chains), (land, nland)):
        lb = 0
        for c in group:
            c.place(here, buf, lb, ss, rs, sem)
            lb += c.landed
            sem += c.nsem


def mega_kernel(sizes, nf, nb, nexp, fb,
                cd, wo, tok, cot, g2, s2, up_ref, upb, down_ref, downb, q_ref, ctx_ref, lse_ref, routes_ref, gates_ref,
                qdoc_ref, kaug_ref, vaug_ref, kt_ref, act1, wq, kvw, g1,
                out, dx, go_o, gq_o, gkv_o, sm_o, gd_o, gu_o,
                mid, rstd, act, actT, dffn, dct, dqd, gub, gsm,
                qaug, daug, rhs, pds, dq, dkv,
                dsrc, fin, osrc, go, qsrc, gq, ksrc, kfin, ssrc, sfin, land, nland, ss, rs, lsem):
    s = pl.program_id(0)
    experts = cd.shape[0] // HEAD
    ntok, keys = tok.shape[0], kaug_ref.shape[0]
    part = 2 * fb
    chains = make_chains(sizes, nf, part, nexp, keys, dsrc, fin, osrc, go, qsrc, gq, ksrc, kfin, ssrc, sfin)
    here = Here(sizes)
    place_all(here, chains, land, nland, ss, rs)
    ticks = [(j, p) for j in range(nf) for p in range(3)] + [(nf + i, p) for i in range(nb) for p in range(4)]
    ticks += [(nf + nb, p) for p in range(4)]
    table, late = {}, []
    for j, group in enumerate(chains["dense"] + [chains["o"]]):
        t0 = ticks.index((j * JOIN + JOIN - 1, 2)) if j < nf // JOIN else ticks.index((nf, 0))
        for k in range(max(c.nsteps for c in group)):
            todo = [(c, k) for c in group if k < c.nsteps]
            if t0 + STRIDE * k // 2 < len(ticks):
                table.setdefault(ticks[t0 + STRIDE * k // 2], []).extend(todo)
            else:
                late.extend(todo)

    def tick(step, pos):
        for at, todo in table.items():
            if at[1] != pos or step != ("f" if at[0] < nf else "b" if at[0] < nf + nb else "t"):
                continue
            if step == "t":
                for c, k in todo:
                    c.step(k)
                continue

            @pl.when(s == at[0])
            def _():
                for c, k in todo:
                    c.step(k)

    def put_owner(src_rows, value, e, order_of):
        for j in range(nexp):
            c = order_of[j]
            block, places = block_places(c.n, c.order, "exp")
            per = HEAD // block
            for b in range(per):
                at = c.base + places[e * per + b] * block
                src_rows[at:at + block, :] = value[j * HEAD + b * block:j * HEAD + (b + 1) * block, :]

    @pl.when(s == 0)
    def _():
        m = tok[...] + dot(cd[...], wo[...], TN)
        mid[...] = m
        cen = m - jnp.mean(m, axis=-1, keepdims=True)
        r = lax.rsqrt(jnp.mean(cen * cen, axis=-1, keepdims=True) + 1e-5)
        xh = cen * r
        rstd[...] = jnp.broadcast_to(r, rstd.shape)
        a = xh * g2[...] + s2[...]
        act[...] = a.astype(bf16)
        actT[...] = jnp.transpose(a).astype(bf16)
        dffn[...] = cot[...].astype(bf16)
        out[...] = m + downb[...]
        dx[...] = jnp.zeros_like(dx)
        greet(here, [g for group in flat(chains) for c in group for g in c.groups])

    @pl.when(s < nf)
    def _():
        up, down = up_ref[...], down_ref[...]
        pre = dot(act[...], up) + upb[...]
        x2 = pre * pre
        th = jnp.tanh(pre * (C0 + C0 * C1 * x2))
        h = 0.5 * (1.0 + th)
        hid = (pre * h).astype(bf16)
        gp = h + (0.5 * pre) * (1.0 - th * th) * (C0 + 3.0 * C0 * C1 * x2)
        out[...] += dot(hid, down)
        tick("f", 0)
        r0 = pl.multiple_of(s * part, part)
        dsrc[pl.ds(r0, fb), :] = dot(hid, dffn[...], TN).astype(bf16)
        tick("f", 1)
        dpb = (dot(dffn[...], down, NT) * gp).astype(bf16)
        gub[pl.ds(s, 1), :] = jnp.sum(dpb.astype(f32), axis=0, keepdims=True)
        dsrc[pl.ds(pl.multiple_of(r0 + fb, fb), fb), :] = dot(actT[...], dpb).astype(bf16)
        dx[...] += dot(dpb, up, NT)
        tick("f", 2)

    @pl.when(s == nf - 1)
    def _():
        d = dx[...]
        m = mid[...]
        xh = (m - jnp.mean(m, axis=-1, keepdims=True)) * rstd[:, 0:1]
        gx = d * g2[...]
        dm = cot[...] + rstd[:, 0:1] * (gx - jnp.mean(gx, axis=-1, keepdims=True)
                                        - xh * jnp.mean(gx * xh, axis=-1, keepdims=True))
        mid[...] = dm
        gsm[...] = jnp.concatenate([jnp.sum(d * xh, axis=0, keepdims=True), jnp.sum(d, axis=0, keepdims=True),
                                    jnp.sum(dffn[...].astype(f32), axis=0, keepdims=True)], axis=0)
        dmb = dm.astype(bf16)
        act[...] = dmb
        dct[...] = dot(wo[...], dmb, NT).astype(bf16)
        w = nexp * HEAD
        for e in range(sizes["exp"]):
            put_owner(osrc, dot(cd[e * w:(e + 1) * w, :], dmb).astype(bf16), e, chains["o"])

    @pl.when(s == nf)
    def _():
        dkv[...] = jnp.zeros_like(dkv)
        rhs[...] = jnp.zeros_like(rhs)

    @pl.when((s >= nf) & (s < nf + nb))
    def _():
        i = s - nf
        lanes = pl.ds(pl.multiple_of(i * TB, TB), TB)
        q = q_ref[0]
        qaug[0:HEAD, :] = q
        rhs[0:HEAD, 0:W] = q
        hi, md, lo = split3(-lse_ref[0])
        qd = qdoc_ref[...]
        qaug[HEAD:HEAD + 16, :] = jnp.concatenate(
            [jnp.concatenate([qd[0:3, :]] * TOP, 1), hi, md, lo, jnp.zeros((10, W), f32)], 0).astype(bf16)
        qaug[HEAD + 16:, :] = jnp.zeros((128 - HEAD - 16, W), bf16)
        r = [jnp.broadcast_to(routes_ref[k:k + 1, :], (8, TB))[None] for k in range(TOP)]
        for k0 in range(0, TOP, 4):
            sel = [jnp.zeros((HEAD // 8, 8, TB), f32) for _ in range(4)]
            for e in range(experts):
                v = dct[e * HEAD:(e + 1) * HEAD, lanes].astype(f32).reshape(HEAD // 8, 8, TB)
                sel = [jnp.where(r[k0 + k] == e, v, sel[k]) for k in range(4)]
            for k in range(4):
                sl = slice((k0 + k) * TB, (k0 + k + 1) * TB)
                dc = (sel[k].reshape(HEAD, TB) * gates_ref[k0 + k:k0 + k + 1, :]).astype(bf16)
                daug[0:HEAD, sl] = dc
                rhs[HEAD:, W + (k0 + k) * TB:W + (k0 + k + 1) * TB] = dc
                dq[0:1, sl] = jnp.sum(dc.astype(f32) * ctx_ref[0, :, sl].astype(f32), axis=0, keepdims=True)
        hi, md, lo = split3(-dq[0:1, :])
        daug[HEAD:HEAD + 16, :] = jnp.concatenate([hi, md, lo, jnp.zeros((13, W), f32)], 0).astype(bf16)
        daug[HEAD + 16:, :] = jnp.zeros((128 - HEAD - 16, W), bf16)
        dq[...] = jnp.zeros_like(dq)
        q0 = lax.axis_index("ctx") * ntok + i * TB
        nfull = q0 // KBB
        kd = pl.multiple_of(nfull * KBB, KBB)

        def block(k0, mask):
            p = jnp.exp2(dot(kaug_ref[pl.ds(k0, KBB), :], qaug[...]))
            if mask is not None:
                p = jnp.concatenate([jnp.where(mask, p[:, k * TB:(k + 1) * TB], 0.0) for k in range(TOP)], 1)
            dp = dot(vaug_ref[pl.ds(k0, KBB), :], daug[...])
            pds[:, W:] = p.astype(bf16)
            pds[:, :W] = (p * dp).astype(bf16)
            dq[...] += dot(kt_ref[:, pl.ds(k0, KBB)], pds[:, :W])
            dkv[pl.ds(k0, KBB), :] += dot(pds[...], rhs[...], NT)

        def body(b, _):
            block(pl.multiple_of(b * KBB, KBB), None)
            return 0

        tick("b", 0)
        lax.fori_loop(0, nfull, body, 0)
        tick("b", 1)
        kp = lax.broadcasted_iota(jnp.int32, (KBB, TB), 0) + (kd - q0)
        tp = lax.broadcasted_iota(jnp.int32, (KBB, TB), 1)
        block(kd, kp <= tp)
        tick("b", 2)
        dq[...] *= 0.125
        for h0 in range(0, HEAD, 32):
            g = [dq[h0:h0 + 32, k * TB:(k + 1) * TB].reshape(4, 8, TB) for k in range(TOP)]
            for e in range(experts):
                o = jnp.zeros((4, 8, TB), f32)
                for k in range(TOP):
                    o = jnp.where(r[k] == e, g[k], o)
                dqd[e * HEAD + h0:e * HEAD + h0 + 32, lanes] = o.reshape(32, TB).astype(bf16)
        tick("b", 3)

    @pl.when(s == nf + nb)
    def _():
        lane = lax.broadcasted_iota(jnp.int32, (1, 128), 1)
        ksrc[...] = (dkv[...] * jnp.where(lane < HEAD, LN2, 1.0)).astype(bf16)
        kc, gc, sc = chains["k"][0], chains["g"][0], chains["s"][0]
        kc.step(0)
        tick("t", 0)
        w = nexp * HEAD
        for e in range(sizes["exp"]):
            put_owner(qsrc, dot(dqd[e * w:(e + 1) * w, :], act1[...]).astype(bf16), e, chains["q"])
        for c in chains["q"]:
            c.step(0)
        for k in range(1, kc.nsteps):
            kc.step(k)
        ssrc[0:D, :] = dot(act1[...], kfin[...], TN).astype(bf16)
        gc.step(0)
        tick("t", 1)
        for c in chains["q"]:
            c.step(1)
        da = dot(dqd[...], wq[...], TN) + dot(kfin[...], kvw[...].astype(bf16), NT)
        gc.step(1)
        tick("t", 2)
        x = tok[...]
        cen = x - jnp.mean(x, axis=-1, keepdims=True)
        r1 = lax.rsqrt(jnp.mean(cen * cen, axis=-1, keepdims=True) + 1e-5)
        xh = cen * r1
        gg1, gs1 = jnp.sum(da * xh, axis=0, keepdims=True), jnp.sum(da, axis=0, keepdims=True)
        vecs = [gsm[0:1, :], gsm[1:2, :], gsm[2:3, :], gg1, gs1] + [gub[j:j + 1, :] for j in range(nf)]
        vecs = [v[:, o:o + 128] for v in vecs for o in range(0, v.shape[1], 128)]
        vecs.append(jnp.zeros((SMALL - D - len(vecs), 128), f32))
        ssrc[D:SMALL, :] = jnp.concatenate(vecs, 0).astype(bf16)
        sc.step(0)
        for c in chains["q"]:
            c.step(2)
        gc.step(2)
        gx = da * g1[...]
        dx[...] = mid[...] + r1 * (gx - jnp.mean(gx, axis=-1, keepdims=True)
                                   - xh * jnp.mean(gx * xh, axis=-1, keepdims=True))
        tick("t", 3)
        rounds = max(c.nsteps for c in (gc, sc, *chains["q"]))
        for k in range(1, rounds):
            for c, lag in [(c, 2) for c in chains["q"]] + [(gc, 2), (sc, 0)]:
                if k + lag < c.nsteps:
                    c.step(k + lag)
            share = -(-len(late) // 3)
            for c, n in late[(k - 1) * share:k * share]:
                c.step(n)
            if k == 3:
                moved = []
                for j in range(nf):
                    r0 = j * part
                    moved.append(pltpu.make_async_copy(
                        fin.at[r0:r0 + fb, :], gd_o.at[j * fb:(j + 1) * fb, :], lsem.at[2 * j]))
                    moved.append(pltpu.make_async_copy(
                        fin.at[r0 + fb:r0 + part, :], gu_o.at[:, j * fb:(j + 1) * fb], lsem.at[2 * j + 1]))
                for c in moved:
                    c.start()
        go_o[...] = go[...].astype(f32)
        gq_o[...] = gq[...].astype(f32)
        gkv_o[...] = sfin[0:D, :].astype(f32)
        sm_o[...] = sfin[D:SMALL, :].astype(f32)
        for c in moved:
            c.wait()


def mega(sizes, nexp, cd, wo, tok, cot, g2, s2, up, upb, down, downb, q, ctx, lse, routes, gates, qdoc, kaug, vaug, kt,
         act1, wq, kvw, g1, fb=512):
    ntok, keys, ff, eh = tok.shape[0], kaug.shape[0], up.shape[1], wo.shape[0]
    nf, nb = ff // fb, ntok // TB
    part = 2 * fb
    sd = jax.ShapeDtypeStruct
    z = [None] * 10
    chains = make_chains(sizes, nf, part, nexp, keys, *z)
    wide, narrow = flat(chains)
    land, nland = sum(c.landed for c in wide), sum(c.landed for c in narrow)
    nsem = sum(c.nsem for c in wide + narrow)
    once = pl.Buffered(1)
    full = lambda a: pl.BlockSpec(a.shape, lambda s: (0,) * a.ndim, pipeline_mode=once)
    fo = lambda *sh: pl.BlockSpec(sh, lambda s: (0,) * len(sh), pipeline_mode=once)
    fj = lambda s: jnp.minimum(s, nf - 1)
    bi = lambda s: jnp.clip(s - nf, 0, nb - 1)
    blk = lambda r: pl.BlockSpec((r, TB), lambda s: (0, bi(s)))
    b3 = lambda a: pl.BlockSpec((1,) + a.shape[1:], lambda s: (bi(s), 0, 0))
    any_ = pl.BlockSpec(memory_space=pl.ANY)
    v = pltpu.VMEM
    return pl.pallas_call(
        functools.partial(mega_kernel, sizes, nf, nb, nexp, fb),
        grid=(nf + nb + 1,),
        in_specs=[full(cd), full(wo), full(tok), full(cot), full(g2), full(s2),
                  pl.BlockSpec((D, fb), lambda s: (0, fj(s))), pl.BlockSpec((1, fb), lambda s: (0, fj(s))),
                  pl.BlockSpec((fb, D), lambda s: (fj(s), 0)), full(downb), b3(q), b3(ctx), b3(lse),
                  blk(TOP), blk(TOP), blk(8), full(kaug), full(vaug), full(kt), full(act1), full(wq), full(kvw), full(g1)],
        out_specs=[fo(ntok, D), fo(ntok, D), fo(nexp * HEAD, D), fo(nexp * HEAD, D), fo(D, 128), fo(SMALL - D, 128), any_, any_],
        out_shape=[sd((ntok, D), f32), sd((ntok, D), f32), sd((nexp * HEAD, D), f32), sd((nexp * HEAD, D), f32),
                   sd((D, 128), f32), sd((SMALL - D, 128), f32), sd((ff, D), bf16), sd((D, ff), bf16)],
        scratch_shapes=[
            v((ntok, D), f32), v((ntok, 128), f32), v((ntok, D), bf16), v((D, ntok), bf16),
            v((ntok, D), bf16), v((eh, ntok), bf16), v((eh, ntok), bf16), v((nf, fb), f32), v((3, D), f32),
            v((128, W), bf16), v((128, W), bf16), v((128, 2 * W), bf16), v((KBB, 2 * W), bf16), v((HEAD, W), f32),
            v((keys, 128), f32),
            v((nf * part, D), bf16), v((nf * part, D), bf16), v((eh, D), bf16), v((nexp * HEAD, D), bf16),
            v((eh, D), bf16), v((nexp * HEAD, D), bf16), v((keys, 128), bf16), v((ntok, 128), bf16),
            v((SMALL, 128), bf16), v((SMALL, 128), bf16), v((land, D), bf16), v((nland, 128), bf16),
            pltpu.SemaphoreType.DMA((nsem,)), pltpu.SemaphoreType.DMA((nsem,)), pltpu.SemaphoreType.DMA((2 * nf,))],
        compiler_params=pltpu.CompilerParams(collective_id=0, has_side_effects=True, vmem_limit_bytes=62 * 2**20),
        name="mega",
    )(cd, wo, tok, cot, g2, s2, up, upb, down, downb, q, ctx, lse, routes, gates, qdoc, kaug, vaug, kt, act1, wq, kvw, g1)


def gather_stages(sizes, here, shard):
    e = lax.axis_index("exp")
    if not small_mesh(sizes) or shard % 64:
        stages = []
        for i, bit in enumerate(mesh_bits(sizes)["exp"]):
            stages.append([((e >> i << i) * shard, shard << i, [bit])])
        return stages, []
    core, zl, zh, x, y = ("exp", 1), ("exp", 2), ("exp", 4), ("dp", 1), ("ctx", 1)
    quarter = shard // 4
    flip = lambda bit, n: n * (1 - 2 * here.bit[bit])
    at = lambda dz: e + (dz & 1) * flip(zl, 2) + (dz >> 1) * flip(zh, 4)
    row = lambda dz: at(dz) * shard + (here.bit[x] * 2 + here.bit[y]) * quarter
    stages = [
        [(row(0), quarter, f) for f in subsets((zl, zh))],
        [(row(d), quarter, f) for d in (1, 2, 3) for f in subsets((x, y))],
        [(at(d) * shard, shard, [core]) for d in (1, 2, 3)],
    ]
    return stages, [(e * shard, shard, [core])]


def head_kernel(sizes, nexp, nsem, tok, g1, s1, kvw, wq3, wo3, lens, up_h, down_h,
                act, kaug, vaug, kt, vt, qdoc, wq_o, wo_o, up_o, down_o,
                wqs, wos, kv, upf, downf, upb, downb, ss, rs, ls):
    here = Here(sizes)
    ntok, keys, shard = tok.shape[0], kv.shape[0], nexp * HEAD
    fetch = [pltpu.make_async_copy(up_h, upf, ls.at[0]), pltpu.make_async_copy(down_h, downf, ls.at[1])]
    for c in fetch:
        c.start()
    mine = lax.axis_index("exp") * shard
    for j in range(nexp):
        r = pl.ds(pl.multiple_of(mine + j * HEAD, HEAD), HEAD)
        wqs[r, :] = wq3[j].astype(bf16)
        wos[r, :] = wo3[j].astype(bf16)
    b = mesh_bits(sizes)
    exact = [tuple(b["exp"][1:]), tuple(b["dp"] + b["ctx"])] if small_mesh(sizes) else []
    greet(here, [(x,) for a in AXES for x in b[a]] + exact)
    count = [0]

    def send(buf, moves):
        out = []
        for start, n, bits in moves:
            r = rows(buf, start, n)
            k = count[0]
            count[0] += 1
            c = pltpu.make_async_remote_copy(src_ref=r, dst_ref=r, send_sem=ss.at[k], recv_sem=rs.at[k],
                                             device_id=here.across(bits), device_id_type=MESH)
            c.start()
            out.append(c)
        return out

    def wait(copies):
        for c in copies:
            c.wait()

    stages, early = gather_stages(sizes, here, shard)
    work = []

    def run(k):
        for buf, lag in ((wqs, 0), (wos, 1)):
            i = k - lag
            if 0 < i <= len(stages):
                wait(flying[buf is wos])
            if 0 <= i < len(stages):
                flying[buf is wos] = send(buf, stages[i])

    flying = [[], []]
    run(0)
    own = send(wqs, early) + send(wos, early)
    x = tok[...]
    cen = x - jnp.mean(x, axis=-1, keepdims=True)
    a = (cen * lax.rsqrt(jnp.mean(cen * cen, axis=-1, keepdims=True) + 1e-5) * g1[...] + s1[...]).astype(bf16)
    act[...] = a
    ctx = lax.axis_index("ctx")
    kv[pl.ds(pl.multiple_of(ctx * ntok, ntok), ntok), :] = dot(a, kvw[...].astype(bf16)).astype(bf16)
    cbits = mesh_bits(sizes)["ctx"]
    share = lambda i: send(kv, [((ctx >> i << i) * ntok, ntok << i, [cbits[i]])])
    swap = share(0)
    run(1)
    put = []

    def cast(k, src, dst, o):
        fetch[k].wait()

        @pl.loop(0, src.shape[0] // 64)
        def _(t):
            r = pl.ds(pl.multiple_of(t * 64, 64), 64)
            dst[r, :] = src[r, :].astype(bf16)

        c = pltpu.make_async_copy(dst, o, ls.at[2 + k])
        c.start()
        put.append(c)

    def ends(pos):
        d, end = jnp.zeros(pos.shape, jnp.int32), 0
        for j in range(lens.shape[0] - 1):
            end = end + lens[j]
            d = d + (pos >= end).astype(jnp.int32)
        return d

    cast(0, upf, upb, up_o)
    slot = lax.broadcasted_iota(jnp.int32, (8, ntok), 0)
    qpos = ends(lax.broadcasted_iota(jnp.int32, (8, ntok), 1) + ctx * ntok)
    qdoc[...] = jnp.where((qpos == slot) | (slot > 2), 0.0, NEG)
    run(2)
    wait(swap)
    for i in range(1, len(cbits)):
        wait(share(i))
    cast(1, downf, downb, down_o)
    run(3)
    lane = lax.broadcasted_iota(jnp.int32, (keys, 128), 1)
    doc = ends(lax.broadcasted_iota(jnp.int32, (keys, 128), 0))
    full = kv[...].astype(f32)
    extra = jnp.where((lane == doc + HEAD) | ((lane > HEAD + 2) & (lane < HEAD + 6)), 1.0, 0.0)
    kaug[...] = jnp.where(lane < HEAD, full, extra).astype(bf16)
    flipped = jnp.concatenate([full[:, HEAD:], full[:, :HEAD]], axis=1)
    vaug[...] = jnp.where(lane < HEAD, flipped, jnp.where(lane < HEAD + 3, 1.0, 0.0)).astype(bf16)
    both = jnp.transpose(full)
    kt[...] = both[:HEAD].astype(bf16)
    vt[...] = jnp.concatenate([both[HEAD:], jnp.ones((1, keys), f32), jnp.zeros((15, keys), f32)], 0).astype(bf16)
    run(4)
    for k in range(5, len(stages) + 2):
        run(k)
    wait(own)
    for k, (src, o) in enumerate(((wqs, wq_o), (wos, wo_o))):
        c = pltpu.make_async_copy(src, o, ls.at[4 + k])
        c.start()
        put.append(c)
    for c in put:
        c.wait()


def head(sizes, nexp, tok, g1, s1, kvw, wq3, wo3, lens, up, down):
    ntok, keys, experts = tok.shape[0], tok.shape[0] * sizes["ctx"], nexp * sizes["exp"]
    vm, any_ = pl.BlockSpec(memory_space=pltpu.VMEM), pl.BlockSpec(memory_space=pl.ANY)
    sd, v = jax.ShapeDtypeStruct, pltpu.VMEM
    nsem = 64
    wide = (experts * HEAD, D)
    return pl.pallas_call(
        functools.partial(head_kernel, sizes, nexp, nsem),
        in_specs=[vm] * 6 + [pl.BlockSpec(memory_space=pltpu.SMEM), any_, any_],
        out_specs=[vm] * 6 + [any_] * 4,
        out_shape=[sd((ntok, D), bf16), sd((keys, 128), bf16), sd((keys, 128), bf16), sd((HEAD, keys), bf16),
                   sd((HEAD + 16, keys), bf16), sd((8, ntok), f32), sd(wide, bf16), sd(wide, bf16),
                   sd(up.shape, bf16), sd(down.shape, bf16)],
        scratch_shapes=[v(wide, bf16), v(wide, bf16), v((keys, 128), bf16), v(up.shape, f32), v(down.shape, f32),
                        v(up.shape, bf16), v(down.shape, bf16), pltpu.SemaphoreType.DMA((nsem,)),
                        pltpu.SemaphoreType.DMA((nsem,)), pltpu.SemaphoreType.DMA((6,))],
        compiler_params=pltpu.CompilerParams(collective_id=1, has_side_effects=True, vmem_limit_bytes=60 * 2**20),
        name="head",
    )(tok, g1, s1, kvw, wq3, wo3, lens, up, down)


def finish_kernel(nc, sm, gd, gu, *refs):
    moves, wide_o, moved, vec_o = refs[:5], refs[5:7], refs[7:12], refs[12:18]
    lows, wides, vias, si, so = refs[18:20], refs[20:22], refs[22:27], refs[27], refs[28]
    ins, outs, parts = [], [], []
    for i, src in enumerate((gd, gu)):
        n = src.shape[0] // nc
        for j in range(nc):
            r = slice(j * n, (j + 1) * n)
            ins.append(pltpu.make_async_copy(src.at[r, :], lows[i].at[r, :], si.at[i * nc + j]))
            outs.append(pltpu.make_async_copy(wides[i].at[r, :], wide_o[i].at[r, :], so.at[i * nc + j]))
            parts.append((i, r))
    for k, (a, via, b) in enumerate(zip(moves, vias, moved)):
        ins.append(pltpu.make_async_copy(a, via, si.at[2 * nc + k]))
        outs.append(pltpu.make_async_copy(via, b, so.at[2 * nc + k]))
        parts.append(None)
    for c in ins:
        c.start()
    at = 0
    for o in vec_o:
        n = o.shape[1] // 128
        o[...] = jnp.concatenate([sm[j:j + 1, :] for j in range(at, at + n)], 1)
        at += n
    for k, part in enumerate(parts):
        ins[k].wait()
        if part:
            i, r = part
            wides[i][r, :] = lows[i][r, :].astype(f32)
        outs[k].start()
    for c in outs:
        c.wait()


def finish(sm, gd, gu, others, nub, nc=4):
    any_, vm = pl.BlockSpec(memory_space=pl.ANY), pl.BlockSpec(memory_space=pltpu.VMEM)
    sd, v = jax.ShapeDtypeStruct, pltpu.VMEM
    sem = pltpu.SemaphoreType.DMA
    return pl.pallas_call(
        functools.partial(finish_kernel, nc),
        in_specs=[vm] + [any_] * 7, out_specs=[any_] * 7 + [vm] * 6,
        out_shape=[sd(gd.shape, f32), sd(gu.shape, f32)] + [sd(o.shape, o.dtype) for o in others]
        + [sd((1, D), f32)] * 5 + [sd((1, nub), f32)],
        scratch_shapes=[v(gd.shape, bf16), v(gu.shape, bf16), v(gd.shape, f32), v(gu.shape, f32)]
        + [v(o.shape, o.dtype) for o in others] + [sem((2 * nc + 5,)), sem((2 * nc + 5,))],
        compiler_params=pltpu.CompilerParams(vmem_limit_bytes=62 * 2**20),
        name="post",
    )(sm, gd, gu, *others)


def local(sizes, tokens, lengths, routes, route_gates, cotangent, gain_one, shift_one, kv_weight,
          query_weight, out_weight, gain_two, shift_two, up_weight, up_bias, down_weight, down_bias):
    x = tokens[0]
    nexp = query_weight.shape[0]
    row = lambda v: v.reshape(1, -1)
    act, kaug, vaug, kt, vt, qdoc, wq, wo, up, down = head(
        sizes, nexp, x, row(gain_one), row(shift_one), kv_weight, jnp.swapaxes(query_weight, 1, 2), out_weight, lengths[0], up_weight,
        down_weight)
    routes_t = routes[0].T
    gates_t = route_gates[0].T
    cd, q, ctx, lse = attn_fwd(act, wq, routes_t, gates_t, qdoc, kaug, vt, KB=384)
    out, dx, go, gq, gkv, small, gdown, gup = mega(
        sizes, nexp, cd, wo, x, cotangent[0], row(gain_two), row(shift_two), up, row(up_bias), down, row(down_bias), q,
        ctx, lse, routes_t, gates_t, qdoc, kaug, vaug, kt, act, wq, kv_weight, row(gain_one))
    gdown, gup, out, dx, go, gq, gkv, *vecs = finish(small, gdown, gup, (out, dx, go, gq, gkv), up_bias.shape[0])
    go = go.reshape(nexp, HEAD, D)
    gq = jnp.swapaxes(gq.reshape(nexp, HEAD, D), 1, 2)
    gg2, gs2, gdb, gg1, gs1, gub = [v.reshape(-1) for v in vecs]
    return (out[None], dx[None], gg1, gs1, gkv, gq, go, gg2, gs2, gup, gub, gdown, gdb)


def solution(mesh):
    tok3 = P(("dp", "exp"), "ctx", None)
    ex = P("exp", None, None)
    r = P()
    in_specs = (tok3, P(("dp", "exp"), None), tok3, tok3, tok3, r, r, r, ex, ex, r, r, r, r, r, r)
    out_specs = (tok3, tok3, r, r, r, ex, ex, r, r, r, r, r, r)
    fn = functools.partial(local, dict(mesh.shape))
    return jax.shard_map(fn, mesh=mesh, in_specs=in_specs, out_specs=out_specs, check_vma=False)
```

```python
import functools
import math

import jax
import jax.numpy as jnp
from jax import lax
from jax.experimental import pallas as pl
from jax.experimental.pallas import tpu as pltpu
from jax.sharding import PartitionSpec as P

f32 = jnp.float32
bf16 = jnp.bfloat16
D = 512
HEAD = 64
TOP = 8
TB = 128
W = TOP * TB
NEG = -1e30
LOG2E = math.log2(math.e)
LN2 = math.log(2.0)
SMALL = 576
KBB = 384
STRIDE = 8
JOIN = 2
SAFE = 50.0
NN = (((1,), (0,)), ((), ()))
NT = (((1,), (1,)), ((), ()))
TN = (((0,), (0,)), ((), ()))
C0 = math.sqrt(2 / math.pi)
C1 = 0.044715
MESH = pl.DeviceIdType.MESH
AXES = ("dp", "ctx", "exp")


def attn_fwd_kernel(act_ref, wq_ref, routes_ref, gates_ref, qdoc_ref, kaug_ref, vt_ref,
                    cd_ref, q_ref, ctx_ref, lse_ref,
                    qt, qaug, s, acc, kn_ref, *, experts, tok, KB):
    i=pl.program_id(0)
    c=lax.axis_index("ctx")
    @pl.when(i==0)
    def _():
        kk=kaug_ref[...].astype(f32)
        kk=jnp.where(lax.broadcasted_iota(jnp.int32,kk.shape,1)<HEAD,kk*kk,0.0)
        kn_ref[0]=jnp.max(jnp.sum(kk,axis=1,keepdims=True))
    qt[...]=lax.dot_general(wq_ref[...], act_ref[...], NT, preferred_element_type=f32)*(0.125*LOG2E)
    n2=[]
    for k0 in range(0,TOP,4):
        r=[jnp.broadcast_to(routes_ref[k0+k:k0+k+1,:],(8,TB))[None] for k in range(4)]
        sel=[jnp.zeros((HEAD//8,8,TB),f32) for _ in range(4)]
        for e in range(experts):
            v=qt[e*HEAD:(e+1)*HEAD,:].reshape(HEAD//8,8,TB)
            sel=[jnp.where(r[k]==e,v,sel[k]) for k in range(4)]
        for k in range(4):
            sk=sel[k].reshape(HEAD,TB)
            n2.append(jnp.max(jnp.sum(sk*sk,axis=0,keepdims=True)))
            qaug[0:HEAD,(k0+k)*TB:(k0+k+1)*TB]=sk.astype(bf16)
    n2=functools.reduce(jnp.maximum,n2)*kn_ref[0]
    fast=n2<=SAFE*SAFE
    q_ref[0]=qaug[0:HEAD,:]
    qd=qdoc_ref[...]
    qaug[HEAD:HEAD+16,:]=jnp.concatenate([jnp.concatenate([qd,jnp.zeros_like(qd)],0)]*TOP,1).astype(bf16)
    qaug[HEAD+16:,:]=jnp.zeros((128-HEAD-16,W),bf16)
    q0=c*tok+i*TB
    nfull=q0//KB
    kd=pl.multiple_of(nfull*KB,KB)
    kp=lax.broadcasted_iota(jnp.int32,(KB,TB),0)+(kd-q0)
    tp=lax.broadcasted_iota(jnp.int32,(KB,TB),1)
    mask=kp<=tp
    acc[...]=jnp.zeros_like(acc)
    def scores(k0,n):
        return jnp.dot(kaug_ref[pl.ds(k0,n),:],qaug[...],preferred_element_type=f32)
    def masked(x):
        return jnp.concatenate([jnp.where(mask,x[:,k*TB:(k+1)*TB],NEG) for k in range(TOP)],1)
    def pv(k0,n,p):
        acc[...]+=jnp.dot(vt_ref[:,pl.ds(k0,n)],p,preferred_element_type=f32)
    def finish(m):
        l=acc[HEAD:HEAD+1,:]
        lse_ref[0]=m+jnp.log2(l)
        acc[0:HEAD,:]=acc[0:HEAD,:]*(1.0/l)
    @pl.when(fast)
    def _():
        def body(b,_):
            k0=pl.multiple_of(b*KB,KB)
            pv(k0,KB,jnp.exp2(scores(k0,KB)).astype(bf16))
            return 0
        lax.fori_loop(0,nfull,body,0)
        pv(kd,KB,jnp.exp2(masked(scores(kd,KB))).astype(bf16))
        finish(0.0)
    @pl.when(jnp.logical_not(fast))
    def _():
        def spass(b,m):
            k0=pl.multiple_of(b*KB,KB)
            x=scores(k0,KB)
            s[pl.ds(k0,KB),:]=x
            return jnp.maximum(m,jnp.max(x.reshape(KB//8,8,W),axis=0))
        m=lax.fori_loop(0,nfull,spass,jnp.full((8,W),NEG*2,f32))
        x=masked(scores(kd,KB))
        s[pl.ds(kd,KB),:]=x
        m=jnp.maximum(m,jnp.max(x.reshape(KB//8,8,W),axis=0))
        m=jnp.max(m,axis=0,keepdims=True)
        def ppass(b,_):
            k0=pl.multiple_of(b*KB,KB)
            pv(k0,KB,jnp.exp2(s[pl.ds(k0,KB),:]-m).astype(bf16))
            return 0
        lax.fori_loop(0,nfull+1,ppass,0)
        finish(m)
    ctx_ref[0]=acc[0:HEAD,:].astype(bf16)
    for k in range(TOP):
        acc[0:HEAD,k*TB:(k+1)*TB]*=gates_ref[k:k+1,:]
    r=[jnp.broadcast_to(routes_ref[k:k+1,:],(8,TB))[None] for k in range(TOP)]
    for h0 in range(0,HEAD,32):
        g=[acc[h0:h0+32,k*TB:(k+1)*TB].reshape(4,8,TB) for k in range(TOP)]
        for e in range(experts):
            o=jnp.zeros((4,8,TB),f32)
            for k in range(TOP):
                o=jnp.where(r[k]==e,g[k],o)
            cd_ref[e*HEAD+h0:e*HEAD+h0+32,:]=o.reshape(32,TB).astype(bf16)

def attn_fwd(act, wq, routesT, gatesT, qdoc, kaug, vt, KB=256):
    tok=act.shape[0]; experts=wq.shape[0]//HEAD; keys=kaug.shape[0]; n=tok//TB; vr=vt.shape[0]
    full=lambda a: pl.BlockSpec(a.shape,lambda i,*_:(0,)*a.ndim)
    return pl.pallas_call(
        functools.partial(attn_fwd_kernel,experts=experts,tok=tok,KB=KB),
        grid_spec=pltpu.PrefetchScalarGridSpec(num_scalar_prefetch=0,grid=(n,),
          in_specs=[pl.BlockSpec((TB,D),lambda i,*_:(i,0)),full(wq),
            pl.BlockSpec((TOP,TB),lambda i,*_:(0,i)),pl.BlockSpec((TOP,TB),lambda i,*_:(0,i)),
            pl.BlockSpec((8,TB),lambda i,*_:(0,i)),full(kaug),full(vt)],
          out_specs=[pl.BlockSpec((experts*HEAD,TB),lambda i,*_:(0,i)),
            pl.BlockSpec((1,HEAD,W),lambda i,*_:(i,0,0)),
            pl.BlockSpec((1,HEAD,W),lambda i,*_:(i,0,0)),
            pl.BlockSpec((1,1,W),lambda i,*_:(i,0,0))],
          scratch_shapes=[pltpu.VMEM((experts*HEAD,TB),f32),pltpu.VMEM((128,W),bf16),
            pltpu.VMEM((keys,W),f32),pltpu.VMEM((vr,W),f32),pltpu.SMEM((1,),f32)]),
        out_shape=[jax.ShapeDtypeStruct((experts*HEAD,tok),bf16),
          jax.ShapeDtypeStruct((n,HEAD,W),bf16),jax.ShapeDtypeStruct((n,HEAD,W),bf16),
          jax.ShapeDtypeStruct((n,1,W),f32)],
        compiler_params=pltpu.CompilerParams(vmem_limit_bytes=60*2**20),
        name="attn_fwd",
    )(act,wq,routesT,gatesT,qdoc,kaug,vt)


def dot(a, b, dims=NN):
    return lax.dot_general(a, b, dims, preferred_element_type=f32)


def split3(x):
    hi = x.astype(bf16).astype(f32)
    r = x - hi
    mid = r.astype(bf16).astype(f32)
    return hi, mid, r - mid


class Here:
    def __init__(self, sizes):
        self.at = {a: lax.axis_index(a) for a in AXES}
        self.bit = {(ax, m): lax.rem(self.at[ax] // m, 2) for bits in mesh_bits(sizes).values() for ax, m in bits}
        self.known = {}

    def across(self, bits):
        bits = tuple(sorted(bits))
        if bits not in self.known:
            at = dict(self.at)
            for ax, m in bits:
                at[ax] = at[ax] + m - 2 * m * self.bit[ax, m]
            self.known[bits] = tuple(at[a] for a in AXES)
        return self.known[bits]


def subsets(group):
    return [[b for i, b in enumerate(group) if d >> i & 1] for d in range(1, 1 << len(group))]


def mesh_bits(sizes):
    return {a: [(a, 1 << i) for i in range(sizes[a].bit_length() - 1)] for a in AXES}


def small_mesh(sizes):
    return sizes["dp"] == sizes["ctx"] == 2 and sizes["exp"] == 8


def chain_orders(sizes):
    b = mesh_bits(sizes)
    e, d, c = b["exp"], b["dp"], b["ctx"]
    one = lambda bits: [(x,) for x in bits]
    late = one(e + d + c)
    if not small_mesh(sizes):
        return [late] * 3, late
    dense = [one(e[:1] + d + c + e[1:]), one(e[:1] + c + d + e[1:]), late]
    fast = [tuple(e[:1]), tuple(d + c), tuple(e[1:])]
    return dense, fast


def chain_plan(n, order):
    plan = []
    for group in order:
        ways = 1 << len(group)
        halve = n % (16 * ways) == 0
        n = n // ways if halve else n
        plan.append((halve, group, n))
    return plan


def rows(ref, start, n):
    return ref.at[pl.ds(pl.multiple_of(start, 16), n), :]


def add_rows(dst, d0, parts, n):
    ch = math.gcd(n, 64)

    @pl.loop(0, n // ch)
    def _(t):
        o = pl.multiple_of(t * ch, ch)
        g = [r[pl.ds(pl.multiple_of(s + o, 16), ch), :] for r, s in parts]
        total = g[0] + g[1] if len(g) == 2 else functools.reduce(jnp.add, [v.astype(f32) for v in g]).astype(bf16)
        dst[pl.ds(pl.multiple_of(d0 + o, 16), ch), :] = total


def block_places(n, order, owner):
    bits = [bit for halve, group, _ in chain_plan(n, order) if halve for bit in group]
    own = sorted([b for b in bits if b[0] == owner], reverse=True)
    nat = own + sorted([b for b in bits if b[0] != owner])
    places = []
    for i in range(1 << len(nat)):
        v = {b: (i >> (len(nat) - 1 - k)) & 1 for k, b in enumerate(nat)}
        places.append(sum(v[b] << (len(bits) - 1 - k) for k, b in enumerate(bits)))
    return n >> len(nat), places


class Chain:
    def __init__(self, work, final, base, n, order, owner=None, fbase=0):
        self.work, self.final, self.base, self.n, self.order = work, final, base, n, order
        self.owner, self.fbase = owner, fbase
        self.plan = chain_plan(n, order)
        self.landed = sum(m * ((1 << len(g)) - 1) for _, g, m in self.plan)
        self.back = [i for i in reversed(range(len(order))) if self.plan[i][0] and order[i][0][0] != owner]
        if owner:
            self.back.sort(key=lambda i: order[i], reverse=True)
        self.m = len(self.plan)
        self.groups = [g for _, g, _ in self.plan] + [order[i] for i in self.back]
        self.nsem = sum((1 << len(g)) - 1 for g in self.groups)
        self.nsteps = len(self.groups) + 1

    def place(self, here, land, lbase, ss, rs, sem):
        self.here, self.land, self.ss, self.rs = here, land, ss, rs
        self.lb, self.sem = [], []
        for _, g, m in self.plan:
            self.lb.append(lbase)
            lbase += m * ((1 << len(g)) - 1)
        for g in self.groups:
            for f in subsets(g):
                here.across(f)
            self.sem.append(sem)
            sem += (1 << len(g)) - 1
        self.offs, off = [], self.base
        for halve, g, m in self.plan:
            self.offs.append(off)
            if halve:
                off = off + self.index(g, []) * m
        self.last = off

    def index(self, group, flipped):
        v = 0
        for b in group:
            w = self.here.bit[b]
            v = 2 * v + (1 - w if b in flipped else w)
        return v

    def final_range(self, j):
        m = self.plan[-1][2]
        if self.owner is None:
            if j == 0:
                return self.last, m
            i = self.back[j - 1]
            return self.offs[i], self.plan[i][2] << len(self.order[i])
        rest = sorted(b for i in self.back for b in self.order[i])
        done = [b for i in self.back[:j] for b in self.order[i]]
        off = self.fbase
        for k, b in enumerate(rest):
            if b not in done:
                off = off + self.here.bit[b] * (m << (len(rest) - 1 - k))
        return off, m << len(done)

    def copies(self, k):
        out, g = [], self.groups[k]
        for d, flipped in enumerate(subsets(g)):
            if k < self.m:
                halve, _, n = self.plan[k]
                start = self.offs[k] + self.index(g, flipped) * n if halve else self.offs[k]
                src, dst = rows(self.work, start, n), rows(self.land, self.lb[k] + d * n, n)
            else:
                src = dst = rows(self.final, *self.final_range(k - self.m))
            out.append(pltpu.make_async_remote_copy(
                src_ref=src, dst_ref=dst, send_sem=self.ss.at[self.sem[k] + d], recv_sem=self.rs.at[self.sem[k] + d],
                device_id=self.here.across(flipped), device_id_type=MESH))
        return out

    def step(self, k):
        if k:
            for c in self.copies(k - 1):
                c.wait()
            if k <= self.m:
                i = k - 1
                halve, g, n = self.plan[i]
                last = i == self.m - 1
                d = self.offs[i] + self.index(g, []) * n if halve else self.offs[i]
                parts = [(self.work, d)] + [(self.land, self.lb[i] + j * n) for j in range((1 << len(g)) - 1)]
                add_rows(self.final if last else self.work, self.final_range(0)[0] if last else d, parts, n)
        if k < len(self.groups):
            for c in self.copies(k):
                c.start()


def meet(here, groups):
    devices = sorted({tuple(sorted(f)) for g in groups for f in subsets(g)})
    bar = pltpu.get_barrier_semaphore()
    for f in devices:
        pl.semaphore_signal(bar, inc=1, device_id=here.across(f), device_id_type=MESH)
    return lambda: pl.semaphore_wait(bar, len(devices))


def dense_parts(n, orders):
    a = n * 3 // 8 // 32 * 32
    return [(0, a, orders[0]), (a, a, orders[1]), (2 * a, n - 2 * a, orders[2])]


def make_chains(sizes, steps, part, nexp, keys, dsrc, fin, osrc, go, qsrc, gq, ksrc, kfin, ssrc, sfin):
    orders, small = chain_orders(sizes)
    n = sizes["exp"] * HEAD
    kbits = [(b,) for b in mesh_bits(sizes)["ctx"][::-1]]
    part = part * JOIN
    dense = [[Chain(dsrc, fin, j * part + b, m, o) for b, m, o in dense_parts(part, orders)] for j in range(steps // JOIN)]
    return dict(
        dense=dense,
        o=[Chain(osrc, go, j * n, n, orders[j % 3], "exp", j * HEAD) for j in range(nexp)],
        q=[Chain(qsrc, gq, j * n, n, orders[j % 3], "exp", j * HEAD) for j in range(nexp)],
        k=[Chain(ksrc, kfin, 0, keys, kbits, "ctx", 0)],
        g=[Chain(ssrc, sfin, 0, D, small)],
        s=[Chain(ssrc, sfin, D, SMALL - D, small)],
    )


def flat(chains):
    wide = [c for g in chains["dense"] for c in g] + chains["o"] + chains["q"]
    return wide, chains["k"] + chains["g"] + chains["s"]


def place_all(here, chains, land, nland, ss, rs):
    sem = 0
    for group, buf in zip(flat(chains), (land, nland)):
        lb = 0
        for c in group:
            c.place(here, buf, lb, ss, rs, sem)
            lb += c.landed
            sem += c.nsem


def mega_kernel(sizes, nf, nb, nexp, fb,
                cd, wo, tok, cot, g2, s2, up_ref, upb, down_ref, downb, q_ref, ctx_ref, lse_ref, routes_ref, gates_ref,
                qdoc_ref, kaug_ref, vaug_ref, kt_ref, act1, wq, kvw, g1,
                out, dx, go_o, gq_o, gkv_o, sm_o, gd_o, gu_o,
                mid, rstd, act, actT, dffn, dct, dqd, gub, gsm,
                qaug, daug, rhs, pds, dq, dkv,
                dsrc, fin, osrc, go, qsrc, gq, ksrc, kfin, ssrc, sfin, land, nland, ss, rs, lsem):
    s = pl.program_id(0)
    experts = cd.shape[0] // HEAD
    ntok, keys = tok.shape[0], kaug_ref.shape[0]
    part = 2 * fb
    chains = make_chains(sizes, nf, part, nexp, keys, dsrc, fin, osrc, go, qsrc, gq, ksrc, kfin, ssrc, sfin)
    here = Here(sizes)
    place_all(here, chains, land, nland, ss, rs)
    ticks = [(j, p) for j in range(nf) for p in range(3)] + [(nf + i, p) for i in range(nb) for p in range(4)]
    ticks += [(nf + nb, p) for p in range(4)]
    table, late = {}, []
    for j, group in enumerate(chains["dense"] + [chains["o"]]):
        t0 = ticks.index((j * JOIN + JOIN - 1, 2)) if j < nf // JOIN else ticks.index((nf, 0))
        for k in range(max(c.nsteps for c in group)):
            todo = [(c, k) for c in group if k < c.nsteps]
            at = t0 + (1 + STRIDE * (k - 1) // 2 if k else 0)
            if at < len(ticks):
                table.setdefault(ticks[at], []).extend(todo)
            else:
                late.extend(todo)

    def tick(step, pos):
        for at, todo in table.items():
            if at[1] != pos or step != ("f" if at[0] < nf else "b" if at[0] < nf + nb else "t"):
                continue
            if step == "t":
                for c, k in todo:
                    c.step(k)
                continue

            @pl.when(s == at[0])
            def _():
                for c, k in todo:
                    c.step(k)

    def put_owner(src_rows, value, e, order_of):
        for j in range(nexp):
            c = order_of[j]
            block, places = block_places(c.n, c.order, "exp")
            per = HEAD // block
            for b in range(per):
                at = c.base + places[e * per + b] * block
                src_rows[at:at + block, :] = value[j * HEAD + b * block:j * HEAD + (b + 1) * block, :]

    @pl.when(s == 0)
    def _():
        met = meet(here, [g for group in flat(chains) for c in group for g in c.groups])
        m = tok[...] + dot(cd[...], wo[...], TN)
        mid[...] = m
        cen = m - jnp.mean(m, axis=-1, keepdims=True)
        r = lax.rsqrt(jnp.mean(cen * cen, axis=-1, keepdims=True) + 1e-5)
        xh = cen * r
        rstd[...] = jnp.broadcast_to(r, rstd.shape)
        a = xh * g2[...] + s2[...]
        act[...] = a.astype(bf16)
        actT[...] = jnp.transpose(a).astype(bf16)
        dffn[...] = cot[...].astype(bf16)
        out[...] = m + downb[...]
        dx[...] = jnp.zeros_like(dx)
        met()

    @pl.when(s < nf)
    def _():
        up, down = up_ref[...], down_ref[...]
        pre = dot(act[...], up) + upb[...]
        x2 = pre * pre
        th = jnp.tanh(pre * (C0 + C0 * C1 * x2))
        h = 0.5 * (1.0 + th)
        hid = (pre * h).astype(bf16)
        gp = h + (0.5 * pre) * (1.0 - th * th) * (C0 + 3.0 * C0 * C1 * x2)
        out[...] += dot(hid, down)
        tick("f", 0)
        r0 = pl.multiple_of(s * part, part)
        dsrc[pl.ds(r0, fb), :] = dot(hid, dffn[...], TN).astype(bf16)
        tick("f", 1)
        dpb = (dot(dffn[...], down, NT) * gp).astype(bf16)
        gub[pl.ds(s, 1), :] = jnp.sum(dpb.astype(f32), axis=0, keepdims=True)
        dsrc[pl.ds(pl.multiple_of(r0 + fb, fb), fb), :] = dot(actT[...], dpb).astype(bf16)
        dx[...] += dot(dpb, up, NT)
        tick("f", 2)

    @pl.when(s == nf - 1)
    def _():
        d = dx[...]
        m = mid[...]
        xh = (m - jnp.mean(m, axis=-1, keepdims=True)) * rstd[:, 0:1]
        gx = d * g2[...]
        dm = cot[...] + rstd[:, 0:1] * (gx - jnp.mean(gx, axis=-1, keepdims=True)
                                        - xh * jnp.mean(gx * xh, axis=-1, keepdims=True))
        mid[...] = dm
        gsm[...] = jnp.concatenate([jnp.sum(d * xh, axis=0, keepdims=True), jnp.sum(d, axis=0, keepdims=True),
                                    jnp.sum(dffn[...].astype(f32), axis=0, keepdims=True)], axis=0)
        dmb = dm.astype(bf16)
        act[...] = dmb
        dct[...] = dot(wo[...], dmb, NT).astype(bf16)
        w = nexp * HEAD
        for e in range(sizes["exp"]):
            put_owner(osrc, dot(cd[e * w:(e + 1) * w, :], dmb).astype(bf16), e, chains["o"])

    @pl.when(s == nf)
    def _():
        dkv[...] = jnp.zeros_like(dkv)
        rhs[...] = jnp.zeros_like(rhs)

    @pl.when((s >= nf) & (s < nf + nb))
    def _():
        i = s - nf
        lanes = pl.ds(pl.multiple_of(i * TB, TB), TB)
        q = q_ref[0]
        qaug[0:HEAD, :] = q
        rhs[0:HEAD, 0:W] = q
        hi, md, lo = split3(-lse_ref[0])
        qd = qdoc_ref[...]
        qaug[HEAD:HEAD + 16, :] = jnp.concatenate(
            [jnp.concatenate([qd[0:3, :]] * TOP, 1), hi, md, lo, jnp.zeros((10, W), f32)], 0).astype(bf16)
        qaug[HEAD + 16:, :] = jnp.zeros((128 - HEAD - 16, W), bf16)
        r = [jnp.broadcast_to(routes_ref[k:k + 1, :], (8, TB))[None] for k in range(TOP)]
        for k0 in range(0, TOP, 4):
            sel = [jnp.zeros((HEAD // 8, 8, TB), f32) for _ in range(4)]
            for e in range(experts):
                v = dct[e * HEAD:(e + 1) * HEAD, lanes].astype(f32).reshape(HEAD // 8, 8, TB)
                sel = [jnp.where(r[k0 + k] == e, v, sel[k]) for k in range(4)]
            for k in range(4):
                sl = slice((k0 + k) * TB, (k0 + k + 1) * TB)
                dc = (sel[k].reshape(HEAD, TB) * gates_ref[k0 + k:k0 + k + 1, :]).astype(bf16)
                daug[0:HEAD, sl] = dc
                rhs[HEAD:, W + (k0 + k) * TB:W + (k0 + k + 1) * TB] = dc
                dq[0:1, sl] = jnp.sum(dc.astype(f32) * ctx_ref[0, :, sl].astype(f32), axis=0, keepdims=True)
        hi, md, lo = split3(-dq[0:1, :])
        daug[HEAD:HEAD + 16, :] = jnp.concatenate([hi, md, lo, jnp.zeros((13, W), f32)], 0).astype(bf16)
        daug[HEAD + 16:, :] = jnp.zeros((128 - HEAD - 16, W), bf16)
        dq[...] = jnp.zeros_like(dq)
        q0 = lax.axis_index("ctx") * ntok + i * TB
        nfull = q0 // KBB
        kd = pl.multiple_of(nfull * KBB, KBB)

        def block(k0, mask):
            p = jnp.exp2(dot(kaug_ref[pl.ds(k0, KBB), :], qaug[...]))
            if mask is not None:
                p = jnp.concatenate([jnp.where(mask, p[:, k * TB:(k + 1) * TB], 0.0) for k in range(TOP)], 1)
            dp = dot(vaug_ref[pl.ds(k0, KBB), :], daug[...])
            pds[:, W:] = p.astype(bf16)
            pds[:, :W] = (p * dp).astype(bf16)
            dq[...] += dot(kt_ref[:, pl.ds(k0, KBB)], pds[:, :W])
            dkv[pl.ds(k0, KBB), :] += dot(pds[...], rhs[...], NT)

        def body(b, _):
            block(pl.multiple_of(b * KBB, KBB), None)
            return 0

        tick("b", 0)
        lax.fori_loop(0, nfull, body, 0)
        tick("b", 1)
        kp = lax.broadcasted_iota(jnp.int32, (KBB, TB), 0) + (kd - q0)
        tp = lax.broadcasted_iota(jnp.int32, (KBB, TB), 1)
        block(kd, kp <= tp)
        tick("b", 2)
        dq[...] *= 0.125
        for h0 in range(0, HEAD, 32):
            g = [dq[h0:h0 + 32, k * TB:(k + 1) * TB].reshape(4, 8, TB) for k in range(TOP)]
            for e in range(experts):
                o = jnp.zeros((4, 8, TB), f32)
                for k in range(TOP):
                    o = jnp.where(r[k] == e, g[k], o)
                dqd[e * HEAD + h0:e * HEAD + h0 + 32, lanes] = o.reshape(32, TB).astype(bf16)
        tick("b", 3)

    @pl.when(s == nf + nb)
    def _():
        lane = lax.broadcasted_iota(jnp.int32, (1, 128), 1)
        ksrc[...] = (dkv[...] * jnp.where(lane < HEAD, LN2, 1.0)).astype(bf16)
        kc, gc, sc = chains["k"][0], chains["g"][0], chains["s"][0]
        kc.step(0)
        tick("t", 0)
        w = nexp * HEAD
        for e in range(sizes["exp"]):
            put_owner(qsrc, dot(dqd[e * w:(e + 1) * w, :], act1[...]).astype(bf16), e, chains["q"])
        for c in chains["q"]:
            c.step(0)
        for k in range(1, kc.nsteps):
            kc.step(k)
        ssrc[0:D, :] = dot(act1[...], kfin[...], TN).astype(bf16)
        gc.step(0)
        tick("t", 1)
        for c in chains["q"]:
            c.step(1)
        da = dot(dqd[...], wq[...], TN) + dot(kfin[...], kvw[...].astype(bf16), NT)
        gc.step(1)
        tick("t", 2)
        x = tok[...]
        cen = x - jnp.mean(x, axis=-1, keepdims=True)
        r1 = lax.rsqrt(jnp.mean(cen * cen, axis=-1, keepdims=True) + 1e-5)
        xh = cen * r1
        gg1, gs1 = jnp.sum(da * xh, axis=0, keepdims=True), jnp.sum(da, axis=0, keepdims=True)
        vecs = [gsm[0:1, :], gsm[1:2, :], gsm[2:3, :], gg1, gs1] + [gub[j:j + 1, :] for j in range(nf)]
        vecs = [v[:, o:o + 128] for v in vecs for o in range(0, v.shape[1], 128)]
        vecs.append(jnp.zeros((SMALL - D - len(vecs), 128), f32))
        ssrc[D:SMALL, :] = jnp.concatenate(vecs, 0).astype(bf16)
        sc.step(0)
        for c in chains["q"]:
            c.step(2)
        gc.step(2)
        gx = da * g1[...]
        dx[...] = mid[...] + r1 * (gx - jnp.mean(gx, axis=-1, keepdims=True)
                                   - xh * jnp.mean(gx * xh, axis=-1, keepdims=True))
        tick("t", 3)
        rounds = max(c.nsteps for c in (gc, sc, *chains["q"]))
        for k in range(1, rounds):
            for c, lag in [(c, 2) for c in chains["q"]] + [(gc, 2), (sc, 0)]:
                if k + lag < c.nsteps:
                    c.step(k + lag)
            share = -(-len(late) // 3)
            for c, n in late[(k - 1) * share:k * share]:
                c.step(n)
            if k == 3:
                moved = []
                for j in range(nf):
                    r0 = j * part
                    moved.append(pltpu.make_async_copy(
                        fin.at[r0:r0 + fb, :], gd_o.at[j * fb:(j + 1) * fb, :], lsem.at[2 * j]))
                    moved.append(pltpu.make_async_copy(
                        fin.at[r0 + fb:r0 + part, :], gu_o.at[:, j * fb:(j + 1) * fb], lsem.at[2 * j + 1]))
                for c in moved:
                    c.start()
        go_o[...] = go[...].astype(f32)
        gq_o[...] = gq[...].astype(f32)
        gkv_o[...] = sfin[0:D, :].astype(f32)
        sm_o[...] = sfin[D:SMALL, :].astype(f32)
        for c in moved:
            c.wait()


def mega(sizes, nexp, cd, wo, tok, cot, g2, s2, up, upb, down, downb, q, ctx, lse, routes, gates, qdoc, kaug, vaug, kt,
         act1, wq, kvw, g1, fb=512):
    ntok, keys, ff, eh = tok.shape[0], kaug.shape[0], up.shape[1], wo.shape[0]
    nf, nb = ff // fb, ntok // TB
    part = 2 * fb
    sd = jax.ShapeDtypeStruct
    z = [None] * 10
    chains = make_chains(sizes, nf, part, nexp, keys, *z)
    wide, narrow = flat(chains)
    land, nland = sum(c.landed for c in wide), sum(c.landed for c in narrow)
    nsem = sum(c.nsem for c in wide + narrow)
    once = pl.Buffered(1)
    full = lambda a: pl.BlockSpec(a.shape, lambda s: (0,) * a.ndim, pipeline_mode=once)
    fo = lambda *sh: pl.BlockSpec(sh, lambda s: (0,) * len(sh), pipeline_mode=once)
    fj = lambda s: jnp.minimum(s, nf - 1)
    bi = lambda s: jnp.clip(s - nf, 0, nb - 1)
    blk = lambda r: pl.BlockSpec((r, TB), lambda s: (0, bi(s)))
    b3 = lambda a: pl.BlockSpec((1,) + a.shape[1:], lambda s: (bi(s), 0, 0))
    any_ = pl.BlockSpec(memory_space=pl.ANY)
    v = pltpu.VMEM
    return pl.pallas_call(
        functools.partial(mega_kernel, sizes, nf, nb, nexp, fb),
        grid=(nf + nb + 1,),
        in_specs=[full(cd), full(wo), full(tok), full(cot), full(g2), full(s2),
                  pl.BlockSpec((D, fb), lambda s: (0, fj(s))), pl.BlockSpec((1, fb), lambda s: (0, fj(s))),
                  pl.BlockSpec((fb, D), lambda s: (fj(s), 0)), full(downb), b3(q), b3(ctx), b3(lse),
                  blk(TOP), blk(TOP), blk(8), full(kaug), full(vaug), full(kt), full(act1), full(wq), full(kvw), full(g1)],
        out_specs=[fo(ntok, D), fo(ntok, D), fo(nexp * HEAD, D), fo(nexp * HEAD, D), fo(D, 128), fo(SMALL - D, 128), any_, any_],
        out_shape=[sd((ntok, D), f32), sd((ntok, D), f32), sd((nexp * HEAD, D), f32), sd((nexp * HEAD, D), f32),
                   sd((D, 128), f32), sd((SMALL - D, 128), f32), sd((ff, D), bf16), sd((D, ff), bf16)],
        scratch_shapes=[
            v((ntok, D), f32), v((ntok, 128), f32), v((ntok, D), bf16), v((D, ntok), bf16),
            v((ntok, D), bf16), v((eh, ntok), bf16), v((eh, ntok), bf16), v((nf, fb), f32), v((3, D), f32),
            v((128, W), bf16), v((128, W), bf16), v((128, 2 * W), bf16), v((KBB, 2 * W), bf16), v((HEAD, W), f32),
            v((keys, 128), f32),
            v((nf * part, D), bf16), v((nf * part, D), bf16), v((eh, D), bf16), v((nexp * HEAD, D), bf16),
            v((eh, D), bf16), v((nexp * HEAD, D), bf16), v((keys, 128), bf16), v((ntok, 128), bf16),
            v((SMALL, 128), bf16), v((SMALL, 128), bf16), v((land, D), bf16), v((nland, 128), bf16),
            pltpu.SemaphoreType.DMA((nsem,)), pltpu.SemaphoreType.DMA((nsem,)), pltpu.SemaphoreType.DMA((2 * nf,))],
        compiler_params=pltpu.CompilerParams(collective_id=0, has_side_effects=True, vmem_limit_bytes=62 * 2**20),
        name="mega",
    )(cd, wo, tok, cot, g2, s2, up, upb, down, downb, q, ctx, lse, routes, gates, qdoc, kaug, vaug, kt, act1, wq, kvw, g1)


def gather_stages(sizes, here, shard):
    e = lax.axis_index("exp")
    if not small_mesh(sizes) or shard % 64:
        stages = []
        for i, bit in enumerate(mesh_bits(sizes)["exp"]):
            stages.append([((e >> i << i) * shard, shard << i, [bit])])
        return stages, []
    core, zl, zh, x, y = ("exp", 1), ("exp", 2), ("exp", 4), ("dp", 1), ("ctx", 1)
    quarter = shard // 4
    flip = lambda bit, n: n * (1 - 2 * here.bit[bit])
    at = lambda dz: e + (dz & 1) * flip(zl, 2) + (dz >> 1) * flip(zh, 4)
    row = lambda dz: at(dz) * shard + (here.bit[x] * 2 + here.bit[y]) * quarter
    stages = [
        [(row(0), quarter, f) for f in subsets((zl, zh))],
        [(row(d), quarter, f) for d in (1, 2, 3) for f in subsets((x, y))],
        [(at(d) * shard, shard, [core]) for d in (1, 2, 3)],
    ]
    return stages, [(e * shard, shard, [core])]


def head_kernel(sizes, nexp, nsem, tok, g1, s1, kvw, wq3, wo3, lens, up_h, down_h,
                act, kaug, vaug, kt, vt, qdoc, wq_o, wo_o, up_o, down_o,
                wqs, wos, kv, upf, downf, upb, downb, ss, rs, ls):
    here = Here(sizes)
    ntok, keys, shard = tok.shape[0], kv.shape[0], nexp * HEAD
    fetch = [pltpu.make_async_copy(up_h, upf, ls.at[0]), pltpu.make_async_copy(down_h, downf, ls.at[1])]
    for c in fetch:
        c.start()
    b = mesh_bits(sizes)
    exact = [tuple(b["exp"][1:]), tuple(b["dp"] + b["ctx"])] if small_mesh(sizes) else []
    met = meet(here, [(x,) for a in AXES for x in b[a]] + exact)
    mine = lax.axis_index("exp") * shard
    for j in range(nexp):
        r = pl.ds(pl.multiple_of(mine + j * HEAD, HEAD), HEAD)
        wqs[r, :] = wq3[j].astype(bf16)
        wos[r, :] = wo3[j].astype(bf16)
    met()
    count = [0]

    def send(buf, moves):
        out = []
        for start, n, bits in moves:
            r = rows(buf, start, n)
            k = count[0]
            count[0] += 1
            c = pltpu.make_async_remote_copy(src_ref=r, dst_ref=r, send_sem=ss.at[k], recv_sem=rs.at[k],
                                             device_id=here.across(bits), device_id_type=MESH)
            c.start()
            out.append(c)
        return out

    def wait(copies):
        for c in copies:
            c.wait()

    stages, early = gather_stages(sizes, here, shard)
    work = []

    def run(k):
        for buf, lag in ((wqs, 0), (wos, 1)):
            i = k - lag
            if 0 < i <= len(stages):
                wait(flying[buf is wos])
            if 0 <= i < len(stages):
                flying[buf is wos] = send(buf, stages[i])

    flying = [[], []]
    run(0)
    own = send(wqs, early) + send(wos, early)
    x = tok[...]
    cen = x - jnp.mean(x, axis=-1, keepdims=True)
    a = (cen * lax.rsqrt(jnp.mean(cen * cen, axis=-1, keepdims=True) + 1e-5) * g1[...] + s1[...]).astype(bf16)
    act[...] = a
    ctx = lax.axis_index("ctx")
    kv[pl.ds(pl.multiple_of(ctx * ntok, ntok), ntok), :] = dot(a, kvw[...].astype(bf16)).astype(bf16)
    cbits = mesh_bits(sizes)["ctx"]
    share = lambda i: send(kv, [((ctx >> i << i) * ntok, ntok << i, [cbits[i]])])
    swap = share(0)
    run(1)
    put = []

    def cast(k, src, dst, o):
        fetch[k].wait()

        @pl.loop(0, src.shape[0] // 64)
        def _(t):
            r = pl.ds(pl.multiple_of(t * 64, 64), 64)
            dst[r, :] = src[r, :].astype(bf16)

        c = pltpu.make_async_copy(dst, o, ls.at[2 + k])
        c.start()
        put.append(c)

    def ends(pos):
        d, end = jnp.zeros(pos.shape, jnp.int32), 0
        for j in range(lens.shape[0] - 1):
            end = end + lens[j]
            d = d + (pos >= end).astype(jnp.int32)
        return d

    cast(0, upf, upb, up_o)
    slot = lax.broadcasted_iota(jnp.int32, (8, ntok), 0)
    qpos = ends(lax.broadcasted_iota(jnp.int32, (8, ntok), 1) + ctx * ntok)
    qdoc[...] = jnp.where((qpos == slot) | (slot > 2), 0.0, NEG)
    run(2)
    wait(swap)
    for i in range(1, len(cbits)):
        wait(share(i))
    cast(1, downf, downb, down_o)
    run(3)
    lane = lax.broadcasted_iota(jnp.int32, (keys, 128), 1)
    doc = ends(lax.broadcasted_iota(jnp.int32, (keys, 128), 0))
    full = kv[...].astype(f32)
    extra = jnp.where((lane == doc + HEAD) | ((lane > HEAD + 2) & (lane < HEAD + 6)), 1.0, 0.0)
    kaug[...] = jnp.where(lane < HEAD, full, extra).astype(bf16)
    flipped = jnp.concatenate([full[:, HEAD:], full[:, :HEAD]], axis=1)
    vaug[...] = jnp.where(lane < HEAD, flipped, jnp.where(lane < HEAD + 3, 1.0, 0.0)).astype(bf16)
    both = jnp.transpose(full)
    kt[...] = both[:HEAD].astype(bf16)
    vt[...] = jnp.concatenate([both[HEAD:], jnp.ones((1, keys), f32), jnp.zeros((15, keys), f32)], 0).astype(bf16)
    run(4)
    for k in range(5, len(stages) + 2):
        run(k)
    wait(own)
    for k, (src, o) in enumerate(((wqs, wq_o), (wos, wo_o))):
        c = pltpu.make_async_copy(src, o, ls.at[4 + k])
        c.start()
        put.append(c)
    for c in put:
        c.wait()


def head(sizes, nexp, tok, g1, s1, kvw, wq3, wo3, lens, up, down):
    ntok, keys, experts = tok.shape[0], tok.shape[0] * sizes["ctx"], nexp * sizes["exp"]
    vm, any_ = pl.BlockSpec(memory_space=pltpu.VMEM), pl.BlockSpec(memory_space=pl.ANY)
    sd, v = jax.ShapeDtypeStruct, pltpu.VMEM
    nsem = 64
    wide = (experts * HEAD, D)
    return pl.pallas_call(
        functools.partial(head_kernel, sizes, nexp, nsem),
        in_specs=[vm] * 6 + [pl.BlockSpec(memory_space=pltpu.SMEM), any_, any_],
        out_specs=[vm] * 6 + [any_] * 4,
        out_shape=[sd((ntok, D), bf16), sd((keys, 128), bf16), sd((keys, 128), bf16), sd((HEAD, keys), bf16),
                   sd((HEAD + 16, keys), bf16), sd((8, ntok), f32), sd(wide, bf16), sd(wide, bf16),
                   sd(up.shape, bf16), sd(down.shape, bf16)],
        scratch_shapes=[v(wide, bf16), v(wide, bf16), v((keys, 128), bf16), v(up.shape, f32), v(down.shape, f32),
                        v(up.shape, bf16), v(down.shape, bf16), pltpu.SemaphoreType.DMA((nsem,)),
                        pltpu.SemaphoreType.DMA((nsem,)), pltpu.SemaphoreType.DMA((6,))],
        compiler_params=pltpu.CompilerParams(collective_id=1, has_side_effects=True, vmem_limit_bytes=60 * 2**20),
        name="head",
    )(tok, g1, s1, kvw, wq3, wo3, lens, up, down)


def finish_kernel(nc, sm, gd, gu, *refs):
    moves, wide_o, moved, vec_o = refs[:5], refs[5:7], refs[7:12], refs[12:18]
    lows, wides, vias, si, so = refs[18:20], refs[20:22], refs[22:27], refs[27], refs[28]
    ins, outs, parts = [], [], []
    for i, src in enumerate((gd, gu)):
        n = src.shape[0] // nc
        for j in range(nc):
            r = slice(j * n, (j + 1) * n)
            ins.append(pltpu.make_async_copy(src.at[r, :], lows[i].at[r, :], si.at[i * nc + j]))
            outs.append(pltpu.make_async_copy(wides[i].at[r, :], wide_o[i].at[r, :], so.at[i * nc + j]))
            parts.append((i, r))
    for k, (a, via, b) in enumerate(zip(moves, vias, moved)):
        ins.append(pltpu.make_async_copy(a, via, si.at[2 * nc + k]))
        outs.append(pltpu.make_async_copy(via, b, so.at[2 * nc + k]))
        parts.append(None)
    for c in ins:
        c.start()
    at = 0
    for o in vec_o:
        n = o.shape[1] // 128
        o[...] = jnp.concatenate([sm[j:j + 1, :] for j in range(at, at + n)], 1)
        at += n
    for k, part in enumerate(parts):
        ins[k].wait()
        if part:
            i, r = part
            wides[i][r, :] = lows[i][r, :].astype(f32)
        outs[k].start()
    for c in outs:
        c.wait()


def finish(sm, gd, gu, others, nub, nc=4):
    any_, vm = pl.BlockSpec(memory_space=pl.ANY), pl.BlockSpec(memory_space=pltpu.VMEM)
    sd, v = jax.ShapeDtypeStruct, pltpu.VMEM
    sem = pltpu.SemaphoreType.DMA
    return pl.pallas_call(
        functools.partial(finish_kernel, nc),
        in_specs=[vm] + [any_] * 7, out_specs=[any_] * 7 + [vm] * 6,
        out_shape=[sd(gd.shape, f32), sd(gu.shape, f32)] + [sd(o.shape, o.dtype) for o in others]
        + [sd((1, D), f32)] * 5 + [sd((1, nub), f32)],
        scratch_shapes=[v(gd.shape, bf16), v(gu.shape, bf16), v(gd.shape, f32), v(gu.shape, f32)]
        + [v(o.shape, o.dtype) for o in others] + [sem((2 * nc + 5,)), sem((2 * nc + 5,))],
        compiler_params=pltpu.CompilerParams(vmem_limit_bytes=62 * 2**20),
        name="post",
    )(sm, gd, gu, *others)


def local(sizes, tokens, lengths, routes, route_gates, cotangent, gain_one, shift_one, kv_weight,
          query_weight, out_weight, gain_two, shift_two, up_weight, up_bias, down_weight, down_bias):
    x = tokens[0]
    nexp = query_weight.shape[0]
    row = lambda v: v.reshape(1, -1)
    act, kaug, vaug, kt, vt, qdoc, wq, wo, up, down = head(
        sizes, nexp, x, row(gain_one), row(shift_one), kv_weight, jnp.swapaxes(query_weight, 1, 2), out_weight, lengths[0], up_weight,
        down_weight)
    routes_t = routes[0].T
    gates_t = route_gates[0].T
    cd, q, ctx, lse = attn_fwd(act, wq, routes_t, gates_t, qdoc, kaug, vt, KB=768)
    out, dx, go, gq, gkv, small, gdown, gup = mega(
        sizes, nexp, cd, wo, x, cotangent[0], row(gain_two), row(shift_two), up, row(up_bias), down, row(down_bias), q,
        ctx, lse, routes_t, gates_t, qdoc, kaug, vaug, kt, act, wq, kv_weight, row(gain_one))
    gdown, gup, out, dx, go, gq, gkv, *vecs = finish(small, gdown, gup, (out, dx, go, gq, gkv), up_bias.shape[0])
    go = go.reshape(nexp, HEAD, D)
    gq = jnp.swapaxes(gq.reshape(nexp, HEAD, D), 1, 2)
    gg2, gs2, gdb, gg1, gs1, gub = [v.reshape(-1) for v in vecs]
    return (out[None], dx[None], gg1, gs1, gkv, gq, go, gg2, gs2, gup, gub, gdown, gdb)


def solution(mesh):
    tok3 = P(("dp", "exp"), "ctx", None)
    ex = P("exp", None, None)
    r = P()
    in_specs = (tok3, P(("dp", "exp"), None), tok3, tok3, tok3, r, r, r, ex, ex, r, r, r, r, r, r)
    out_specs = (tok3, tok3, r, r, r, ex, ex, r, r, r, r, r, r)
    fn = functools.partial(local, dict(mesh.shape))
    return jax.shard_map(fn, mesh=mesh, in_specs=in_specs, out_specs=out_specs, check_vma=False)
```

```python
import functools
import math

import jax
import jax.numpy as jnp
from jax import lax
from jax.experimental import pallas as pl
from jax.experimental.pallas import tpu as pltpu
from jax.sharding import PartitionSpec as P

f32 = jnp.float32
bf16 = jnp.bfloat16
D = 512
HEAD = 64
TOP = 8
TB = 128
W = TOP * TB
NEG = -1e30
LOG2E = math.log2(math.e)
LN2 = math.log(2.0)
SMALL = 576
KBB = 384
STRIDE = 8
JOIN = 2
SAFE = 50.0
NN = (((1,), (0,)), ((), ()))
NT = (((1,), (1,)), ((), ()))
TN = (((0,), (0,)), ((), ()))
C0 = math.sqrt(2 / math.pi)
C1 = 0.044715
MESH = pl.DeviceIdType.MESH
AXES = ("dp", "ctx", "exp")


def attn_fwd_kernel(act_ref, wq_ref, routes_ref, gates_ref, qdoc_ref, kaug_ref, vt_ref,
                    cd_ref, q_ref, ctx_ref, lse_ref,
                    qt, qaug, s, acc, kn_ref, *, experts, tok, KB):
    i=pl.program_id(0)
    c=lax.axis_index("ctx")
    @pl.when(i==0)
    def _():
        kk=kaug_ref[...].astype(f32)
        kk=jnp.where(lax.broadcasted_iota(jnp.int32,kk.shape,1)<HEAD,kk*kk,0.0)
        kn_ref[0]=jnp.max(jnp.sum(kk,axis=1,keepdims=True))
    qt[...]=lax.dot_general(wq_ref[...], act_ref[...], NT, preferred_element_type=f32)*(0.125*LOG2E)
    n2=[]
    for k0 in range(0,TOP,4):
        r=[jnp.broadcast_to(routes_ref[k0+k:k0+k+1,:],(8,TB))[None] for k in range(4)]
        sel=[jnp.zeros((HEAD//8,8,TB),f32) for _ in range(4)]
        for e in range(experts):
            v=qt[e*HEAD:(e+1)*HEAD,:].reshape(HEAD//8,8,TB)
            sel=[jnp.where(r[k]==e,v,sel[k]) for k in range(4)]
        for k in range(4):
            sk=sel[k].reshape(HEAD,TB)
            n2.append(jnp.max(jnp.sum(sk*sk,axis=0,keepdims=True)))
            qaug[0:HEAD,(k0+k)*TB:(k0+k+1)*TB]=sk.astype(bf16)
    n2=functools.reduce(jnp.maximum,n2)*kn_ref[0]
    fast=n2<=SAFE*SAFE
    q_ref[0]=qaug[0:HEAD,:]
    qd=qdoc_ref[...]
    qaug[HEAD:HEAD+16,:]=jnp.concatenate([jnp.concatenate([qd,jnp.zeros_like(qd)],0)]*TOP,1).astype(bf16)
    qaug[HEAD+16:,:]=jnp.zeros((128-HEAD-16,W),bf16)
    q0=c*tok+i*TB
    nfull=q0//KB
    kd=pl.multiple_of(nfull*KB,KB)
    kp=lax.broadcasted_iota(jnp.int32,(KB,TB),0)+(kd-q0)
    tp=lax.broadcasted_iota(jnp.int32,(KB,TB),1)
    mask=kp<=tp
    acc[...]=jnp.zeros_like(acc)
    def scores(k0,n):
        return jnp.dot(kaug_ref[pl.ds(k0,n),:],qaug[...],preferred_element_type=f32)
    def masked(x):
        return jnp.concatenate([jnp.where(mask,x[:,k*TB:(k+1)*TB],NEG) for k in range(TOP)],1)
    def pv(k0,n,p):
        acc[...]+=jnp.dot(vt_ref[:,pl.ds(k0,n)],p,preferred_element_type=f32)
    def finish(m):
        l=acc[HEAD:HEAD+1,:]
        lse_ref[0]=m+jnp.log2(l)
        acc[0:HEAD,:]=acc[0:HEAD,:]*(1.0/l)
    @pl.when(fast)
    def _():
        def body(b,_):
            k0=pl.multiple_of(b*KB,KB)
            pv(k0,KB,jnp.exp2(scores(k0,KB)).astype(bf16))
            return 0
        lax.fori_loop(0,nfull,body,0)
        pv(kd,KB,jnp.exp2(masked(scores(kd,KB))).astype(bf16))
        finish(0.0)
    @pl.when(jnp.logical_not(fast))
    def _():
        def spass(b,m):
            k0=pl.multiple_of(b*KB,KB)
            x=scores(k0,KB)
            s[pl.ds(k0,KB),:]=x
            return jnp.maximum(m,jnp.max(x.reshape(KB//8,8,W),axis=0))
        m=lax.fori_loop(0,nfull,spass,jnp.full((8,W),NEG*2,f32))
        x=masked(scores(kd,KB))
        s[pl.ds(kd,KB),:]=x
        m=jnp.maximum(m,jnp.max(x.reshape(KB//8,8,W),axis=0))
        m=jnp.max(m,axis=0,keepdims=True)
        def ppass(b,_):
            k0=pl.multiple_of(b*KB,KB)
            pv(k0,KB,jnp.exp2(s[pl.ds(k0,KB),:]-m).astype(bf16))
            return 0
        lax.fori_loop(0,nfull+1,ppass,0)
        finish(m)
    ctx_ref[0]=acc[0:HEAD,:].astype(bf16)
    for k in range(TOP):
        acc[0:HEAD,k*TB:(k+1)*TB]*=gates_ref[k:k+1,:]
    r=[jnp.broadcast_to(routes_ref[k:k+1,:],(8,TB))[None] for k in range(TOP)]
    for h0 in range(0,HEAD,32):
        g=[acc[h0:h0+32,k*TB:(k+1)*TB].reshape(4,8,TB) for k in range(TOP)]
        for e in range(experts):
            o=jnp.zeros((4,8,TB),f32)
            for k in range(TOP):
                o=jnp.where(r[k]==e,g[k],o)
            cd_ref[e*HEAD+h0:e*HEAD+h0+32,:]=o.reshape(32,TB).astype(bf16)

def attn_fwd(act, wq, routesT, gatesT, qdoc, kaug, vt, KB=256):
    tok=act.shape[0]; experts=wq.shape[0]//HEAD; keys=kaug.shape[0]; n=tok//TB; vr=vt.shape[0]
    full=lambda a: pl.BlockSpec(a.shape,lambda i,*_:(0,)*a.ndim)
    return pl.pallas_call(
        functools.partial(attn_fwd_kernel,experts=experts,tok=tok,KB=KB),
        grid_spec=pltpu.PrefetchScalarGridSpec(num_scalar_prefetch=0,grid=(n,),
          in_specs=[pl.BlockSpec((TB,D),lambda i,*_:(i,0)),full(wq),
            pl.BlockSpec((TOP,TB),lambda i,*_:(0,i)),pl.BlockSpec((TOP,TB),lambda i,*_:(0,i)),
            pl.BlockSpec((8,TB),lambda i,*_:(0,i)),full(kaug),full(vt)],
          out_specs=[pl.BlockSpec((experts*HEAD,TB),lambda i,*_:(0,i)),
            pl.BlockSpec((1,HEAD,W),lambda i,*_:(i,0,0)),
            pl.BlockSpec((1,HEAD,W),lambda i,*_:(i,0,0)),
            pl.BlockSpec((1,1,W),lambda i,*_:(i,0,0))],
          scratch_shapes=[pltpu.VMEM((experts*HEAD,TB),f32),pltpu.VMEM((128,W),bf16),
            pltpu.VMEM((keys,W),f32),pltpu.VMEM((vr,W),f32),pltpu.SMEM((1,),f32)]),
        out_shape=[jax.ShapeDtypeStruct((experts*HEAD,tok),bf16),
          jax.ShapeDtypeStruct((n,HEAD,W),bf16),jax.ShapeDtypeStruct((n,HEAD,W),bf16),
          jax.ShapeDtypeStruct((n,1,W),f32)],
        compiler_params=pltpu.CompilerParams(vmem_limit_bytes=60*2**20),
        name="attn_fwd",
    )(act,wq,routesT,gatesT,qdoc,kaug,vt)


def dot(a, b, dims=NN):
    return lax.dot_general(a, b, dims, preferred_element_type=f32)


def split3(x):
    hi = x.astype(bf16).astype(f32)
    r = x - hi
    mid = r.astype(bf16).astype(f32)
    return hi, mid, r - mid


class Here:
    def __init__(self, sizes):
        self.at = {a: lax.axis_index(a) for a in AXES}
        self.bit = {(ax, m): lax.rem(self.at[ax] // m, 2) for bits in mesh_bits(sizes).values() for ax, m in bits}
        self.known = {}

    def across(self, bits):
        bits = tuple(sorted(bits))
        if bits not in self.known:
            at = dict(self.at)
            for ax, m in bits:
                at[ax] = at[ax] + m - 2 * m * self.bit[ax, m]
            self.known[bits] = tuple(at[a] for a in AXES)
        return self.known[bits]


def subsets(group):
    return [[b for i, b in enumerate(group) if d >> i & 1] for d in range(1, 1 << len(group))]


def mesh_bits(sizes):
    return {a: [(a, 1 << i) for i in range(sizes[a].bit_length() - 1)] for a in AXES}


def small_mesh(sizes):
    return sizes["dp"] == sizes["ctx"] == 2 and sizes["exp"] == 8


def chain_orders(sizes):
    b = mesh_bits(sizes)
    e, d, c = b["exp"], b["dp"], b["ctx"]
    one = lambda bits: [(x,) for x in bits]
    late = one(e + d + c)
    if not small_mesh(sizes):
        return [late] * 3, late
    dense = [one(e[:1] + d + c + e[1:]), one(e[:1] + c + d + e[1:]), late]
    fast = [tuple(e[:1]), tuple(d + c), tuple(e[1:])]
    return dense, fast


def chain_plan(n, order):
    plan = []
    for group in order:
        ways = 1 << len(group)
        halve = n % (16 * ways) == 0
        n = n // ways if halve else n
        plan.append((halve, group, n))
    return plan


def rows(ref, start, n):
    return ref.at[pl.ds(pl.multiple_of(start, 16), n), :]


def add_rows(dst, d0, parts, n):
    ch = math.gcd(n, 64)

    @pl.loop(0, n // ch)
    def _(t):
        o = pl.multiple_of(t * ch, ch)
        g = [r[pl.ds(pl.multiple_of(s + o, 16), ch), :] for r, s in parts]
        total = g[0] + g[1] if len(g) == 2 else functools.reduce(jnp.add, [v.astype(f32) for v in g]).astype(bf16)
        dst[pl.ds(pl.multiple_of(d0 + o, 16), ch), :] = total


def block_places(n, order, owner):
    bits = [bit for halve, group, _ in chain_plan(n, order) if halve for bit in group]
    own = sorted([b for b in bits if b[0] == owner], reverse=True)
    nat = own + sorted([b for b in bits if b[0] != owner])
    places = []
    for i in range(1 << len(nat)):
        v = {b: (i >> (len(nat) - 1 - k)) & 1 for k, b in enumerate(nat)}
        places.append(sum(v[b] << (len(bits) - 1 - k) for k, b in enumerate(bits)))
    return n >> len(nat), places


class Chain:
    def __init__(self, work, final, base, n, order, owner=None, fbase=0):
        self.work, self.final, self.base, self.n, self.order = work, final, base, n, order
        self.owner, self.fbase = owner, fbase
        self.plan = chain_plan(n, order)
        self.landed = sum(m * ((1 << len(g)) - 1) for _, g, m in self.plan)
        self.back = [i for i in reversed(range(len(order))) if self.plan[i][0] and order[i][0][0] != owner]
        if owner:
            self.back.sort(key=lambda i: order[i], reverse=True)
        self.m = len(self.plan)
        self.groups = [g for _, g, _ in self.plan] + [order[i] for i in self.back]
        self.nsem = sum((1 << len(g)) - 1 for g in self.groups)
        self.nsteps = len(self.groups) + 1

    def place(self, here, land, lbase, ss, rs, sem):
        self.here, self.land, self.ss, self.rs = here, land, ss, rs
        self.lb, self.sem = [], []
        for _, g, m in self.plan:
            self.lb.append(lbase)
            lbase += m * ((1 << len(g)) - 1)
        for g in self.groups:
            for f in subsets(g):
                here.across(f)
            self.sem.append(sem)
            sem += (1 << len(g)) - 1
        self.offs, off = [], self.base
        for halve, g, m in self.plan:
            self.offs.append(off)
            if halve:
                off = off + self.index(g, []) * m
        self.last = off

    def index(self, group, flipped):
        v = 0
        for b in group:
            w = self.here.bit[b]
            v = 2 * v + (1 - w if b in flipped else w)
        return v

    def final_range(self, j):
        m = self.plan[-1][2]
        if self.owner is None:
            if j == 0:
                return self.last, m
            i = self.back[j - 1]
            return self.offs[i], self.plan[i][2] << len(self.order[i])
        rest = sorted(b for i in self.back for b in self.order[i])
        done = [b for i in self.back[:j] for b in self.order[i]]
        off = self.fbase
        for k, b in enumerate(rest):
            if b not in done:
                off = off + self.here.bit[b] * (m << (len(rest) - 1 - k))
        return off, m << len(done)

    def copies(self, k):
        out, g = [], self.groups[k]
        for d, flipped in enumerate(subsets(g)):
            if k < self.m:
                halve, _, n = self.plan[k]
                start = self.offs[k] + self.index(g, flipped) * n if halve else self.offs[k]
                src, dst = rows(self.work, start, n), rows(self.land, self.lb[k] + d * n, n)
            else:
                src = dst = rows(self.final, *self.final_range(k - self.m))
            out.append(pltpu.make_async_remote_copy(
                src_ref=src, dst_ref=dst, send_sem=self.ss.at[self.sem[k] + d], recv_sem=self.rs.at[self.sem[k] + d],
                device_id=self.here.across(flipped), device_id_type=MESH))
        return out

    def step(self, k):
        if k:
            for c in self.copies(k - 1):
                c.wait()
            if k <= self.m:
                i = k - 1
                halve, g, n = self.plan[i]
                last = i == self.m - 1
                d = self.offs[i] + self.index(g, []) * n if halve else self.offs[i]
                parts = [(self.work, d)] + [(self.land, self.lb[i] + j * n) for j in range((1 << len(g)) - 1)]
                add_rows(self.final if last else self.work, self.final_range(0)[0] if last else d, parts, n)
        if k < len(self.groups):
            for c in self.copies(k):
                c.start()


def meet(here, groups):
    devices = sorted({tuple(sorted(f)) for g in groups for f in subsets(g)})
    bar = pltpu.get_barrier_semaphore()
    for f in devices:
        pl.semaphore_signal(bar, inc=1, device_id=here.across(f), device_id_type=MESH)
    return lambda: pl.semaphore_wait(bar, len(devices))


def dense_parts(n, orders):
    a = n * 3 // 8 // 32 * 32
    return [(0, a, orders[0]), (a, a, orders[1]), (2 * a, n - 2 * a, orders[2])]


def make_chains(sizes, steps, part, nexp, keys, dsrc, fin, osrc, go, qsrc, gq, ksrc, kfin, ssrc, sfin):
    orders, small = chain_orders(sizes)
    n = sizes["exp"] * HEAD
    kbits = [(b,) for b in mesh_bits(sizes)["ctx"][::-1]]
    part = part * JOIN
    dense = [[Chain(dsrc, fin, j * part + b, m, o) for b, m, o in dense_parts(part, orders)] for j in range(steps // JOIN)]
    return dict(
        dense=dense,
        o=[Chain(osrc, go, j * n, n, orders[j % 3], "exp", j * HEAD) for j in range(nexp)],
        q=[Chain(qsrc, gq, j * n, n, orders[j % 3], "exp", j * HEAD) for j in range(nexp)],
        k=[Chain(ksrc, kfin, 0, keys, kbits, "ctx", 0)],
        g=[Chain(ssrc, sfin, 0, D, small)],
        s=[Chain(ssrc, sfin, D, SMALL - D, small)],
    )


def flat(chains):
    wide = [c for g in chains["dense"] for c in g] + chains["o"] + chains["q"]
    return wide, chains["k"] + chains["g"] + chains["s"]


def place_all(here, chains, land, nland, ss, rs):
    sem = 0
    for group, buf in zip(flat(chains), (land, nland)):
        lb = 0
        for c in group:
            c.place(here, buf, lb, ss, rs, sem)
            lb += c.landed
            sem += c.nsem


def mega_kernel(sizes, nf, nb, nexp, fb,
                cd, wo, tok, cot, g2, s2, up_ref, upb, down_ref, downb, q_ref, ctx_ref, lse_ref, routes_ref, gates_ref,
                qdoc_ref, kaug_ref, vaug_ref, kt_ref, act1, wq, kvw, g1,
                out, dx, go_o, gq_o, gkv_o, sm_o, gd_o, gu_o,
                mid, rstd, act, actT, dffn, dct, dqd, gub, gsm,
                qaug, daug, rhs, pds, dq, dkv,
                dsrc, fin, osrc, go, qsrc, gq, ksrc, kfin, ssrc, sfin, land, nland, ss, rs, lsem):
    s = pl.program_id(0)
    experts = cd.shape[0] // HEAD
    ntok, keys = tok.shape[0], kaug_ref.shape[0]
    part = 2 * fb
    chains = make_chains(sizes, nf, part, nexp, keys, dsrc, fin, osrc, go, qsrc, gq, ksrc, kfin, ssrc, sfin)
    here = Here(sizes)
    place_all(here, chains, land, nland, ss, rs)
    ticks = [(j, p) for j in range(nf) for p in range(3)] + [(nf + i, p) for i in range(nb) for p in range(4)]
    ticks += [(nf + nb, p) for p in range(4)]
    table, late = {}, []
    for j, group in enumerate(chains["dense"] + [chains["o"]]):
        t0 = ticks.index((j * JOIN + JOIN - 1, 2)) if j < nf // JOIN else ticks.index((nf, 0))
        for k in range(max(c.nsteps for c in group)):
            todo = [(c, k) for c in group if k < c.nsteps]
            at = t0 + (1 + STRIDE * (k - 1) // 2 if k else 0)
            if at < len(ticks):
                table.setdefault(ticks[at], []).extend(todo)
            else:
                late.extend(todo)

    def tick(step, pos):
        for at, todo in table.items():
            if at[1] != pos or step != ("f" if at[0] < nf else "b" if at[0] < nf + nb else "t"):
                continue
            if step == "t":
                for c, k in todo:
                    c.step(k)
                continue

            @pl.when(s == at[0])
            def _():
                for c, k in todo:
                    c.step(k)

    def put_owner(src_rows, value, e, order_of):
        for j in range(nexp):
            c = order_of[j]
            block, places = block_places(c.n, c.order, "exp")
            per = HEAD // block
            for b in range(per):
                at = c.base + places[e * per + b] * block
                src_rows[at:at + block, :] = value[j * HEAD + b * block:j * HEAD + (b + 1) * block, :]

    @pl.when(s == 0)
    def _():
        met = meet(here, [g for group in flat(chains) for c in group for g in c.groups])
        m = tok[...] + dot(cd[...], wo[...], TN)
        mid[...] = m
        cen = m - jnp.mean(m, axis=-1, keepdims=True)
        r = lax.rsqrt(jnp.mean(cen * cen, axis=-1, keepdims=True) + 1e-5)
        xh = cen * r
        rstd[...] = jnp.broadcast_to(r, rstd.shape)
        a = xh * g2[...] + s2[...]
        act[...] = a.astype(bf16)
        actT[...] = jnp.transpose(a).astype(bf16)
        dffn[...] = cot[...].astype(bf16)
        out[...] = m + downb[...]
        dx[...] = jnp.zeros_like(dx)
        met()

    @pl.when(s < nf)
    def _():
        up, down = up_ref[...], down_ref[...]
        pre = dot(act[...], up) + upb[...]
        x2 = pre * pre
        th = jnp.tanh(pre * (C0 + C0 * C1 * x2))
        h = 0.5 * (1.0 + th)
        hid = (pre * h).astype(bf16)
        gp = h + (0.5 * pre) * (1.0 - th * th) * (C0 + 3.0 * C0 * C1 * x2)
        out[...] += dot(hid, down)
        tick("f", 0)
        r0 = pl.multiple_of(s * part, part)
        dsrc[pl.ds(r0, fb), :] = dot(hid, dffn[...], TN).astype(bf16)
        tick("f", 1)
        dpb = (dot(dffn[...], down, NT) * gp).astype(bf16)
        gub[pl.ds(s, 1), :] = jnp.sum(dpb.astype(f32), axis=0, keepdims=True)
        dsrc[pl.ds(pl.multiple_of(r0 + fb, fb), fb), :] = dot(actT[...], dpb).astype(bf16)
        dx[...] += dot(dpb, up, NT)
        tick("f", 2)

    @pl.when(s == nf - 1)
    def _():
        d = dx[...]
        m = mid[...]
        xh = (m - jnp.mean(m, axis=-1, keepdims=True)) * rstd[:, 0:1]
        gx = d * g2[...]
        dm = cot[...] + rstd[:, 0:1] * (gx - jnp.mean(gx, axis=-1, keepdims=True)
                                        - xh * jnp.mean(gx * xh, axis=-1, keepdims=True))
        mid[...] = dm
        gsm[...] = jnp.concatenate([jnp.sum(d * xh, axis=0, keepdims=True), jnp.sum(d, axis=0, keepdims=True),
                                    jnp.sum(dffn[...].astype(f32), axis=0, keepdims=True)], axis=0)
        dmb = dm.astype(bf16)
        act[...] = dmb
        dct[...] = dot(wo[...], dmb, NT).astype(bf16)
        w = nexp * HEAD
        for e in range(sizes["exp"]):
            put_owner(osrc, dot(cd[e * w:(e + 1) * w, :], dmb).astype(bf16), e, chains["o"])

    @pl.when(s == nf)
    def _():
        dkv[...] = jnp.zeros_like(dkv)
        rhs[...] = jnp.zeros_like(rhs)

    @pl.when((s >= nf) & (s < nf + nb))
    def _():
        i = s - nf
        lanes = pl.ds(pl.multiple_of(i * TB, TB), TB)
        q = q_ref[0]
        qaug[0:HEAD, :] = q
        rhs[0:HEAD, 0:W] = q
        hi, md, lo = split3(-lse_ref[0])
        qd = qdoc_ref[...]
        qaug[HEAD:HEAD + 16, :] = jnp.concatenate(
            [jnp.concatenate([qd[0:3, :]] * TOP, 1), hi, md, lo, jnp.zeros((10, W), f32)], 0).astype(bf16)
        qaug[HEAD + 16:, :] = jnp.zeros((128 - HEAD - 16, W), bf16)
        r = [jnp.broadcast_to(routes_ref[k:k + 1, :], (8, TB))[None] for k in range(TOP)]
        for k0 in range(0, TOP, 4):
            sel = [jnp.zeros((HEAD // 8, 8, TB), f32) for _ in range(4)]
            for e in range(experts):
                v = dct[e * HEAD:(e + 1) * HEAD, lanes].astype(f32).reshape(HEAD // 8, 8, TB)
                sel = [jnp.where(r[k0 + k] == e, v, sel[k]) for k in range(4)]
            for k in range(4):
                sl = slice((k0 + k) * TB, (k0 + k + 1) * TB)
                dc = (sel[k].reshape(HEAD, TB) * gates_ref[k0 + k:k0 + k + 1, :]).astype(bf16)
                daug[0:HEAD, sl] = dc
                rhs[HEAD:, W + (k0 + k) * TB:W + (k0 + k + 1) * TB] = dc
                dq[0:1, sl] = jnp.sum(dc.astype(f32) * ctx_ref[0, :, sl].astype(f32), axis=0, keepdims=True)
        hi, md, lo = split3(-dq[0:1, :])
        daug[HEAD:HEAD + 16, :] = jnp.concatenate([hi, md, lo, jnp.zeros((13, W), f32)], 0).astype(bf16)
        daug[HEAD + 16:, :] = jnp.zeros((128 - HEAD - 16, W), bf16)
        dq[...] = jnp.zeros_like(dq)
        q0 = lax.axis_index("ctx") * ntok + i * TB
        nfull = q0 // KBB
        kd = pl.multiple_of(nfull * KBB, KBB)

        def block(k0, mask):
            p = jnp.exp2(dot(kaug_ref[pl.ds(k0, KBB), :], qaug[...]))
            if mask is not None:
                p = jnp.concatenate([jnp.where(mask, p[:, k * TB:(k + 1) * TB], 0.0) for k in range(TOP)], 1)
            dp = dot(vaug_ref[pl.ds(k0, KBB), :], daug[...])
            pds[:, W:] = p.astype(bf16)
            pds[:, :W] = (p * dp).astype(bf16)
            dq[...] += dot(kt_ref[:, pl.ds(k0, KBB)], pds[:, :W])
            dkv[pl.ds(k0, KBB), :] += dot(pds[...], rhs[...], NT)

        def body(b, _):
            block(pl.multiple_of(b * KBB, KBB), None)
            return 0

        tick("b", 0)
        lax.fori_loop(0, nfull, body, 0)
        tick("b", 1)
        kp = lax.broadcasted_iota(jnp.int32, (KBB, TB), 0) + (kd - q0)
        tp = lax.broadcasted_iota(jnp.int32, (KBB, TB), 1)
        block(kd, kp <= tp)
        tick("b", 2)
        dq[...] *= 0.125
        for h0 in range(0, HEAD, 32):
            g = [dq[h0:h0 + 32, k * TB:(k + 1) * TB].reshape(4, 8, TB) for k in range(TOP)]
            for e in range(experts):
                o = jnp.zeros((4, 8, TB), f32)
                for k in range(TOP):
                    o = jnp.where(r[k] == e, g[k], o)
                dqd[e * HEAD + h0:e * HEAD + h0 + 32, lanes] = o.reshape(32, TB).astype(bf16)
        tick("b", 3)

    @pl.when(s == nf + nb)
    def _():
        lane = lax.broadcasted_iota(jnp.int32, (1, 128), 1)
        ksrc[...] = (dkv[...] * jnp.where(lane < HEAD, LN2, 1.0)).astype(bf16)
        kc, gc, sc = chains["k"][0], chains["g"][0], chains["s"][0]
        kc.step(0)
        tick("t", 0)
        w = nexp * HEAD
        for e in range(sizes["exp"]):
            put_owner(qsrc, dot(dqd[e * w:(e + 1) * w, :], act1[...]).astype(bf16), e, chains["q"])
        for c in chains["q"]:
            c.step(0)
        for k in range(1, kc.nsteps):
            kc.step(k)
        ssrc[0:D, :] = dot(act1[...], kfin[...], TN).astype(bf16)
        gc.step(0)
        tick("t", 1)
        for c in chains["q"]:
            c.step(1)
        da = dot(dqd[...], wq[...], TN) + dot(kfin[...], kvw[...].astype(bf16), NT)
        gc.step(1)
        tick("t", 2)
        x = tok[...]
        cen = x - jnp.mean(x, axis=-1, keepdims=True)
        r1 = lax.rsqrt(jnp.mean(cen * cen, axis=-1, keepdims=True) + 1e-5)
        xh = cen * r1
        gg1, gs1 = jnp.sum(da * xh, axis=0, keepdims=True), jnp.sum(da, axis=0, keepdims=True)
        vecs = [gsm[0:1, :], gsm[1:2, :], gsm[2:3, :], gg1, gs1] + [gub[j:j + 1, :] for j in range(nf)]
        vecs = [v[:, o:o + 128] for v in vecs for o in range(0, v.shape[1], 128)]
        vecs.append(jnp.zeros((SMALL - D - len(vecs), 128), f32))
        ssrc[D:SMALL, :] = jnp.concatenate(vecs, 0).astype(bf16)
        sc.step(0)
        for c in chains["q"]:
            c.step(2)
        gc.step(2)
        gx = da * g1[...]
        dx[...] = mid[...] + r1 * (gx - jnp.mean(gx, axis=-1, keepdims=True)
                                   - xh * jnp.mean(gx * xh, axis=-1, keepdims=True))
        tick("t", 3)
        rounds = max(c.nsteps for c in (gc, sc, *chains["q"]))
        for k in range(1, rounds):
            for c, lag in [(c, 2) for c in chains["q"]] + [(gc, 2), (sc, 0)]:
                if k + lag < c.nsteps:
                    c.step(k + lag)
            share = -(-len(late) // 3)
            for c, n in late[(k - 1) * share:k * share]:
                c.step(n)
            if k == 3:
                moved = []
                for j in range(nf):
                    r0 = j * part
                    moved.append(pltpu.make_async_copy(
                        fin.at[r0:r0 + fb, :], gd_o.at[j * fb:(j + 1) * fb, :], lsem.at[2 * j]))
                    moved.append(pltpu.make_async_copy(
                        fin.at[r0 + fb:r0 + part, :], gu_o.at[:, j * fb:(j + 1) * fb], lsem.at[2 * j + 1]))
                for c in moved:
                    c.start()
        go_o[...] = go[...].astype(f32)
        gq_o[...] = gq[...].astype(f32)
        gkv_o[...] = sfin[0:D, :].astype(f32)
        sm_o[...] = sfin[D:SMALL, :].astype(f32)
        for c in moved:
            c.wait()


def mega(sizes, nexp, cd, wo, tok, cot, g2, s2, up, upb, down, downb, q, ctx, lse, routes, gates, qdoc, kaug, vaug, kt,
         act1, wq, kvw, g1, fb=512):
    ntok, keys, ff, eh = tok.shape[0], kaug.shape[0], up.shape[1], wo.shape[0]
    nf, nb = ff // fb, ntok // TB
    part = 2 * fb
    sd = jax.ShapeDtypeStruct
    z = [None] * 10
    chains = make_chains(sizes, nf, part, nexp, keys, *z)
    wide, narrow = flat(chains)
    land, nland = sum(c.landed for c in wide), sum(c.landed for c in narrow)
    nsem = sum(c.nsem for c in wide + narrow)
    once = pl.Buffered(1)
    full = lambda a: pl.BlockSpec(a.shape, lambda s: (0,) * a.ndim, pipeline_mode=once)
    fo = lambda *sh: pl.BlockSpec(sh, lambda s: (0,) * len(sh), pipeline_mode=once)
    fj = lambda s: jnp.minimum(s, nf - 1)
    bi = lambda s: jnp.clip(s - nf, 0, nb - 1)
    blk = lambda r: pl.BlockSpec((r, TB), lambda s: (0, bi(s)))
    b3 = lambda a: pl.BlockSpec((1,) + a.shape[1:], lambda s: (bi(s), 0, 0))
    any_ = pl.BlockSpec(memory_space=pl.ANY)
    v = pltpu.VMEM
    return pl.pallas_call(
        functools.partial(mega_kernel, sizes, nf, nb, nexp, fb),
        grid=(nf + nb + 1,),
        in_specs=[full(cd), full(wo), full(tok), full(cot), full(g2), full(s2),
                  pl.BlockSpec((D, fb), lambda s: (0, fj(s))), pl.BlockSpec((1, fb), lambda s: (0, fj(s))),
                  pl.BlockSpec((fb, D), lambda s: (fj(s), 0)), full(downb), b3(q), b3(ctx), b3(lse),
                  blk(TOP), blk(TOP), blk(8), full(kaug), full(vaug), full(kt), full(act1), full(wq), full(kvw), full(g1)],
        out_specs=[fo(ntok, D), fo(ntok, D), fo(nexp * HEAD, D), fo(nexp * HEAD, D), fo(D, 128), fo(SMALL - D, 128), any_, any_],
        out_shape=[sd((ntok, D), f32), sd((ntok, D), f32), sd((nexp * HEAD, D), f32), sd((nexp * HEAD, D), f32),
                   sd((D, 128), f32), sd((SMALL - D, 128), f32), sd((ff, D), bf16), sd((D, ff), bf16)],
        scratch_shapes=[
            v((ntok, D), f32), v((ntok, 128), f32), v((ntok, D), bf16), v((D, ntok), bf16),
            v((ntok, D), bf16), v((eh, ntok), bf16), v((eh, ntok), bf16), v((nf, fb), f32), v((3, D), f32),
            v((128, W), bf16), v((128, W), bf16), v((128, 2 * W), bf16), v((KBB, 2 * W), bf16), v((HEAD, W), f32),
            v((keys, 128), f32),
            v((nf * part, D), bf16), v((nf * part, D), bf16), v((eh, D), bf16), v((nexp * HEAD, D), bf16),
            v((eh, D), bf16), v((nexp * HEAD, D), bf16), v((keys, 128), bf16), v((ntok, 128), bf16),
            v((SMALL, 128), bf16), v((SMALL, 128), bf16), v((land, D), bf16), v((nland, 128), bf16),
            pltpu.SemaphoreType.DMA((nsem,)), pltpu.SemaphoreType.DMA((nsem,)), pltpu.SemaphoreType.DMA((2 * nf,))],
        compiler_params=pltpu.CompilerParams(collective_id=0, has_side_effects=True, vmem_limit_bytes=62 * 2**20),
        name="mega",
    )(cd, wo, tok, cot, g2, s2, up, upb, down, downb, q, ctx, lse, routes, gates, qdoc, kaug, vaug, kt, act1, wq, kvw, g1)


def gather_stages(sizes, here, shard):
    e = lax.axis_index("exp")
    if not small_mesh(sizes) or shard % 64:
        stages = []
        for i, bit in enumerate(mesh_bits(sizes)["exp"]):
            stages.append([((e >> i << i) * shard, shard << i, [bit])])
        return stages, []
    core, zl, zh, x, y = ("exp", 1), ("exp", 2), ("exp", 4), ("dp", 1), ("ctx", 1)
    quarter = shard // 4
    flip = lambda bit, n: n * (1 - 2 * here.bit[bit])
    at = lambda dz: e + (dz & 1) * flip(zl, 2) + (dz >> 1) * flip(zh, 4)
    row = lambda dz: at(dz) * shard + (here.bit[x] * 2 + here.bit[y]) * quarter
    stages = [
        [(row(0), quarter, f) for f in subsets((zl, zh))],
        [(row(d), quarter, f) for d in (1, 2, 3) for f in subsets((x, y))],
        [(at(d) * shard, shard, [core]) for d in (1, 2, 3)],
    ]
    return stages, [(e * shard, shard, [core])]


def head_kernel(sizes, nexp, nsem, tok, g1, s1, kvw, wq3, wo3, lens, up_h, down_h,
                act, kaug, vaug, kt, vt, qdoc, wq_o, wo_o, up_o, down_o,
                wqs, wos, kv, upf, downf, upb, downb, ss, rs, ls):
    here = Here(sizes)
    ntok, keys, shard = tok.shape[0], kv.shape[0], nexp * HEAD
    fetch = [pltpu.make_async_copy(up_h, upf, ls.at[0]), pltpu.make_async_copy(down_h, downf, ls.at[1])]
    for c in fetch:
        c.start()
    b = mesh_bits(sizes)
    exact = [tuple(b["exp"][1:]), tuple(b["dp"] + b["ctx"])] if small_mesh(sizes) else []
    met = meet(here, [(x,) for a in AXES for x in b[a]] + exact)
    mine = lax.axis_index("exp") * shard
    for j in range(nexp):
        r = pl.ds(pl.multiple_of(mine + j * HEAD, HEAD), HEAD)
        wqs[r, :] = wq3[j].astype(bf16)
        wos[r, :] = wo3[j].astype(bf16)
    met()
    count = [0]

    def send(buf, moves):
        out = []
        for start, n, bits in moves:
            r = rows(buf, start, n)
            k = count[0]
            count[0] += 1
            c = pltpu.make_async_remote_copy(src_ref=r, dst_ref=r, send_sem=ss.at[k], recv_sem=rs.at[k],
                                             device_id=here.across(bits), device_id_type=MESH)
            c.start()
            out.append(c)
        return out

    def wait(copies):
        for c in copies:
            c.wait()

    stages, early = gather_stages(sizes, here, shard)
    work = []

    def run(k):
        for buf, lag in ((wqs, 0), (wos, 1)):
            i = k - lag
            if 0 < i <= len(stages):
                wait(flying[buf is wos])
            if 0 <= i < len(stages):
                flying[buf is wos] = send(buf, stages[i])

    flying = [[], []]
    run(0)
    own = send(wqs, early) + send(wos, early)
    x = tok[...]
    cen = x - jnp.mean(x, axis=-1, keepdims=True)
    a = (cen * lax.rsqrt(jnp.mean(cen * cen, axis=-1, keepdims=True) + 1e-5) * g1[...] + s1[...]).astype(bf16)
    act[...] = a
    ctx = lax.axis_index("ctx")
    kv[pl.ds(pl.multiple_of(ctx * ntok, ntok), ntok), :] = dot(a, kvw[...].astype(bf16)).astype(bf16)
    cbits = mesh_bits(sizes)["ctx"]
    share = lambda i: send(kv, [((ctx >> i << i) * ntok, ntok << i, [cbits[i]])])
    swap = share(0)
    run(1)
    put = []

    def cast(k, src, dst, o):
        fetch[k].wait()

        @pl.loop(0, src.shape[0] // 64)
        def _(t):
            r = pl.ds(pl.multiple_of(t * 64, 64), 64)
            dst[r, :] = src[r, :].astype(bf16)

        c = pltpu.make_async_copy(dst, o, ls.at[2 + k])
        c.start()
        put.append(c)

    def ends(pos):
        d, end = jnp.zeros(pos.shape, jnp.int32), 0
        for j in range(lens.shape[0] - 1):
            end = end + lens[j]
            d = d + (pos >= end).astype(jnp.int32)
        return d

    cast(0, upf, upb, up_o)
    slot = lax.broadcasted_iota(jnp.int32, (8, ntok), 0)
    qpos = ends(lax.broadcasted_iota(jnp.int32, (8, ntok), 1) + ctx * ntok)
    qdoc[...] = jnp.where((qpos == slot) | (slot > 2), 0.0, NEG)
    run(2)
    wait(swap)
    for i in range(1, len(cbits)):
        wait(share(i))
    cast(1, downf, downb, down_o)
    run(3)
    lane = lax.broadcasted_iota(jnp.int32, (keys, 128), 1)
    doc = ends(lax.broadcasted_iota(jnp.int32, (keys, 128), 0))
    full = kv[...].astype(f32)
    extra = jnp.where((lane == doc + HEAD) | ((lane > HEAD + 2) & (lane < HEAD + 6)), 1.0, 0.0)
    kaug[...] = jnp.where(lane < HEAD, full, extra).astype(bf16)
    flipped = jnp.concatenate([full[:, HEAD:], full[:, :HEAD]], axis=1)
    vaug[...] = jnp.where(lane < HEAD, flipped, jnp.where(lane < HEAD + 3, 1.0, 0.0)).astype(bf16)
    both = jnp.transpose(full)
    kt[...] = both[:HEAD].astype(bf16)
    vt[...] = jnp.concatenate([both[HEAD:], jnp.ones((1, keys), f32), jnp.zeros((15, keys), f32)], 0).astype(bf16)
    run(4)
    for k in range(5, len(stages) + 2):
        run(k)
    wait(own)
    for k, (src, o) in enumerate(((wqs, wq_o), (wos, wo_o))):
        c = pltpu.make_async_copy(src, o, ls.at[4 + k])
        c.start()
        put.append(c)
    for c in put:
        c.wait()


def head(sizes, nexp, tok, g1, s1, kvw, wq3, wo3, lens, up, down):
    ntok, keys, experts = tok.shape[0], tok.shape[0] * sizes["ctx"], nexp * sizes["exp"]
    vm, any_ = pl.BlockSpec(memory_space=pltpu.VMEM), pl.BlockSpec(memory_space=pl.ANY)
    sd, v = jax.ShapeDtypeStruct, pltpu.VMEM
    nsem = 64
    wide = (experts * HEAD, D)
    return pl.pallas_call(
        functools.partial(head_kernel, sizes, nexp, nsem),
        in_specs=[vm] * 6 + [pl.BlockSpec(memory_space=pltpu.SMEM), any_, any_],
        out_specs=[vm] * 6 + [any_] * 4,
        out_shape=[sd((ntok, D), bf16), sd((keys, 128), bf16), sd((keys, 128), bf16), sd((HEAD, keys), bf16),
                   sd((HEAD + 16, keys), bf16), sd((8, ntok), f32), sd(wide, bf16), sd(wide, bf16),
                   sd(up.shape, bf16), sd(down.shape, bf16)],
        scratch_shapes=[v(wide, bf16), v(wide, bf16), v((keys, 128), bf16), v(up.shape, f32), v(down.shape, f32),
                        v(up.shape, bf16), v(down.shape, bf16), pltpu.SemaphoreType.DMA((nsem,)),
                        pltpu.SemaphoreType.DMA((nsem,)), pltpu.SemaphoreType.DMA((6,))],
        compiler_params=pltpu.CompilerParams(collective_id=1, has_side_effects=True, vmem_limit_bytes=60 * 2**20),
        name="head",
    )(tok, g1, s1, kvw, wq3, wo3, lens, up, down)


def finish_kernel(nc, sm, gd, gu, *refs):
    moves, wide_o, moved, vec_o = refs[:5], refs[5:7], refs[7:12], refs[12:18]
    lows, wides, vias, si, so = refs[18:20], refs[20:22], refs[22:27], refs[27], refs[28]
    ins, outs, parts = [], [], []
    for k, (a, via, b) in enumerate(zip(moves, vias, moved)):
        ins.append(pltpu.make_async_copy(a, via, si.at[2 * nc + k]))
        outs.append(pltpu.make_async_copy(via, b, so.at[2 * nc + k]))
        parts.append(None)
    for i, src in enumerate((gd, gu)):
        n = src.shape[0] // nc
        for j in range(nc):
            r = slice(j * n, (j + 1) * n)
            ins.append(pltpu.make_async_copy(src.at[r, :], lows[i].at[r, :], si.at[i * nc + j]))
            outs.append(pltpu.make_async_copy(wides[i].at[r, :], wide_o[i].at[r, :], so.at[i * nc + j]))
            parts.append((i, r))
    for c in ins:
        c.start()
    at = 0
    for o in vec_o:
        n = o.shape[1] // 128
        o[...] = jnp.concatenate([sm[j:j + 1, :] for j in range(at, at + n)], 1)
        at += n
    for k, part in enumerate(parts):
        ins[k].wait()
        if part:
            i, r = part
            wides[i][r, :] = lows[i][r, :].astype(f32)
        outs[k].start()
    for c in outs:
        c.wait()


def finish(sm, gd, gu, others, nub, nc=8):
    any_, vm = pl.BlockSpec(memory_space=pl.ANY), pl.BlockSpec(memory_space=pltpu.VMEM)
    sd, v = jax.ShapeDtypeStruct, pltpu.VMEM
    sem = pltpu.SemaphoreType.DMA
    return pl.pallas_call(
        functools.partial(finish_kernel, nc),
        in_specs=[vm] + [any_] * 7, out_specs=[any_] * 7 + [vm] * 6,
        out_shape=[sd(gd.shape, f32), sd(gu.shape, f32)] + [sd(o.shape, o.dtype) for o in others]
        + [sd((1, D), f32)] * 5 + [sd((1, nub), f32)],
        scratch_shapes=[v(gd.shape, bf16), v(gu.shape, bf16), v(gd.shape, f32), v(gu.shape, f32)]
        + [v(o.shape, o.dtype) for o in others] + [sem((2 * nc + 5,)), sem((2 * nc + 5,))],
        compiler_params=pltpu.CompilerParams(vmem_limit_bytes=62 * 2**20),
        name="post",
    )(sm, gd, gu, *others)


def local(sizes, tokens, lengths, routes, route_gates, cotangent, gain_one, shift_one, kv_weight,
          query_weight, out_weight, gain_two, shift_two, up_weight, up_bias, down_weight, down_bias):
    x = tokens[0]
    nexp = query_weight.shape[0]
    row = lambda v: v.reshape(1, -1)
    act, kaug, vaug, kt, vt, qdoc, wq, wo, up, down = head(
        sizes, nexp, x, row(gain_one), row(shift_one), kv_weight, jnp.swapaxes(query_weight, 1, 2), out_weight, lengths[0], up_weight,
        down_weight)
    routes_t = routes[0].T
    gates_t = route_gates[0].T
    cd, q, ctx, lse = attn_fwd(act, wq, routes_t, gates_t, qdoc, kaug, vt, KB=768)
    out, dx, go, gq, gkv, small, gdown, gup = mega(
        sizes, nexp, cd, wo, x, cotangent[0], row(gain_two), row(shift_two), up, row(up_bias), down, row(down_bias), q,
        ctx, lse, routes_t, gates_t, qdoc, kaug, vaug, kt, act, wq, kv_weight, row(gain_one))
    gdown, gup, out, dx, go, gq, gkv, *vecs = finish(small, gdown, gup, (out, dx, go, gq, gkv), up_bias.shape[0])
    go = go.reshape(nexp, HEAD, D)
    gq = jnp.swapaxes(gq.reshape(nexp, HEAD, D), 1, 2)
    gg2, gs2, gdb, gg1, gs1, gub = [v.reshape(-1) for v in vecs]
    return (out[None], dx[None], gg1, gs1, gkv, gq, go, gg2, gs2, gup, gub, gdown, gdb)


def solution(mesh):
    tok3 = P(("dp", "exp"), "ctx", None)
    ex = P("exp", None, None)
    r = P()
    in_specs = (tok3, P(("dp", "exp"), None), tok3, tok3, tok3, r, r, r, ex, ex, r, r, r, r, r, r)
    out_specs = (tok3, tok3, r, r, r, ex, ex, r, r, r, r, r, r)
    fn = functools.partial(local, dict(mesh.shape))
    return jax.shard_map(fn, mesh=mesh, in_specs=in_specs, out_specs=out_specs, check_vma=False)
```
